32 devices in a mesh: head: 4 (over z), tok: 8 (over y, x, core).
Axes of the slice: x: 2, y: 2, z: 4, core: 2. Of those that a mesh axis runs over, the one named last changes fastest.
Arguments:
- tokens: bfloat16 [8192, 2048], P('tok', 'head'), may hold values from -6 to 6
- mix_gain: float32 [2048], P('head'), may hold values from 0.5 to 1.5
- mix_bias: float32 [2048], P('head'), may hold values from -1.5 to 1.5
- query_weight: bfloat16 [2048, 2048], P(None, 'head'), may hold values from -0.125 to 0.125
- key_weight: bfloat16 [2048, 2048], P(None, 'head'), may hold values from -0.125 to 0.125
- value_weight: bfloat16 [2048, 4096], P(None, 'head'), may hold values from -0.125 to 0.125
- gate_weight: bfloat16 [2048, 4096], P(None, 'head'), may hold values from -0.125 to 0.125
- output_weight: bfloat16 [4096, 2048], P('head'), may hold values from -0.1875 to 0.1875
- feed_gain: float32 [2048], P('head'), may hold values from 0.5 to 1.5
- feed_bias: float32 [2048], P('head'), may hold values from -1.5 to 1.5
- up_weight: bfloat16 [2048, 4096], P(None, 'head'), may hold values from -0.125 to 0.125
- down_weight: bfloat16 [4096, 2048], P('head'), may hold values from -0.09375 to 0.09375
- doc_ids: int32 [8192], P('tok'), may hold values from 0 to 15, never falling along the last dimension, each value on 1 to 3072 neighbouring positions
- pad_mask: int32 [8192], P('tok'), may hold values 0 or 1
- out_grad: bfloat16 [8192, 2048], P('tok', 'head'), may hold values from -6 to 6
Outputs:
- layer_out: bfloat16 [8192, 2048], P('tok', 'head')
- tokens_grad: float32 [8192, 2048], P('tok', 'head')
- mix_gain_grad: float32 [2048], P('head')
- mix_bias_grad: float32 [2048], P('head')
- query_weight_grad: float32 [2048, 2048], P(None, 'head')
- key_weight_grad: float32 [2048, 2048], P(None, 'head')
- value_weight_grad: float32 [2048, 4096], P(None, 'head')
- gate_weight_grad: float32 [2048, 4096], P(None, 'head')
- output_weight_grad: float32 [4096, 2048], P('head')
- feed_gain_grad: float32 [2048], P('head')
- feed_bias_grad: float32 [2048], P('head')
- up_weight_grad: float32 [2048, 4096], P(None, 'head')
- down_weight_grad: float32 [4096, 2048], P('head')
The draws below stay inside these ranges and needn't reach their ends.
Inputs may be any that keep to these rules, and one draw needn't show every extreme that they name: `doc_ids`: document numbers never fall along the stream; a document has 1 to 3072 tokens, and one has exactly that many.
All inputs are finite; a program needn't handle non-finite values. No bound on the sum of `pad_mask` on one device may be relied on, other than what follows from the above.
Results may differ from the reference program's by a relative error of at most 0.014.
Values may be sent and summed in bfloat16 or wider, within the bound.
No kernel may reach another device: no remote copies, remote signals or barrier semaphores. Data moves between devices by JAX's collectives and lax.ppermute only.
A program may use at most 256 MiB of HBM per device.

```python
import math
from functools import partial
import jax
import jax.numpy as jnp
import numpy as np
from jax import lax

D = 2048
HEADS = 8
KD = 256
VD = 512
FF = 4096
TOK_DEV = 1024
TOKENS = 8192
N_TOK = 8


def with_ends(values, key, least, high):
    longest = values.shape.index(max(values.shape))
    spots = []
    for shift in (0, 1):
        where = [jax.random.randint(jax.random.fold_in(key, axis), (), 0, length) for axis, length in enumerate(values.shape)]
        where[longest] = (where[longest] + shift) % values.shape[longest]
        spots.append(tuple(where))
    return values.at[spots[0]].set(least).at[spots[1]].set(high)


def steps_of(rng, shape, split, least, top_value):
    def one(axis_at, blocks):
        draws = jax.random.uniform(jax.random.fold_in(jax.random.fold_in(rng, 6), axis_at), (blocks,), jnp.float32, least / len(split), top_value / len(split))
        return jnp.repeat(jnp.exp(draws), shape[axis_at] // blocks).reshape((-1,) + (1,) * (len(shape) - axis_at - 1))

    loudness = one(*split[0])
    for cut in split[1:]:
        loudness = loudness * one(*cut)
    return loudness


def split_up(amount, total, limit, slope):
    portions = [(1 << 20) // math.isqrt(grade ** slope) + 1 for grade in range(2, amount + 1)]
    spare, given = total - limit - (amount - 1), [1] * (amount - 1)
    while spare > 0:
        free = [i for i in range(amount - 1) if given[i] < limit]
        whole, left = sum([portions[i] for i in free]), spare
        for i in free:
            addition = min(limit - given[i], max(1, left * portions[i] // whole), spare)
            given[i] = given[i] + addition
            spare = spare - addition
    return np.array([limit] + given)


def uneven_parts(stream_key, amount, total, most, slope):
    if amount == 2:
        one = jax.random.randint(stream_key, (), max(1, total - most), min(most, total - 1) + 1)
        return jnp.stack([one, total - one])
    tallies = jnp.asarray(split_up(amount, total, most, slope), jnp.int32)
    pairs = (amount - 1) // 2
    source_of, receiver = tallies[1:1 + 2 * pairs:2], tallies[2:2 + 2 * pairs:2]
    slack = jnp.minimum(source_of - 1, most - receiver)
    shifted = jax.random.randint(jax.random.fold_in(stream_key, 1), (pairs,), 0, 1 << 20) % (slack + 1)
    tallies = tallies.at[1:1 + 2 * pairs:2].set(source_of - shifted).at[2:2 + 2 * pairs:2].set(receiver + shifted)
    return tallies[jax.random.permutation(jax.random.fold_in(stream_key, 2), amount)]


def normal_values(stream_key, dims, spread, most, pieces=(), kind=jnp.bfloat16):
    loudness = steps_of(stream_key, dims, pieces, -0.22, 0.18) if pieces else 1.0
    entries = jax.random.normal(stream_key, dims, jnp.float32) * spread * loudness
    return jnp.minimum(jnp.maximum(entries, -most), most).astype(kind)


def setup_inputs(seed: int = 0) -> dict:
    key_list = jax.random.split(jax.random.key(seed), 16)
    tokens = normal_values(key_list[0], (TOKENS, D), 1.0, 6.0, ((0, 8), (1, 4)))
    mix_gain = jnp.clip(1.0 + 0.1 * jax.random.normal(key_list[1], (D,), jnp.float32), 0.5, 1.5)
    mix_bias = normal_values(key_list[2], (D,), 0.3, 1.5, ((0, 4),), jnp.float32)
    query_weight = normal_values(key_list[3], (D, HEADS * KD), D ** -0.5, 0.125, ((1, 4),))
    key_weight = normal_values(key_list[4], (D, HEADS * KD), D ** -0.5, 0.125, ((1, 4),))
    value_weight = normal_values(key_list[5], (D, HEADS * VD), D ** -0.5, 0.125, ((1, 4),))
    gate_weight = normal_values(key_list[6], (D, HEADS * VD), D ** -0.5, 0.125, ((1, 4),))
    output_weight = normal_values(key_list[7], (HEADS * VD, D), (HEADS * VD // 4) ** -0.5, 0.1875, ((0, 4),))
    feed_gain = jnp.clip(1.0 + 0.1 * jax.random.normal(key_list[8], (D,), jnp.float32), 0.5, 1.5)
    feed_bias = normal_values(key_list[9], (D,), 0.3, 1.5, ((0, 4),), jnp.float32)
    up_weight = normal_values(key_list[10], (D, FF), D ** -0.5, 0.125, ((1, 4),))
    down_weight = normal_values(key_list[11], (FF, D), FF ** -0.5, 0.09375, ((0, 4),))
    doc_ids = jnp.searchsorted(jnp.cumsum(uneven_parts(key_list[12], 2 * N_TOK, TOKENS, 3 * TOK_DEV, 1)), jnp.arange(TOKENS), side="right").astype(jnp.int32)
    pad_mask = with_ends((jax.random.randint(key_list[13], (TOKENS,), 0, 8) < 7).astype(jnp.int32), jax.random.fold_in(key_list[13], 1), 0, 1)
    out_grad = normal_values(key_list[14], (TOKENS, D), 1.0, 6.0, ((0, 8), (1, 4)))
    return {"tokens": tokens, "mix_gain": mix_gain, "mix_bias": mix_bias, "query_weight": query_weight, "key_weight": key_weight, "value_weight": value_weight, "gate_weight": gate_weight, "output_weight": output_weight, "feed_gain": feed_gain, "feed_bias": feed_bias, "up_weight": up_weight, "down_weight": down_weight, "doc_ids": doc_ids, "pad_mask": pad_mask, "out_grad": out_grad}


HIGHEST = lax.Precision.HIGHEST
EPSILON = 1e-05

@jax.custom_vjp
def low(v):
    return lax.optimization_barrier(v.astype(jnp.bfloat16)).astype(jnp.float32)

@jax.custom_vjp
def low_back(v):
    return v

def low_keep(v):
    return (low(v), None)

def low_pass(kept, grad):
    return (grad,)

def back_keep(v):
    return (v, None)

def back_low(kept, grad):
    return (low(grad),)
low.defvjp(low_keep, low_pass)
low_back.defvjp(back_keep, back_low)

def matmul(left, right):
    return jnp.dot(left, right, precision=HIGHEST, preferred_element_type=jnp.float32)

def norm_rows(values, gain_vec, bias_vec):
    row_mean = lax.optimization_barrier(jnp.mean(values, axis=-1, keepdims=True))
    row_var = lax.optimization_barrier(jnp.mean(values * values, axis=-1, keepdims=True)) - row_mean * row_mean
    return (values - row_mean) * lax.rsqrt(row_var + EPSILON) * gain_vec + bias_vec

def rotate(values, angles):
    half_dim = values.shape[-1] // 2
    cosine = jnp.cos(angles)[:, None, :]
    sine_vals = jnp.sin(angles)[:, None, :]
    front_half = values[..., :half_dim]
    back_half = values[..., half_dim:]
    return jnp.concatenate([front_half * cosine - back_half * sine_vals, back_half * cosine + front_half * sine_vals], axis=-1)

def group_norm(mixed):
    group_mean = lax.optimization_barrier(jnp.mean(mixed, axis=-1, keepdims=True))
    group_var = lax.optimization_barrier(jnp.mean(mixed * mixed, axis=-1, keepdims=True)) - group_mean * group_mean
    return (mixed - group_mean) * lax.rsqrt(group_var + 1.0)

def layer_block(params, state, inputs):
    mix_gain, mix_bias, query_weight, key_weight, value_weight, gate_weight, output_weight, feed_gain, feed_bias, up_weight, down_weight = params
    block_rows, block_docs, block_pad, previous, offset = inputs
    float_type = block_rows.dtype
    block_len = block_rows.shape[0]
    position = jnp.arange(block_len, dtype=jnp.int32)
    head_index = jnp.arange(HEADS, dtype=jnp.int32).astype(float_type)
    log_decay = jnp.log(1.0 - 2.0 ** (-5.0 - head_index))
    frequency = 10000.0 ** (-2.0 * jnp.arange(KD // 2, dtype=jnp.int32).astype(float_type) / KD)
    angles = (offset.astype(jnp.int32) + position).astype(float_type)[:, None] * frequency[None, :]
    low_first = low(norm_rows(block_rows, mix_gain, mix_bias))
    queries = low_back(matmul(low_first, query_weight)).reshape(block_len, HEADS, KD)
    key_proj = low_back(matmul(low_first, key_weight)).reshape(block_len, HEADS, KD)
    values = low(low_back(matmul(low_first, value_weight))).reshape(block_len, HEADS, VD)
    gate_pre = low_back(matmul(low_first, gate_weight))
    query_rot = low(rotate(queries, angles))
    key_rot = low(rotate(key_proj, angles) * KD ** (-0.5))
    distance = (position[:, None] - position[None, :]).astype(jnp.int32)
    allowed = ((block_docs[:, None] == block_docs[None, :]) & (distance >= 0)).astype(float_type) * block_pad[None, :]
    decay_mat = jnp.exp(jnp.maximum(distance, 0).astype(float_type)[None] * log_decay[:, None, None]) * allowed[None]
    scores = low_back(jnp.einsum('nha,mha->hnm', query_rot, key_rot, precision=HIGHEST))
    weights = low(scores * decay_mat)
    inner_part = jnp.einsum('hnm,mhb->nhb', weights, values, precision=HIGHEST)
    same_doc = (block_docs + 1 == previous).astype(float_type)
    carry_factor = same_doc[:, None] * jnp.exp((position + 1).astype(float_type)[:, None] * log_decay[None, :])
    query_carry = low(query_rot * carry_factor[:, :, None])
    outer_part = jnp.einsum('nha,hab->nhb', query_carry, low(state), precision=HIGHEST)
    mixed = low_back(inner_part + outer_part)
    grouped = group_norm(mixed).reshape(block_len, HEADS * VD)
    gated = low(block_pad[:, None] * jax.nn.silu(gate_pre) * grouped)
    hidden = block_rows + low_back(matmul(gated, output_weight))
    low_second = low(norm_rows(hidden, feed_gain, feed_bias))
    activation = low(jax.nn.gelu(low_back(matmul(low_second, up_weight)), approximate=False))
    result = hidden + low_back(matmul(activation, down_weight))
    last_doc = block_docs[block_len - 1]
    end_factor = (block_pad * (block_docs == last_doc).astype(float_type))[:, None] * jnp.exp((block_len - 1 - position).astype(float_type)[:, None] * log_decay[None, :])
    key_end = low(key_rot * end_factor[:, :, None])
    summary = low_back(jnp.einsum('nha,nhb->hab', key_end, values, precision=HIGHEST))
    keep_factor = (last_doc + 1 == previous).astype(float_type) * jnp.exp(float(block_len) * log_decay)
    new_state = summary + keep_factor[:, None, None] * state
    return (new_state.astype(state.dtype), result)

def reference(tokens, mix_gain, mix_bias, query_weight, key_weight, value_weight, gate_weight, output_weight, feed_gain, feed_bias, up_weight, down_weight, doc_ids, pad_mask, out_grad):
    doc_rows = doc_ids.astype(jnp.int32).reshape(N_TOK, TOK_DEV)
    pad_rows = pad_mask.astype(jnp.float32).reshape(N_TOK, TOK_DEV)
    previous = jnp.concatenate([jnp.zeros((1,), jnp.int32), (doc_rows[:-1, -1] + 1).astype(jnp.int32)])
    starts = (jnp.arange(N_TOK, dtype=jnp.int32) * TOK_DEV).astype(jnp.int32)

    def forward(inputs_all, *weight_list):
        block_step = jax.checkpoint(partial(layer_block, weight_list))
        blocks = inputs_all.reshape(N_TOK, TOK_DEV, D)
        zero_state = jnp.zeros((HEADS, KD, VD), inputs_all.dtype)
        final_state, out_rows = lax.scan(block_step, zero_state, (blocks, doc_rows, pad_rows.astype(inputs_all.dtype), previous, starts))
        return out_rows.reshape(TOKENS, D)
    result, pullback = jax.vjp(forward, tokens.astype(jnp.float32), mix_gain.astype(jnp.float32), mix_bias.astype(jnp.float32), query_weight.astype(jnp.float32), key_weight.astype(jnp.float32), value_weight.astype(jnp.float32), gate_weight.astype(jnp.float32), output_weight.astype(jnp.float32), feed_gain.astype(jnp.float32), feed_bias.astype(jnp.float32), up_weight.astype(jnp.float32), down_weight.astype(jnp.float32))
    grad_list = pullback(out_grad.astype(jnp.float32))
    return (result.astype(jnp.bfloat16), grad_list[0], grad_list[1], grad_list[2], grad_list[3], grad_list[4], grad_list[5], grad_list[6], grad_list[7], grad_list[8], grad_list[9], grad_list[10], grad_list[11])
```

```python
from functools import partial

import jax
import jax.numpy as jnp
from jax import lax
from jax.sharding import PartitionSpec as P

KD = 256
VD = 512
EPSILON = 1e-05
BF = jnp.bfloat16
F32 = jnp.float32


def after(value, *others):
    return lax.optimization_barrier((value, *others))[0]


def shifted(value, by):
    length = lax.axis_size("tok")
    pairs = [(i, i + by) for i in range(length) if 0 <= i + by < length]
    return lax.ppermute(value, "tok", pairs)


def swapped(value, bit):
    length = lax.axis_size("tok")
    return lax.ppermute(value, "tok", [(i, i ^ (1 << bit)) for i in range(length)])


def my_bit(bit):
    return (lax.axis_index("tok") >> bit) & 1


def bit_orders():
    bits = lax.axis_size("tok").bit_length() - 1
    first = list(range(bits))
    second = [0, 2, 1] if bits == 3 else first[bits // 2 :] + first[: bits // 2]
    return first, second


def halves(value, bit):
    pieces = value.reshape(2, value.shape[0] // 2, value.shape[1])
    mine = my_bit(bit)
    keep = lax.dynamic_index_in_dim(pieces, mine, 0, keepdims=False)
    give = lax.dynamic_index_in_dim(pieces, 1 - mine, 0, keepdims=False)
    return keep, give


def scatter_sum(value, order):
    for bit in order:
        keep, give = halves(value, bit)
        value = keep.astype(F32) + swapped(give.astype(BF), bit).astype(F32)
    return value.astype(BF)


def gather_back(value, order):
    for bit in order[::-1]:
        other = swapped(value, bit)
        low_first = my_bit(bit) == 0
        value = jnp.where(
            low_first,
            jnp.concatenate([value, other], axis=0),
            jnp.concatenate([other, value], axis=0),
        )
    return value.astype(F32)


def token_sum(first, second):
    order_one, order_two = bit_orders()
    one = scatter_sum(first, order_one)
    two = scatter_sum(second, order_two)
    return gather_back(one, order_one), gather_back(two, order_two)


def gather_rows(values):
    return lax.all_gather(values, "head", axis=1, tiled=True)


def sum_rows(values):
    return lax.psum_scatter(values.astype(BF), "head", scatter_dimension=1, tiled=True)


def my_columns(full, width):
    return lax.dynamic_slice_in_dim(full, lax.axis_index("head") * width, width, axis=-1)


def row_norm(rows):
    mean = jnp.mean(rows, axis=1)
    scale = lax.rsqrt(jnp.mean(rows * rows, axis=1) - mean * mean + EPSILON)
    return mean, scale


def rotate(values, cosine, sine, sign):
    half_dim = values.shape[-1] // 2
    front = values[..., :half_dim]
    back = values[..., half_dim:]
    sine = sine * sign
    return jnp.concatenate([front * cosine - back * sine, back * cosine + front * sine], axis=-1)


def group_norm(mixed):
    group_mean = jnp.mean(mixed, axis=-1, keepdims=True)
    group_var = jnp.mean(mixed * mixed, axis=-1, keepdims=True) - group_mean * group_mean
    return (mixed - group_mean) * lax.rsqrt(group_var + 1.0)


def body(
    tokens,
    mix_gain,
    mix_bias,
    query_weight,
    key_weight,
    value_weight,
    gate_weight,
    output_weight,
    feed_gain,
    feed_bias,
    up_weight,
    down_weight,
    doc_ids,
    pad_mask,
    out_grad,
):
    row_count, width = tokens.shape
    heads_here = query_weight.shape[1] // KD
    full_width = width * lax.axis_size("head")
    block = lax.axis_index("tok")
    blocks = lax.axis_size("tok")

    rows_raw = gather_rows(tokens)
    grad_rows = gather_rows(after(out_grad, rows_raw))

    vectors = lax.all_gather(
        jnp.stack([mix_gain, mix_bias, feed_gain, feed_bias]), "head", axis=1, tiled=True
    )
    last_docs = lax.all_gather(doc_ids[row_count - 1 :], "tok", axis=0, tiled=True)

    first_head = lax.axis_index("head") * heads_here
    log_decay = jnp.log(
        1.0 - 2.0 ** (-5.0 - (first_head + jnp.arange(heads_here, dtype=jnp.int32)).astype(F32))
    )
    position = jnp.arange(row_count, dtype=jnp.int32)
    frequency = 10000.0 ** (-2.0 * jnp.arange(KD // 2, dtype=jnp.int32).astype(F32) / KD)
    angles = (block * row_count + position).astype(F32)[:, None] * frequency[None, :]
    cosine, sine = jnp.cos(angles)[:, None, :], jnp.sin(angles)[:, None, :]
    padding = pad_mask.astype(F32)
    last_doc = doc_ids[row_count - 1]

    def doc_of(index):
        return last_docs[jnp.clip(index, 0, blocks - 1)]

    before = doc_of(block - 1)
    block_decay = jnp.exp(row_count * log_decay)
    back_two = (doc_of(block - 2) == before).astype(F32) * block_decay
    back_three = (doc_of(block - 3) == before).astype(F32) * block_decay * block_decay
    ahead_two = (doc_of(block + 1) == last_doc).astype(F32) * block_decay
    ahead_three = (doc_of(block + 2) == last_doc).astype(F32) * block_decay * block_decay

    distance = position[:, None] - position[None, :]
    allowed = ((doc_ids[:, None] == doc_ids[None, :]) & (distance >= 0)).astype(F32) * padding[
        None, :
    ]
    decay_mat = (
        jnp.exp(jnp.maximum(distance, 0).astype(F32)[None] * log_decay[:, None, None])
        * allowed[None]
    )
    carry_factor = ((doc_ids == before) & (block > 0)).astype(F32)[:, None] * jnp.exp(
        (position + 1).astype(F32)[:, None] * log_decay[None, :]
    )
    end_factor = (padding * (doc_ids == last_doc).astype(F32))[:, None] * jnp.exp(
        (row_count - 1 - position).astype(F32)[:, None] * log_decay[None, :]
    )

    rows_f = rows_raw.astype(F32)
    mean_first, rstd_first = row_norm(rows_f)
    rows_first = (
        (rows_f - mean_first[:, None]) * rstd_first[:, None] * vectors[0] + vectors[1]
    ).astype(BF)
    queries = jnp.dot(rows_first, query_weight, preferred_element_type=F32).reshape(
        row_count, heads_here, KD
    )
    key_proj = jnp.dot(rows_first, key_weight, preferred_element_type=F32).reshape(
        row_count, heads_here, KD
    )
    values = (
        jnp.dot(rows_first, value_weight, preferred_element_type=F32)
        .astype(BF)
        .reshape(row_count, heads_here, VD)
    )
    gate_pre = jnp.dot(rows_first, gate_weight, preferred_element_type=F32)
    query_rot = rotate(queries, cosine, sine, 1.0).astype(BF)
    key_rot = (rotate(key_proj, cosine, sine, 1.0) * KD ** (-0.5)).astype(BF)
    key_end = (key_rot * end_factor[:, :, None]).astype(BF)
    summary = jnp.einsum("nha,nhb->hab", key_end, values, preferred_element_type=F32).astype(BF)
    state_in = (
        shifted(summary, 1).astype(F32)
        + shifted(summary, 2).astype(F32) * back_two[:, None, None]
        + shifted(summary, 3).astype(F32) * back_three[:, None, None]
    )
    state_low = state_in.astype(BF)
    scores = jnp.einsum("nha,mha->hnm", query_rot, key_rot, preferred_element_type=F32)
    weights = (scores * decay_mat).astype(BF)
    inner_part = jnp.einsum("hnm,mhb->nhb", weights, values, preferred_element_type=F32)
    query_carry = (query_rot * carry_factor[:, :, None]).astype(BF)
    mixed = inner_part + jnp.einsum(
        "nha,hab->nhb", query_carry, state_low, preferred_element_type=F32
    )
    grouped, group_pull = jax.vjp(group_norm, mixed)
    gate_act, gate_pull = jax.vjp(jax.nn.silu, gate_pre)
    flat_group = grouped.reshape(row_count, heads_here * VD)
    gated = (padding[:, None] * gate_act * flat_group).astype(BF)
    hidden = tokens.astype(F32) + sum_rows(
        jnp.dot(gated, output_weight, preferred_element_type=F32)
    ).astype(F32)
    hidden_rows = gather_rows(hidden.astype(BF))
    hidden_f = hidden_rows.astype(F32)
    mean_second, rstd_second = row_norm(hidden_f)
    norm_rows = (hidden_f - mean_second[:, None]) * rstd_second[:, None]
    rows_second = (norm_rows * vectors[2] + vectors[3]).astype(BF)
    up_proj = jnp.dot(rows_second, up_weight, preferred_element_type=F32)
    activation, act_pull = jax.vjp(partial(jax.nn.gelu, approximate=False), up_proj)
    act_low = activation.astype(BF)
    grad_act = jnp.einsum("nd,fd->nf", grad_rows, down_weight, preferred_element_type=F32)
    grad_up = act_pull(grad_act)[0].astype(BF)
    grad_ln2_part = jnp.einsum("nf,df->nd", grad_up, up_weight, preferred_element_type=F32)
    grad_ln2 = sum_rows(grad_ln2_part).astype(F32)
    scaled_part = grad_ln2_part * vectors[2]
    sums_second = lax.psum(
        jnp.stack([jnp.sum(scaled_part, axis=1), jnp.sum(scaled_part * norm_rows, axis=1)]), "head"
    )
    down_part = jnp.dot(act_low, down_weight, preferred_element_type=F32).astype(BF)
    grad_down = jnp.einsum("nf,nd->fd", act_low, grad_rows, preferred_element_type=F32).astype(BF)
    grad_upw = jnp.einsum("nd,nf->df", rows_second, grad_up, preferred_element_type=F32).astype(BF)

    norm_second = (hidden - mean_second[:, None]) * rstd_second[:, None]
    grad_hidden = out_grad.astype(F32) + rstd_second[:, None] * (
        grad_ln2 * feed_gain
        - sums_second[0][:, None] / full_width
        - norm_second * sums_second[1][:, None] / full_width
    )
    column_second = jnp.stack([jnp.sum(grad_ln2 * norm_second, axis=0), jnp.sum(grad_ln2, axis=0)])
    grad_branch = gather_rows(grad_hidden.astype(BF))
    result = hidden + sum_rows(after(down_part, grad_branch)).astype(F32)
    layer_out = result.astype(BF)

    grad_down, grad_upw = token_sum(grad_down, grad_upw)

    grad_outw = jnp.einsum("nc,nd->cd", gated, grad_branch, preferred_element_type=F32).astype(BF)
    grad_gated = jnp.einsum("nd,cd->nc", grad_branch, output_weight, preferred_element_type=F32)
    grad_masked = grad_gated * padding[:, None]
    grad_gate = gate_pull(grad_masked * flat_group)[0].astype(BF)
    grad_mixed = group_pull((grad_masked * gate_act).reshape(row_count, heads_here, VD))[0].astype(
        BF
    )
    grad_gw = jnp.einsum("nd,nc->dc", rows_first, grad_gate, preferred_element_type=F32).astype(BF)
    grad_outw, grad_gw = token_sum(grad_outw, grad_gw)

    grad_state = jnp.einsum(
        "nha,nhb->hab", query_carry, grad_mixed, preferred_element_type=F32
    ).astype(BF)
    state_grad = (
        shifted(grad_state, -1).astype(F32)
        + shifted(grad_state, -2).astype(F32) * ahead_two[:, None, None]
        + shifted(grad_state, -3).astype(F32) * ahead_three[:, None, None]
    )
    state_grad_low = state_grad.astype(BF)
    grad_weights = jnp.einsum("nhb,mhb->hnm", grad_mixed, values, preferred_element_type=F32)
    grad_scores = (grad_weights * decay_mat).astype(BF)
    grad_query_rot = jnp.einsum(
        "hnm,mha->nha", grad_scores, key_rot, preferred_element_type=F32
    ) + carry_factor[:, :, None] * jnp.einsum(
        "nhb,hab->nha", grad_mixed, state_low, preferred_element_type=F32
    )
    grad_key_rot = jnp.einsum(
        "hnm,nha->mha", grad_scores, query_rot, preferred_element_type=F32
    ) + end_factor[:, :, None] * jnp.einsum(
        "nhb,hab->nha", values, state_grad_low, preferred_element_type=F32
    )
    grad_values = (
        (
            jnp.einsum("hnm,nhb->mhb", weights, grad_mixed, preferred_element_type=F32)
            + jnp.einsum("nha,hab->nhb", key_end, state_grad_low, preferred_element_type=F32)
        )
        .astype(BF)
        .reshape(row_count, heads_here * VD)
    )
    grad_queries = (
        rotate(grad_query_rot, cosine, sine, -1.0).astype(BF).reshape(row_count, heads_here * KD)
    )
    grad_keys = (
        (rotate(grad_key_rot, cosine, sine, -1.0) * KD ** (-0.5))
        .astype(BF)
        .reshape(row_count, heads_here * KD)
    )
    grad_ln1_part = (
        jnp.einsum("nc,dc->nd", grad_queries, query_weight, preferred_element_type=F32)
        + jnp.einsum("nc,dc->nd", grad_keys, key_weight, preferred_element_type=F32)
        + jnp.einsum("nc,dc->nd", grad_values, value_weight, preferred_element_type=F32)
        + jnp.einsum("nc,dc->nd", grad_gate, gate_weight, preferred_element_type=F32)
    )
    grad_ln1 = sum_rows(grad_ln1_part).astype(F32)
    norm_full = (rows_f - mean_first[:, None]) * rstd_first[:, None]
    scaled_one = grad_ln1_part * vectors[0]
    sums_first = lax.psum(
        jnp.stack([jnp.sum(scaled_one, axis=1), jnp.sum(scaled_one * norm_full, axis=1)]), "head"
    )
    query_key = jnp.concatenate([grad_queries, grad_keys], axis=1)
    grad_vw = jnp.einsum("nd,nc->dc", rows_first, grad_values, preferred_element_type=F32)
    grad_qkw = jnp.einsum("nd,nc->dc", rows_first, query_key, preferred_element_type=F32)
    grad_vw, grad_qkw = token_sum(grad_vw.astype(BF), grad_qkw.astype(BF))
    grad_qw, grad_kw = grad_qkw[:, : heads_here * KD], grad_qkw[:, heads_here * KD :]

    norm_first = (tokens.astype(F32) - mean_first[:, None]) * rstd_first[:, None]
    tokens_grad = grad_hidden + rstd_first[:, None] * (
        grad_ln1 * mix_gain
        - sums_first[0][:, None] / full_width
        - norm_first * sums_first[1][:, None] / full_width
    )
    column_first = jnp.stack([jnp.sum(grad_ln1 * norm_first, axis=0), jnp.sum(grad_ln1, axis=0)])
    columns = lax.psum(jnp.concatenate([column_first, column_second]), "tok")
    return (
        layer_out,
        tokens_grad,
        columns[0],
        columns[1],
        grad_qw,
        grad_kw,
        grad_vw,
        grad_gw,
        grad_outw,
        columns[2],
        columns[3],
        grad_upw,
        grad_down,
    )


def solution(mesh):
    rows = P("tok", "head")
    columns = P(None, "head")
    return jax.shard_map(
        body,
        mesh=mesh,
        in_specs=(
            rows,
            P("head"),
            P("head"),
            columns,
            columns,
            columns,
            columns,
            P("head", None),
            P("head"),
            P("head"),
            columns,
            P("head", None),
            P("tok"),
            P("tok"),
            rows,
        ),
        out_specs=(
            rows,
            rows,
            P("head"),
            P("head"),
            columns,
            columns,
            columns,
            columns,
            P("head", None),
            P("head"),
            P("head"),
            columns,
            P("head", None),
        ),
        check_vma=False,
    )
```

```python
from functools import partial

import jax
import jax.numpy as jnp
from jax import lax
from jax.experimental import pallas as pl
from jax.experimental.pallas import tpu as pltpu
from jax.sharding import PartitionSpec as P

KD = 256
VD = 512
EPSILON = 1e-05
BF = jnp.bfloat16
F32 = jnp.float32


def after(value, *others):
    return lax.optimization_barrier((value, *others))[0]


def shifted(value, by):
    length = lax.axis_size("tok")
    pairs = [(i, i + by) for i in range(length) if 0 <= i + by < length]
    return lax.ppermute(value, "tok", pairs)


def swapped(value, axis, mask):
    return lax.ppermute(value, axis, [(i, i ^ mask) for i in range(lax.axis_size(axis))])


def my_bit(axis, bit):
    return (lax.axis_index(axis) >> bit) & 1


def joined(value, other, first, axis):
    return jnp.where(
        first,
        jnp.concatenate([value, other], axis=axis),
        jnp.concatenate([other, value], axis=axis),
    )


def bit_orders():
    bits = lax.axis_size("tok").bit_length() - 1
    first = list(range(bits))
    second = [0, 2, 1] if bits == 3 else first[bits // 2 :] + first[: bits // 2]
    return first, second


def halves(value, axis, bit, dim):
    shape = value.shape
    pieces = value.reshape(*shape[:dim], 2, shape[dim] // 2, *shape[dim + 1 :])
    mine = my_bit(axis, bit)
    keep = lax.dynamic_index_in_dim(pieces, mine, dim, keepdims=False)
    give = lax.dynamic_index_in_dim(pieces, 1 - mine, dim, keepdims=False)
    return keep, give


def own_piece(value, order, dim=0):
    for bit in order:
        value = halves(value, "tok", bit, dim)[0]
    return value


def scatter_sum(value, order, dim=0, waits=()):
    values = []
    for place, bit in enumerate(order):
        keep, give = halves(value, "tok", bit, dim)
        if place == 1 and waits:
            give = after(give, *waits)
        value = keep.astype(F32) + swapped(give.astype(BF), "tok", 1 << bit).astype(F32)
        values.append(value)
    return values


def gather_back(value, order, dim=0):
    for bit in order[::-1]:
        other = swapped(value, "tok", 1 << bit)
        value = joined(value, other, my_bit("tok", bit) == 0, dim)
    return value


def in_order(pieces, order):
    bits, shape = len(order), pieces.shape
    pieces = pieces.reshape(*[2] * bits, *shape[1:])
    pieces = pieces.transpose(*[bits - 1 - bit for bit in order], bits, bits + 1)
    return pieces.reshape(shape[0] * shape[1], shape[2]).astype(F32)


def far_swap(first, second):
    rows = first.shape[0]
    both = jnp.concatenate([first, second.reshape(-1, first.shape[1])], axis=0)
    both = swapped(both, "head", lax.axis_size("head") // 2)
    return both[:rows], both[rows:].reshape(second.shape)


def side_bits():
    return range(lax.axis_size("head").bit_length() - 2)


def gather_side(value):
    for bit in side_bits():
        other = swapped(value, "head", 1 << bit)
        value = joined(value, other, my_bit("head", bit) == 0, 1)
    return value


def scatter_side(value):
    for bit in list(side_bits())[::-1]:
        keep, give = halves(value, "head", bit, 1)
        value = keep.astype(F32) + swapped(give.astype(BF), "head", 1 << bit).astype(F32)
    return value[:, 0]


def sum_side(value):
    for bit in side_bits():
        value = value + swapped(value, "head", 1 << bit)
    return value


TILE = 256
EXTRA = 16
CHUNK = 512
VMEM_LIMIT = 58 << 20


def dot(left, right):
    return jnp.dot(left, right, preferred_element_type=F32)


def dot_nt(left, right):
    return lax.dot_general(left, right, (((1,), (1,)), ((), ())), preferred_element_type=F32)


def dot_tn(left, right):
    return lax.dot_general(left, right, (((0,), (0,)), ((), ())), preferred_element_type=F32)


def tiles(columns):
    return pl.BlockSpec((TILE, columns), lambda i: (i, 0))


def whole(*shape):
    zeros = (0,) * len(shape)
    return pl.BlockSpec(shape, lambda i: zeros, pipeline_mode=pl.Buffered(1))


def held(*shape):
    zeros = (0,) * len(shape)
    return pl.BlockSpec(shape, lambda i: zeros)


SCALARS = pl.BlockSpec(memory_space=pltpu.SMEM)


def call(kernel, rows, in_specs, outs, out_specs, scratch=()):
    return pl.pallas_call(
        kernel,
        grid=(rows // TILE,),
        in_specs=in_specs,
        out_specs=out_specs,
        out_shape=[jax.ShapeDtypeStruct(shape, dtype) for shape, dtype in outs],
        scratch_shapes=list(scratch),
        cost_estimate=pl.CostEstimate(flops=0, bytes_accessed=0, transcendentals=0),
        compiler_params=pltpu.CompilerParams(vmem_limit_bytes=VMEM_LIMIT),
    )


def turned(value, cosine, sine):
    half_dim = KD // 2
    front, back = value[:, :half_dim], value[:, half_dim:]
    return jnp.concatenate([front * cosine - back * sine, back * cosine + front * sine], axis=1)


def tile_decay(log_decay, behind, docs_col, docs_row, pads_row):
    rows = lax.broadcasted_iota(jnp.int32, (TILE, 1), 0)
    cols = lax.broadcasted_iota(jnp.int32, (1, TILE), 1)
    allowed = (docs_col == docs_row) & (rows + behind >= cols) & (pads_row > 0)
    rise = jnp.exp(rows.astype(F32) * log_decay)
    fall = jnp.exp((behind - cols).astype(F32) * log_decay)
    return jnp.where(allowed, rise * fall, 0.0)


def send_state(docs, acc, sum_out):
    sum_out[:, :KD, :] = acc[...].astype(BF)
    sum_out[:, KD:, :] = jnp.full((acc.shape[0], EXTRA, VD), docs[0].astype(F32), F32).astype(BF)


def lanes(shards):
    return jnp.concatenate([shards[i] for i in range(shards.shape[0])], axis=1)


def vector_of(rows, index):
    return rows[3 * index : 3 * index + 1] + rows[3 * index + 1 : 3 * index + 2] + rows[
        3 * index + 2 : 3 * index + 3
    ]


def entry_kernel(x, one, two, three, four, out):
    rows = x.shape[0]
    out[:rows] = x[...]
    pieces = []
    for vector in (one, two, three, four):
        value = vector[...]
        for _ in range(3):
            piece = value.astype(BF)
            pieces.append(piece.astype(F32))
            value = value - piece.astype(F32)
    pieces.append(jnp.zeros((EXTRA - len(pieces), x.shape[1]), F32))
    out[rows:] = jnp.concatenate(pieces, axis=0).astype(BF)


def project_kernel(
    heads, docs, x, vec, wq, wk, wv, cos, sin, end, ln_out, q_out, k_out, v_out, stat_out,
    sum_out, acc
):
    step = pl.program_id(0)
    rows = lanes(x).astype(F32)
    vectors = lanes(vec).astype(F32)
    mean = jnp.mean(rows, axis=1, keepdims=True)
    scale = lax.rsqrt(jnp.mean(rows * rows, axis=1, keepdims=True) - mean * mean + EPSILON)
    low = ((rows - mean) * scale * vector_of(vectors, 0) + vector_of(vectors, 1)).astype(BF)
    ln_out[...] = low
    stat_out[...] = jnp.concatenate([mean, scale], axis=1)
    values = dot(low, wv[...]).astype(BF)
    v_out[...] = values
    queries = dot(low, wq[...])
    keys = dot(low, wk[...])
    cosine, sine = cos[...], sin[...]

    @pl.when(step == 0)
    def _():
        acc[...] = jnp.zeros_like(acc)

    for h in range(heads):
        mine = slice(h * KD, (h + 1) * KD)
        q_out[:, mine] = turned(queries[:, mine], cosine, sine).astype(BF)
        key = (turned(keys[:, mine], cosine, sine) * KD ** (-0.5)).astype(BF)
        k_out[:, mine] = key
        key_end = (key.astype(F32) * end[:, h : h + 1]).astype(BF)
        acc[h] += dot_tn(key_end, values[:, h * VD : (h + 1) * VD])

    @pl.when(step == pl.num_programs(0) - 1)
    def _():
        send_state(docs, acc, sum_out)


def inner_kernel(heads, decay, low, wg, q, k, v, dcol, drow, prow, gate_out, inner_out):
    step = pl.program_id(0)
    gate_out[...] = dot(low[...], wg[...])
    docs_col = dcol[...]

    def turn(j, totals):
        at = pl.ds(pl.multiple_of(j * TILE, TILE), TILE)
        sums = []
        for h in range(heads):
            mine = slice(h * KD, (h + 1) * KD)
            wide = slice(h * VD, (h + 1) * VD)
            factor = tile_decay(decay[h], (step - j) * TILE, docs_col, drow[:, at], prow[:, at])
            weights = (dot_nt(q[:, mine], k[at, mine]) * factor).astype(BF)
            sums.append(totals[h] + dot(weights, v[at, wide]))
        return tuple(sums)

    zeros = tuple(jnp.zeros((TILE, VD), F32) for _ in range(heads))
    totals = lax.fori_loop(0, step + 1, turn, zeros)
    for h in range(heads):
        inner_out[:, h * VD : (h + 1) * VD] = totals[h]


def joined_state(decay, rows, one, two, three, link_two, link_three):
    states = []
    for h in range(one.shape[0]):
        far = jnp.exp(jnp.full((1, 1), rows, F32) * decay[h])
        states.append(
            (
                one[h, :KD].astype(F32)
                + two[h, :KD].astype(F32) * (link_two * far)
                + three[h, :KD].astype(F32) * (link_three * far * far)
            ).astype(BF)
        )
    return states


def doc_in(payload):
    return payload[0, KD : KD + 1, 0:1].astype(F32)


def mix_kernel(
    heads, rows, decay, inner, q, one, two, three, gate, dcol, pcol, wo, group_out, scale_out,
    gated_out, part_out, state_out, carry_out
):
    step = pl.program_id(0)
    before = doc_in(one)

    @pl.when(step == 0)
    def _():
        link_two = (doc_in(two) == before).astype(F32)
        link_three = (doc_in(three) == before).astype(F32)
        states = joined_state(decay, rows, one, two, three, link_two, link_three)
        for h in range(heads):
            state_out[h] = states[h]

    same = (dcol[...].astype(F32) == before).astype(F32)
    place = (step * TILE + 1 + lax.broadcasted_iota(jnp.int32, (TILE, 1), 0)).astype(F32)
    for h in range(heads):
        mine = slice(h * KD, (h + 1) * KD)
        wide = slice(h * VD, (h + 1) * VD)
        carry = same * jnp.exp(place * decay[h])
        carry_out[:, h : h + 1] = carry
        carried = (q[:, mine].astype(F32) * carry).astype(BF)
        mixed = inner[:, wide] + dot(carried, state_out[h])
        mean = jnp.mean(mixed, axis=1, keepdims=True)
        scale = lax.rsqrt(jnp.mean(mixed * mixed, axis=1, keepdims=True) - mean * mean + 1.0)
        grouped = (mixed - mean) * scale
        group_out[:, wide] = grouped
        scale_out[:, h : h + 1] = scale
        gate_h = gate[:, wide]
        gated_out[:, wide] = (pcol[...] * gate_h * jax.nn.sigmoid(gate_h) * grouped).astype(BF)
    part = dot(gated_out[...], wo[...]).astype(BF)
    sides, width = part_out.shape[1], part_out.shape[4]
    for side in range(sides):
        for f in range(2):
            first = (f * sides + side) * width
            part_out[0, side, f] = part[:, first : first + width]


def gate_kernel(heads, grad, wo, gate, group, scale, pcol, dgate_out, mix_out):
    sides = grad.shape[1]
    rows = jnp.concatenate(
        [grad[0, side, f] for f in range(2) for side in range(sides)], axis=1
    )
    passed = dot_nt(rows, wo[...]) * pcol[...]
    for h in range(heads):
        wide = slice(h * VD, (h + 1) * VD)
        gate_h, grouped = gate[:, wide], group[:, wide]
        squash = jax.nn.sigmoid(gate_h)
        upstream = passed[:, wide]
        dgate_out[:, wide] = (
            upstream * grouped * (squash + gate_h * squash * (1.0 - squash))
        ).astype(BF)
        grad_group = upstream * gate_h * squash
        mean = jnp.mean(grad_group, axis=1, keepdims=True)
        cross = jnp.mean(grad_group * grouped, axis=1, keepdims=True)
        mix_out[:, wide] = (scale[:, h : h + 1] * (grad_group - mean - grouped * cross)).astype(BF)


def outer_kernel(gated, grad, out):
    rows = jnp.concatenate([grad[0, 0, 0], grad[1, 0, 0]], axis=0)
    out[...] = dot_tn(gated[...], rows).astype(BF)


def back_kernel(
    heads, docs, decay, mix, q, k, v, carry, state, dcol, drow, prow, cos, sin, dq_out, dk_out,
    dv_out, sum_out, acc
):
    step = pl.program_id(0)

    @pl.when(step == 0)
    def _():
        acc[...] = jnp.zeros_like(acc)
        dk_out[...] = jnp.zeros_like(dk_out)
        dv_out[...] = jnp.zeros_like(dv_out)

    docs_col = dcol[...]

    def turn(j, totals):
        at = pl.ds(pl.multiple_of(j * TILE, TILE), TILE)
        sums = []
        for h in range(heads):
            mine = slice(h * KD, (h + 1) * KD)
            wide = slice(h * VD, (h + 1) * VD)
            query, grad_mixed, key = q[:, mine], mix[:, wide], k[at, mine]
            factor = tile_decay(decay[h], (step - j) * TILE, docs_col, drow[:, at], prow[:, at])
            weights = (dot_nt(query, key) * factor).astype(BF)
            grads = (dot_nt(grad_mixed, v[at, wide]) * factor).astype(BF)
            dk_out[at, mine] += dot_tn(grads, query)
            dv_out[at, wide] += dot_tn(weights, grad_mixed)
            sums.append(totals[h] + dot(grads, key))
        return tuple(sums)

    zeros = tuple(jnp.zeros((TILE, KD), F32) for _ in range(heads))
    totals = lax.fori_loop(0, step + 1, turn, zeros)
    for h in range(heads):
        mine = slice(h * KD, (h + 1) * KD)
        wide = slice(h * VD, (h + 1) * VD)
        lift = carry[:, h : h + 1]
        total = totals[h] + lift * dot_nt(mix[:, wide], state[h])
        dq_out[:, mine] = turned(total, cos[...], -sin[...]).astype(BF)
        acc[h] += dot_tn((q[:, mine].astype(F32) * lift).astype(BF), mix[:, wide])

    @pl.when(step == pl.num_programs(0) - 1)
    def _():
        send_state(docs, acc, sum_out)


def finish_kernel(
    heads, size, docs, decay, dk_in, dv_in, k, v, end, one, two, three, dq, dgate, wq, wk, wv, wg,
    cos, sin, x, stat, vec, dk_out, dv_out, part_out, rows_out, cols_out, state
):
    step = pl.program_id(0)

    @pl.when(step == 0)
    def _():
        last = docs[0].astype(F32)
        link_two = (doc_in(one) == last).astype(F32)
        link_three = (doc_in(two) == last).astype(F32)
        states = joined_state(decay, size, one, two, three, link_two, link_three)
        for h in range(heads):
            state[h] = states[h]

    cosine, sine = cos[...], -sin[...]
    for h in range(heads):
        mine = slice(h * KD, (h + 1) * KD)
        wide = slice(h * VD, (h + 1) * VD)
        lift = end[:, h : h + 1]
        grad_key = dk_in[:, mine] + lift * dot_nt(v[:, wide], state[h])
        dk_out[:, mine] = (turned(grad_key, cosine, sine) * KD ** (-0.5)).astype(BF)
        key_end = (k[:, mine].astype(F32) * lift).astype(BF)
        dv_out[:, wide] = (dv_in[:, wide] + dot(key_end, state[h])).astype(BF)
    part = (
        dot_nt(dq[...], wq[...])
        + dot_nt(dk_out[...], wk[...])
        + dot_nt(dv_out[...], wv[...])
        + dot_nt(dgate[...], wg[...])
    )
    count, width = part_out.shape[0], part_out.shape[2]
    for shard in range(count):
        part_out[shard] = part[:, shard * width : (shard + 1) * width].astype(BF)
    normed = (lanes(x).astype(F32) - stat[:, 0:1]) * stat[:, 1:2]
    scaled = part * vec[0:1, :]
    ones = jnp.ones((8, scaled.shape[1]), BF)
    rows_out[0, 0:8] = dot_nt(ones, scaled.astype(BF))
    rows_out[0, 8:16] = dot_nt(ones, (scaled * normed).astype(BF))
    sums = jnp.concatenate(
        [jnp.sum(part * normed, axis=0, keepdims=True), jnp.sum(part, axis=0, keepdims=True)],
        axis=0,
    )

    @pl.when(step == 0)
    def _():
        cols_out[...] = jnp.zeros_like(cols_out)

    cols_out[...] += sums


def feed_kernel(
    chunks, x, grads, vec, up_near, up_far, down_near, down_far, ln_out, grad_out, act_out,
    dup_out, part_out, stat_out, rows_out, cols_out, acc
):
    step = pl.program_id(0)
    count = x.shape[1]
    steps = count // TILE

    def at_rows(r):
        return pl.ds(pl.multiple_of(r * TILE, TILE), TILE)

    @pl.when(step == 0)
    def _():
        def start(r, carry):
            at = at_rows(r)
            rows = jnp.concatenate([x[i, at, :] for i in range(x.shape[0])], axis=1).astype(F32)
            mean = jnp.mean(rows, axis=1, keepdims=True)
            scale = lax.rsqrt(jnp.mean(rows * rows, axis=1, keepdims=True) - mean * mean + EPSILON)
            stat_out[at, :] = jnp.concatenate([mean, scale], axis=1)
            ln_out[at, :] = ((rows - mean) * scale * vec[2:3, :] + vec[3:4, :]).astype(BF)
            grad_out[at, :] = jnp.concatenate(
                [grads[i, at, :] for i in range(grads.shape[0])], axis=1
            )
            acc[at, :] = jnp.zeros((TILE, acc.shape[1]), F32)
            return carry

        lax.fori_loop(0, steps, start, 0)

    def units(up, down):
        def turn(r, carry):
            at = at_rows(r)
            lifted = dot(ln_out[at, :], up[...])
            share = 0.5 * (1.0 + lax.erf(lifted * 0.5**0.5))
            act_out[at, :] = (lifted * share).astype(BF)
            slope = share + lifted * jnp.exp(-0.5 * lifted * lifted) * 0.3989422804014327
            lowered = (slope * dot_nt(grad_out[at, :], down[...])).astype(BF)
            dup_out[at, :] = lowered
            acc[at, :] += dot_nt(lowered, up[...])
            return carry

        lax.fori_loop(0, steps, turn, 0)

    @pl.when(step < chunks)
    def _():
        units(up_near, down_near)

    @pl.when(step >= chunks)
    def _():
        units(up_far, down_far)

    @pl.when(step == pl.num_programs(0) - 1)
    def _():
        cols_out[...] = jnp.zeros_like(cols_out)
        sides, width = part_out.shape[1], part_out.shape[3]

        def finish(r, carry):
            at = at_rows(r)
            part = acc[at, :]
            for f in range(2):
                for side in range(sides):
                    first = (f * sides + side) * width
                    part_out[f, side, at, :] = part[:, first : first + width].astype(BF)
            rows = jnp.concatenate([x[i, at, :] for i in range(x.shape[0])], axis=1).astype(F32)
            normed = (rows - stat_out[at, 0:1]) * stat_out[at, 1:2]
            scaled = part * vec[2:3, :]
            rows_out[at, :] = jnp.concatenate(
                [
                    jnp.sum(scaled, axis=1, keepdims=True),
                    jnp.sum(scaled * normed, axis=1, keepdims=True),
                ],
                axis=1,
            )
            cols_out[...] += jnp.concatenate(
                [
                    jnp.sum(part * normed, axis=0, keepdims=True),
                    jnp.sum(part, axis=0, keepdims=True),
                ],
                axis=0,
            )
            return carry

        lax.fori_loop(0, steps, finish, 0)


def lower_kernel(act, down_near, down_far, out):
    units = down_near.shape[0]
    part = (dot(act[:, :units], down_near[...]) + dot(act[:, units:], down_far[...])).astype(BF)
    sides, width = out.shape[1], out.shape[3]
    for f in range(2):
        for side in range(sides):
            first = (f * sides + side) * width
            out[f, side] = part[:, first : first + width]


def weight_kernel(left, *rights):
    out = rights[-1]
    first = 0
    for right in rights[:-1]:
        width = right.shape[1]
        out[:, first : first + width] = dot_tn(left[...], right[...]).astype(BF)
        first += width


def weight_grad(left, *rights):
    rows, columns = left.shape
    width = sum(right.shape[1] for right in rights)
    return pl.pallas_call(
        weight_kernel,
        grid=(columns // CHUNK,),
        in_specs=[pl.BlockSpec((rows, CHUNK), lambda i: (0, i))]
        + [whole(*right.shape) for right in rights],
        out_specs=pl.BlockSpec((CHUNK, width), lambda i: (i, 0)),
        out_shape=jax.ShapeDtypeStruct((columns, width), BF),
        cost_estimate=pl.CostEstimate(flops=0, bytes_accessed=0, transcendentals=0),
        compiler_params=pltpu.CompilerParams(vmem_limit_bytes=VMEM_LIMIT),
    )(left, *rights)


def body(
    tokens,
    mix_gain,
    mix_bias,
    query_weight,
    key_weight,
    value_weight,
    gate_weight,
    output_weight,
    feed_gain,
    feed_bias,
    up_weight,
    down_weight,
    doc_ids,
    pad_mask,
    out_grad,
):
    row_count, width = tokens.shape
    heads_here = query_weight.shape[1] // KD
    shards = lax.axis_size("head")
    full_width = width * shards
    sides = shards // 2
    spread = lax.axis_index("head") // sides
    side = lax.axis_index("head") % sides
    half_rows = row_count // 2
    block = lax.axis_index("tok")

    packed = pl.pallas_call(
        entry_kernel,
        out_shape=jax.ShapeDtypeStruct((row_count + EXTRA, width), BF),
        compiler_params=pltpu.CompilerParams(vmem_limit_bytes=VMEM_LIMIT),
    )(tokens, mix_gain[None], mix_bias[None], feed_gain[None], feed_bias[None])
    rows_raw = lax.all_gather(packed, "head", axis=0)
    vector_rows = rows_raw[:, row_count:, :].astype(F32)
    vectors = (vector_rows[:, 0:12:3] + vector_rows[:, 1:12:3] + vector_rows[:, 2:12:3]).transpose(
        1, 0, 2
    )
    side_vectors = lax.dynamic_index_in_dim(
        vectors.reshape(4, 2, sides, width), side, 2, keepdims=False
    )
    vectors = vectors.reshape(4, full_width)

    order_one, order_two = bit_orders()
    up_piece, down_piece = own_piece(up_weight, order_one), own_piece(down_weight, order_two)
    late_up, late_down, late_grad, _ = lax.optimization_barrier(
        (up_piece, down_piece, out_grad, rows_raw)
    )
    up_seen, down_seen = far_swap(late_up, late_down)
    grad_keep, grad_give = halves(late_grad, "head", shards.bit_length() - 2, 0)
    side_grads = joined(
        grad_keep[None], swapped(grad_give, "head", sides)[None], spread == 0, 0
    )
    grad_rows = gather_side(side_grads[:, None]).reshape(shards, half_rows, width)
    up_other = gather_back(up_seen, order_one)
    down_other = gather_back(down_seen, order_two)

    first_head = lax.axis_index("head") * heads_here
    log_decay = jnp.log(
        1.0 - 2.0 ** (-5.0 - (first_head + jnp.arange(heads_here, dtype=jnp.int32)).astype(F32))
    )
    position = jnp.arange(row_count, dtype=jnp.int32)
    frequency = 10000.0 ** (-2.0 * jnp.arange(KD // 2, dtype=jnp.int32).astype(F32) / KD)
    angles = (block * row_count + position).astype(F32)[:, None] * frequency[None, :]
    cosine, sine = jnp.cos(angles), jnp.sin(angles)
    padding = pad_mask.astype(F32)
    last_doc = doc_ids[row_count - 1]

    end_factor = (padding * (doc_ids == last_doc).astype(F32))[:, None] * jnp.exp(
        (row_count - 1 - position).astype(F32)[:, None] * log_decay[None, :]
    )

    docs_col, docs_row = doc_ids[:, None], doc_ids[None, :]
    pads_col, pads_row = padding[:, None], padding[None, :]
    inner_width, value_width = heads_here * KD, heads_here * VD
    states = pltpu.VMEM((heads_here, KD, VD), F32)
    state_shape = (heads_here, KD, VD)
    sent_shape = (heads_here, KD + EXTRA, VD)
    shard_tiles = pl.BlockSpec((shards, TILE, width), lambda i: (0, i, 0))
    per_half = half_rows // TILE
    split_tiles = pl.BlockSpec(
        (1, sides, 2, TILE, width), lambda i: (i // per_half, 0, 0, i % per_half, 0)
    )
    last_docs = doc_ids[row_count - 1 :]
    rows_first, query_rot, key_rot, values, stats, summary = call(
        partial(project_kernel, heads_here),
        row_count,
        [
            SCALARS,
            shard_tiles,
            pl.BlockSpec((shards, EXTRA, width), lambda i: (0, row_count // EXTRA, 0)),
            whole(full_width, inner_width),
            whole(full_width, inner_width),
            whole(full_width, value_width),
            tiles(KD // 2),
            tiles(KD // 2),
            tiles(heads_here),
        ],
        [
            ((row_count, full_width), BF),
            ((row_count, inner_width), BF),
            ((row_count, inner_width), BF),
            ((row_count, value_width), BF),
            ((row_count, 2), F32),
            (sent_shape, BF),
        ],
        [
            tiles(full_width),
            tiles(inner_width),
            tiles(inner_width),
            tiles(value_width),
            tiles(2),
            held(*sent_shape),
        ],
        [states],
    )(
        last_docs,
        rows_raw,
        rows_raw,
        query_weight,
        key_weight,
        value_weight,
        cosine,
        sine,
        end_factor,
    )
    one_back, two_back, three_back = (shifted(summary, by) for by in (1, 2, 3))
    gate_pre, inner_part = call(
        partial(inner_kernel, heads_here),
        row_count,
        [
            SCALARS,
            tiles(full_width),
            whole(full_width, value_width),
            tiles(inner_width),
            whole(row_count, inner_width),
            whole(row_count, value_width),
            tiles(1),
            whole(1, row_count),
            whole(1, row_count),
        ],
        [((row_count, value_width), F32)] * 2,
        [tiles(value_width)] * 2,
    )(
        log_decay,
        rows_first,
        gate_weight,
        query_rot,
        key_rot,
        values,
        docs_col,
        docs_row,
        pads_row,
    )
    flat_group, group_scale, gated, mix_part, state_low, carry_factor = call(
        partial(mix_kernel, heads_here, row_count),
        row_count,
        [
            SCALARS,
            tiles(value_width),
            tiles(inner_width),
            whole(*sent_shape),
            whole(*sent_shape),
            whole(*sent_shape),
            tiles(value_width),
            tiles(1),
            tiles(1),
            whole(value_width, full_width),
        ],
        [
            ((row_count, value_width), F32),
            ((row_count, heads_here), F32),
            ((row_count, value_width), BF),
            ((2, sides, 2, half_rows, width), BF),
            (state_shape, BF),
            ((row_count, heads_here), F32),
        ],
        [
            tiles(value_width),
            tiles(heads_here),
            tiles(value_width),
            split_tiles,
            held(*state_shape),
            tiles(heads_here),
        ],
    )(
        after(log_decay, side_grads),
        inner_part,
        query_rot,
        one_back,
        two_back,
        three_back,
        gate_pre,
        docs_col,
        pads_col,
        output_weight,
    )
    mix_part = after(mix_part, up_seen, down_seen)
    side_tokens = lax.dynamic_index_in_dim(
        lax.dynamic_slice_in_dim(rows_raw, spread * half_rows, half_rows, axis=1).reshape(
            2, sides, half_rows, width
        ),
        side,
        1,
        keepdims=False,
    )
    mixed_sum = lax.psum_scatter(
        mix_part.reshape(shards, 2, half_rows, width), "head", scatter_dimension=0
    )
    hidden = side_tokens.astype(F32) + mixed_sum.astype(F32)
    hidden_rows = gather_side(hidden.astype(BF)[:, None]).reshape(shards, half_rows, width)
    units = up_weight.shape[1]
    chunks = units // CHUNK
    rows_second, grad_plain, act_low, grad_up, feed_part, stats_second, row_second, cols_second = (
        pl.pallas_call(
            partial(feed_kernel, chunks),
            grid=(2 * chunks,),
            in_specs=[
                whole(shards, half_rows, width),
                whole(shards, half_rows, width),
                whole(4, full_width),
                pl.BlockSpec((full_width, CHUNK), lambda i: (0, jnp.minimum(i, chunks - 1))),
                pl.BlockSpec((full_width, CHUNK), lambda i: (0, jnp.maximum(i - chunks, 0))),
                pl.BlockSpec((CHUNK, full_width), lambda i: (jnp.minimum(i, chunks - 1), 0)),
                pl.BlockSpec((CHUNK, full_width), lambda i: (jnp.maximum(i - chunks, 0), 0)),
            ],
            out_specs=[
                held(half_rows, full_width),
                held(half_rows, full_width),
                pl.BlockSpec((half_rows, CHUNK), lambda i: (0, i)),
                pl.BlockSpec((half_rows, CHUNK), lambda i: (0, i)),
                held(2, sides, half_rows, width),
                held(half_rows, 2),
                held(half_rows, 2),
                held(2, full_width),
            ],
            out_shape=[
                jax.ShapeDtypeStruct((half_rows, full_width), BF),
                jax.ShapeDtypeStruct((half_rows, full_width), BF),
                jax.ShapeDtypeStruct((half_rows, 2 * units), BF),
                jax.ShapeDtypeStruct((half_rows, 2 * units), BF),
                jax.ShapeDtypeStruct((2, sides, half_rows, width), BF),
                jax.ShapeDtypeStruct((half_rows, 2), F32),
                jax.ShapeDtypeStruct((half_rows, 2), F32),
                jax.ShapeDtypeStruct((2, full_width), F32),
            ],
            scratch_shapes=[pltpu.VMEM((half_rows, full_width), F32)],
            cost_estimate=pl.CostEstimate(flops=0, bytes_accessed=0, transcendentals=0),
            compiler_params=pltpu.CompilerParams(vmem_limit_bytes=VMEM_LIMIT),
        )(hidden_rows, grad_rows, vectors, up_weight, up_other, down_weight, down_other)
    )
    grad_ln2 = scatter_side(feed_part)
    row_second = sum_side(row_second) / full_width
    norm_second = (hidden - stats_second[None, :, 0:1]) * stats_second[None, :, 1:2]
    grad_hidden = side_grads.astype(F32) + stats_second[None, :, 1:2] * (
        grad_ln2 * side_vectors[2][:, None, :]
        - row_second[None, :, 0:1]
        - norm_second * row_second[None, :, 1:2]
    )
    grad_branch = lax.all_gather(grad_hidden.astype(BF), "head", axis=0).reshape(
        2, sides, 2, half_rows, width
    )

    down_part = pl.pallas_call(
        lower_kernel,
        grid=(half_rows // TILE,),
        in_specs=[tiles(2 * units), whole(units, full_width), whole(units, full_width)],
        out_specs=pl.BlockSpec((2, sides, TILE, width), lambda i: (0, 0, i, 0)),
        out_shape=jax.ShapeDtypeStruct((2, sides, half_rows, width), BF),
        cost_estimate=pl.CostEstimate(flops=0, bytes_accessed=0, transcendentals=0),
        compiler_params=pltpu.CompilerParams(vmem_limit_bytes=VMEM_LIMIT),
    )(act_low, down_weight, down_other)

    branch = grad_hidden.astype(BF)
    grad_down = weight_grad(after(act_low, branch), grad_plain)
    grad_down = grad_down.reshape(2, units, full_width)
    grad_upw = weight_grad(rows_second, after(grad_up, branch))
    down_sum = scatter_sum(grad_down, order_one, 1)
    up_sum = scatter_sum(grad_upw, order_two)

    grad_outw = pl.pallas_call(
        outer_kernel,
        grid=(shards,),
        in_specs=[
            whole(row_count, value_width),
            pl.BlockSpec((2, 1, 1, half_rows, width), lambda i: (0, i % sides, i // sides, 0, 0)),
        ],
        out_specs=pl.BlockSpec((value_width, width), lambda i: (0, i)),
        out_shape=jax.ShapeDtypeStruct((value_width, full_width), BF),
        cost_estimate=pl.CostEstimate(flops=0, bytes_accessed=0, transcendentals=0),
        compiler_params=pltpu.CompilerParams(vmem_limit_bytes=VMEM_LIMIT),
    )(after(gated, down_sum[1], up_sum[1]), grad_branch)
    outw_sum = scatter_sum(grad_outw, order_one)
    dgate, grad_mixed = call(
        partial(gate_kernel, heads_here),
        row_count,
        [
            split_tiles,
            whole(value_width, full_width),
            tiles(value_width),
            tiles(value_width),
            tiles(heads_here),
            tiles(1),
        ],
        [((row_count, value_width), BF), ((row_count, value_width), BF)],
        [tiles(value_width), tiles(value_width)],
    )(
        grad_branch,
        output_weight,
        gate_pre,
        flat_group,
        group_scale,
        after(pads_col, grad_outw),
    )
    up_last, down_last = up_sum[-1], down_sum[-1]
    up_far, down_far = far_swap(up_last[:, units:].astype(BF), down_last[1].astype(BF))
    down_near = down_last[0] + down_far.astype(F32)
    up_near = up_last[:, :units] + up_far.astype(F32)
    grad_gw = weight_grad(rows_first, dgate)
    dq, dk_part, dv_part, grad_state = call(
        partial(back_kernel, heads_here),
        row_count,
        [
            SCALARS,
            SCALARS,
            tiles(value_width),
            tiles(inner_width),
            whole(row_count, inner_width),
            whole(row_count, value_width),
            tiles(heads_here),
            whole(*state_shape),
            tiles(1),
            whole(1, row_count),
            whole(1, row_count),
            tiles(KD // 2),
            tiles(KD // 2),
        ],
        [
            ((row_count, inner_width), BF),
            ((row_count, inner_width), F32),
            ((row_count, value_width), F32),
            (sent_shape, BF),
        ],
        [
            tiles(inner_width),
            held(row_count, inner_width),
            held(row_count, value_width),
            held(*sent_shape),
        ],
        [states],
    )(
        last_docs,
        after(log_decay, down_last, up_last, outw_sum[0], down_part),
        grad_mixed,
        query_rot,
        key_rot,
        values,
        carry_factor,
        state_low,
        docs_col,
        docs_row,
        pads_row,
        cosine,
        sine,
    )
    gw_sum = scatter_sum(grad_gw, order_two)
    one_on, two_on, three_on = (shifted(grad_state, -by) for by in (1, 2, 3))
    dk, dv, last_part, row_sums, column_first = call(
        partial(finish_kernel, heads_here, row_count),
        row_count,
        [
            SCALARS,
            SCALARS,
            tiles(inner_width),
            tiles(value_width),
            tiles(inner_width),
            tiles(value_width),
            tiles(heads_here),
            whole(*sent_shape),
            whole(*sent_shape),
            whole(*sent_shape),
            tiles(inner_width),
            tiles(value_width),
            whole(full_width, inner_width),
            whole(full_width, inner_width),
            whole(full_width, value_width),
            whole(full_width, value_width),
            tiles(KD // 2),
            tiles(KD // 2),
            shard_tiles,
            tiles(2),
            whole(4, full_width),
        ],
        [
            ((row_count, inner_width), BF),
            ((row_count, value_width), BF),
            ((shards, row_count + EXTRA, width), BF),
            ((row_count // TILE, 16, TILE), F32),
            ((2, full_width), F32),
        ],
        [
            tiles(inner_width),
            tiles(value_width),
            shard_tiles,
            pl.BlockSpec((1, 16, TILE), lambda i: (i, 0, 0)),
            held(2, full_width),
        ],
        [pltpu.VMEM(state_shape, BF)],
    )(
        last_docs,
        after(log_decay, down_near, up_near, outw_sum[1], gw_sum[0]),
        dk_part,
        dv_part,
        key_rot,
        values,
        end_factor,
        one_on,
        two_on,
        three_on,
        dq,
        dgate,
        query_weight,
        key_weight,
        value_weight,
        gate_weight,
        cosine,
        sine,
        rows_raw,
        stats,
        vectors,
    )
    count = row_count // TILE
    line = jnp.concatenate([row_sums[:, 0], row_sums[:, 8]], axis=0)
    line = jnp.pad(line, ((0, EXTRA - 2 * count - 4), (0, width - TILE)))
    columns = jnp.concatenate([column_first, cols_second]).reshape(4, shards, width)
    extra = jnp.concatenate(
        [jnp.broadcast_to(line[None], (shards, *line.shape)), columns.transpose(1, 0, 2)], axis=1
    )
    last_part = lax.dynamic_update_slice_in_dim(last_part, extra.astype(BF), row_count, axis=1)
    last_sum = lax.psum_scatter(last_part, "head", scatter_dimension=0).astype(F32)
    grad_ln1 = last_sum[:row_count]
    sums_first = last_sum[row_count:, :TILE] / full_width
    sums_first = jnp.stack(
        [sums_first[:count].reshape(row_count), sums_first[count : 2 * count].reshape(row_count)],
        axis=1,
    )
    columns = lax.psum(last_sum[row_count + EXTRA - 4 :], "tok")
    grad_vw = weight_grad(rows_first, dv)
    grad_qkw = weight_grad(rows_first, dq, dk)

    down_back = gather_back(down_near.astype(BF), order_one)
    up_back = gather_back(up_near.astype(BF), order_two)
    grad_down, grad_upw = down_back.astype(F32), up_back.astype(F32)
    waits = (outw_sum[-1], gw_sum[-1], down_back, up_back)
    vw_sum = scatter_sum(grad_vw, order_one, 0, waits)[-1].astype(BF)
    qkw_sum = scatter_sum(grad_qkw, order_two, 0, waits)[-1].astype(BF)
    grad_outw = gather_back(outw_sum[-1].astype(BF), order_one).astype(F32)
    grad_gw = gather_back(gw_sum[-1].astype(BF), order_two).astype(F32)
    pieces = after(jnp.stack([vw_sum, qkw_sum]), grad_outw, grad_gw, grad_down, grad_upw)
    pieces = lax.all_gather(pieces, "tok", axis=0)
    grad_vw = in_order(pieces[:, 0], order_one)
    grad_qkw = in_order(pieces[:, 1], order_two)
    grad_qw, grad_kw = grad_qkw[:, :inner_width], grad_qkw[:, inner_width:]

    late_down_part = after(down_part, last_sum)
    result = (hidden + scatter_side(late_down_part)).astype(BF)
    result_keep = lax.dynamic_index_in_dim(result, spread, 0, keepdims=False)
    result_give = lax.dynamic_index_in_dim(result, 1 - spread, 0, keepdims=False)
    layer_out = joined(result_keep, swapped(result_give, "head", sides), spread == 0, 0)

    norm_first = (tokens.astype(F32) - stats[:, 0:1]) * stats[:, 1:2]
    branch_rows = lax.dynamic_index_in_dim(
        lax.dynamic_index_in_dim(grad_branch, side, 1, keepdims=False), spread, 1, keepdims=False
    ).reshape(row_count, width)
    tokens_grad = branch_rows.astype(F32) + stats[:, 1:2] * (
        grad_ln1 * mix_gain - sums_first[:, 0:1] - norm_first * sums_first[:, 1:2]
    )
    return (
        layer_out,
        tokens_grad,
        columns[0],
        columns[1],
        grad_qw,
        grad_kw,
        grad_vw,
        grad_gw,
        grad_outw,
        columns[2],
        columns[3],
        grad_upw,
        grad_down,
    )


def solution(mesh):
    rows = P("tok", "head")
    columns = P(None, "head")
    return jax.shard_map(
        body,
        mesh=mesh,
        in_specs=(
            rows,
            P("head"),
            P("head"),
            columns,
            columns,
            columns,
            columns,
            P("head", None),
            P("head"),
            P("head"),
            columns,
            P("head", None),
            P("tok"),
            P("tok"),
            rows,
        ),
        out_specs=(
            rows,
            rows,
            P("head"),
            P("head"),
            columns,
            columns,
            columns,
            columns,
            P("head", None),
            P("head"),
            P("head"),
            columns,
            P("head", None),
        ),
        check_vma=False,
    )
```

```python
from functools import partial

import jax
import jax.numpy as jnp
from jax import lax
from jax.experimental import pallas as pl
from jax.experimental.pallas import tpu as pltpu
from jax.sharding import PartitionSpec as P

KD = 256
VD = 512
EPSILON = 1e-05
BF = jnp.bfloat16
F32 = jnp.float32


def after(value, *others):
    return lax.optimization_barrier((value, *others))[0]


def shifted(value, by):
    length = lax.axis_size("tok")
    pairs = [(i, i + by) for i in range(length) if 0 <= i + by < length]
    return lax.ppermute(value, "tok", pairs)


def swapped(value, axis, mask):
    return lax.ppermute(value, axis, [(i, i ^ mask) for i in range(lax.axis_size(axis))])


def my_bit(axis, bit):
    return (lax.axis_index(axis) >> bit) & 1


def joined(value, other, first, axis):
    return jnp.where(
        first,
        jnp.concatenate([value, other], axis=axis),
        jnp.concatenate([other, value], axis=axis),
    )


def bit_orders():
    bits = lax.axis_size("tok").bit_length() - 1
    first = list(range(bits))
    second = [0, 2, 1] if bits == 3 else first[bits // 2 :] + first[: bits // 2]
    return first, second


def halves(value, axis, bit, dim):
    shape = value.shape
    pieces = value.reshape(*shape[:dim], 2, shape[dim] // 2, *shape[dim + 1 :])
    mine = my_bit(axis, bit)
    keep = lax.dynamic_index_in_dim(pieces, mine, dim, keepdims=False)
    give = lax.dynamic_index_in_dim(pieces, 1 - mine, dim, keepdims=False)
    return keep, give


def own_piece(value, order, dim=0):
    for bit in order:
        value = halves(value, "tok", bit, dim)[0]
    return value


def gather_back(value, order):
    for bit in order[::-1]:
        other = swapped(value, "tok", 1 << bit)
        value = joined(value, other, my_bit("tok", bit) == 0, 0)
    return value


def far_swap(*values):
    return [swapped(value, "head", lax.axis_size("head") // 2) for value in values]


def side_bits():
    return range(lax.axis_size("head").bit_length() - 2)


def gather_side(value):
    for bit in side_bits():
        other = swapped(value, "head", 1 << bit)
        value = joined(value, other, my_bit("head", bit) == 0, 1)
    return value


def scatter_side_start(value):
    for bit in list(side_bits())[:0:-1]:
        keep, give = halves(value, "head", bit, 1)
        value = keep.astype(F32) + swapped(give.astype(BF), "head", 1 << bit).astype(F32)
    give = halves(value, "head", 0, 1)[1]
    return value, swapped(give.astype(BF), "head", 1)


def scatter_side(value):
    for bit in list(side_bits())[::-1]:
        keep, give = halves(value, "head", bit, 1)
        value = keep.astype(F32) + swapped(give.astype(BF), "head", 1 << bit).astype(F32)
    return value[:, 0]


def sum_side(value):
    for bit in side_bits():
        value = value + swapped(value, "head", 1 << bit)
    return value


TILE = 256
EXTRA = 16
CHUNK = 512
VMEM_LIMIT = 58 << 20


def dot(left, right):
    return jnp.dot(left, right, preferred_element_type=F32)


def dot_nt(left, right):
    return lax.dot_general(left, right, (((1,), (1,)), ((), ())), preferred_element_type=F32)


def dot_tn(left, right):
    return lax.dot_general(left, right, (((0,), (0,)), ((), ())), preferred_element_type=F32)


def tiles(columns):
    return pl.BlockSpec((TILE, columns), lambda i: (i, 0))


def whole(*shape):
    zeros = (0,) * len(shape)
    return pl.BlockSpec(shape, lambda i: zeros, pipeline_mode=pl.Buffered(1))


def held(*shape):
    zeros = (0,) * len(shape)
    return pl.BlockSpec(shape, lambda i: zeros)


SCALARS = pl.BlockSpec(memory_space=pltpu.SMEM)


def call(kernel, rows, in_specs, outs, out_specs, scratch=(), flops=0):
    return pl.pallas_call(
        kernel,
        grid=(rows // TILE,),
        in_specs=in_specs,
        out_specs=out_specs,
        out_shape=[jax.ShapeDtypeStruct(shape, dtype) for shape, dtype in outs],
        scratch_shapes=list(scratch),
        cost_estimate=pl.CostEstimate(flops=flops, bytes_accessed=0, transcendentals=0),
        compiler_params=pltpu.CompilerParams(vmem_limit_bytes=VMEM_LIMIT),
    )


def turned(value, cosine, sine):
    half_dim = KD // 2
    front, back = value[:, :half_dim], value[:, half_dim:]
    return jnp.concatenate([front * cosine - back * sine, back * cosine + front * sine], axis=1)


def tile_decay(log_decay, behind, docs_col, docs_row, pads_row):
    rows = lax.broadcasted_iota(jnp.int32, (TILE, 1), 0)
    cols = lax.broadcasted_iota(jnp.int32, (1, TILE), 1)
    allowed = (docs_col == docs_row) & (rows + behind >= cols) & (pads_row > 0)
    rise = jnp.exp(rows.astype(F32) * log_decay)
    fall = jnp.exp((behind - cols).astype(F32) * log_decay)
    return jnp.where(allowed, rise * fall, 0.0)


def send_state(docs, acc, sum_out):
    sum_out[:, :KD, :] = acc[...].astype(BF)
    sum_out[:, KD:, :] = jnp.full((acc.shape[0], EXTRA, VD), docs[0].astype(F32), F32).astype(BF)


def lanes(shards):
    return jnp.concatenate([shards[i] for i in range(shards.shape[0])], axis=1)


def vector_of(rows, index):
    return rows[3 * index : 3 * index + 1] + rows[3 * index + 1 : 3 * index + 2] + rows[
        3 * index + 2 : 3 * index + 3
    ]


def entry_kernel(x, one, two, three, four, out):
    rows = x.shape[0]
    out[:rows] = x[...]
    pieces = []
    for vector in (one, two, three, four):
        value = vector[...]
        for _ in range(3):
            piece = value.astype(BF)
            pieces.append(piece.astype(F32))
            value = value - piece.astype(F32)
    pieces.append(jnp.zeros((EXTRA - len(pieces), x.shape[1]), F32))
    out[rows:] = jnp.concatenate(pieces, axis=0).astype(BF)


def project_kernel(
    heads, docs, x, vec, wq, wk, wv, cos, sin, end, ln_out, q_out, k_out, v_out, stat_out,
    sum_out, acc
):
    step = pl.program_id(0)
    rows = lanes(x).astype(F32)
    vectors = lanes(vec).astype(F32)
    mean = jnp.mean(rows, axis=1, keepdims=True)
    scale = lax.rsqrt(jnp.mean(rows * rows, axis=1, keepdims=True) - mean * mean + EPSILON)
    low = ((rows - mean) * scale * vector_of(vectors, 0) + vector_of(vectors, 1)).astype(BF)
    ln_out[...] = low
    stat_out[...] = jnp.concatenate([mean, scale], axis=1)
    values = dot(low, wv[...]).astype(BF)
    v_out[...] = values
    queries = dot(low, wq[...])
    keys = dot(low, wk[...])
    cosine, sine = cos[...], sin[...]

    @pl.when(step == 0)
    def _():
        acc[...] = jnp.zeros_like(acc)

    for h in range(heads):
        mine = slice(h * KD, (h + 1) * KD)
        q_out[:, mine] = turned(queries[:, mine], cosine, sine).astype(BF)
        key = (turned(keys[:, mine], cosine, sine) * KD ** (-0.5)).astype(BF)
        k_out[:, mine] = key
        key_end = (key.astype(F32) * end[:, h : h + 1]).astype(BF)
        acc[h] += dot_tn(key_end, values[:, h * VD : (h + 1) * VD])

    @pl.when(step == pl.num_programs(0) - 1)
    def _():
        send_state(docs, acc, sum_out)


def inner_kernel(heads, decay, low, wg, q, k, v, dcol, drow, prow, gate_out, inner_out):
    step = pl.program_id(0)
    gate_out[...] = dot(low[...], wg[...])
    docs_col = dcol[...]

    def turn(j, totals):
        at = pl.ds(pl.multiple_of(j * TILE, TILE), TILE)
        sums = []
        for h in range(heads):
            mine = slice(h * KD, (h + 1) * KD)
            wide = slice(h * VD, (h + 1) * VD)
            factor = tile_decay(decay[h], (step - j) * TILE, docs_col, drow[:, at], prow[:, at])
            weights = (dot_nt(q[:, mine], k[at, mine]) * factor).astype(BF)
            sums.append(totals[h] + dot(weights, v[at, wide]))
        return tuple(sums)

    zeros = tuple(jnp.zeros((TILE, VD), F32) for _ in range(heads))
    totals = lax.fori_loop(0, step + 1, turn, zeros)
    for h in range(heads):
        inner_out[:, h * VD : (h + 1) * VD] = totals[h]


def joined_state(decay, rows, one, two, three, link_two, link_three):
    states = []
    for h in range(one.shape[0]):
        far = jnp.exp(jnp.full((1, 1), rows, F32) * decay[h])
        states.append(
            (
                one[h, :KD].astype(F32)
                + two[h, :KD].astype(F32) * (link_two * far)
                + three[h, :KD].astype(F32) * (link_three * far * far)
            ).astype(BF)
        )
    return states


def doc_in(payload):
    return payload[0, KD : KD + 1, 0:1].astype(F32)


def mix_kernel(
    heads, rows, decay, inner, q, one, two, three, gate, dcol, pcol, wo, group_out, scale_out,
    gated_out, part_out, state_out, carry_out
):
    step = pl.program_id(0)
    before = doc_in(one)

    @pl.when(step == 0)
    def _():
        link_two = (doc_in(two) == before).astype(F32)
        link_three = (doc_in(three) == before).astype(F32)
        states = joined_state(decay, rows, one, two, three, link_two, link_three)
        for h in range(heads):
            state_out[h] = states[h]

    same = (dcol[...].astype(F32) == before).astype(F32)
    place = (step * TILE + 1 + lax.broadcasted_iota(jnp.int32, (TILE, 1), 0)).astype(F32)
    for h in range(heads):
        mine = slice(h * KD, (h + 1) * KD)
        wide = slice(h * VD, (h + 1) * VD)
        carry = same * jnp.exp(place * decay[h])
        carry_out[:, h : h + 1] = carry
        carried = (q[:, mine].astype(F32) * carry).astype(BF)
        mixed = inner[:, wide] + dot(carried, state_out[h])
        mean = jnp.mean(mixed, axis=1, keepdims=True)
        scale = lax.rsqrt(jnp.mean(mixed * mixed, axis=1, keepdims=True) - mean * mean + 1.0)
        grouped = (mixed - mean) * scale
        group_out[:, wide] = grouped
        scale_out[:, h : h + 1] = scale
        gate_h = gate[:, wide]
        gated_out[:, wide] = (pcol[...] * gate_h * jax.nn.sigmoid(gate_h) * grouped).astype(BF)
    part = dot(gated_out[...], wo[...]).astype(BF)
    sides, width = part_out.shape[1], part_out.shape[4]
    for side in range(sides):
        for f in range(2):
            first = (f * sides + side) * width
            part_out[0, side, f] = part[:, first : first + width]


def gate_kernel(heads, grad, wo, gate, group, scale, pcol, dgate_out, mix_out):
    sides = grad.shape[1]
    rows = jnp.concatenate(
        [grad[0, side, f] for f in range(2) for side in range(sides)], axis=1
    )
    passed = dot_nt(rows, wo[...]) * pcol[...]
    for h in range(heads):
        wide = slice(h * VD, (h + 1) * VD)
        gate_h, grouped = gate[:, wide], group[:, wide]
        squash = jax.nn.sigmoid(gate_h)
        upstream = passed[:, wide]
        dgate_out[:, wide] = (
            upstream * grouped * (squash + gate_h * squash * (1.0 - squash))
        ).astype(BF)
        grad_group = upstream * gate_h * squash
        mean = jnp.mean(grad_group, axis=1, keepdims=True)
        cross = jnp.mean(grad_group * grouped, axis=1, keepdims=True)
        mix_out[:, wide] = (scale[:, h : h + 1] * (grad_group - mean - grouped * cross)).astype(BF)


def back_kernel(
    heads, docs, decay, mix, q, k, v, carry, state, dcol, drow, prow, cos, sin, dq_out, dk_out,
    dv_out, sum_out, acc
):
    step = pl.program_id(0)

    @pl.when(step == 0)
    def _():
        acc[...] = jnp.zeros_like(acc)
        dk_out[...] = jnp.zeros_like(dk_out)
        dv_out[...] = jnp.zeros_like(dv_out)

    docs_col = dcol[...]

    def turn(j, totals):
        at = pl.ds(pl.multiple_of(j * TILE, TILE), TILE)
        sums = []
        for h in range(heads):
            mine = slice(h * KD, (h + 1) * KD)
            wide = slice(h * VD, (h + 1) * VD)
            query, grad_mixed, key = q[:, mine], mix[:, wide], k[at, mine]
            factor = tile_decay(decay[h], (step - j) * TILE, docs_col, drow[:, at], prow[:, at])
            weights = (dot_nt(query, key) * factor).astype(BF)
            grads = (dot_nt(grad_mixed, v[at, wide]) * factor).astype(BF)
            dk_out[at, mine] += dot_tn(grads, query)
            dv_out[at, wide] += dot_tn(weights, grad_mixed)
            sums.append(totals[h] + dot(grads, key))
        return tuple(sums)

    zeros = tuple(jnp.zeros((TILE, KD), F32) for _ in range(heads))
    totals = lax.fori_loop(0, step + 1, turn, zeros)
    for h in range(heads):
        mine = slice(h * KD, (h + 1) * KD)
        wide = slice(h * VD, (h + 1) * VD)
        lift = carry[:, h : h + 1]
        total = totals[h] + lift * dot_nt(mix[:, wide], state[h])
        dq_out[:, mine] = turned(total, cos[...], -sin[...]).astype(BF)
        acc[h] += dot_tn((q[:, mine].astype(F32) * lift).astype(BF), mix[:, wide])

    @pl.when(step == pl.num_programs(0) - 1)
    def _():
        send_state(docs, acc, sum_out)


def finish_kernel(
    heads, size, docs, decay, dk_in, dv_in, k, v, end, one, two, three, dq, dgate, wq, wk, wv, wg,
    cos, sin, x, stat, vec, dk_out, dv_out, part_out, rows_out, cols_out, state
):
    step = pl.program_id(0)

    @pl.when(step == 0)
    def _():
        last = docs[0].astype(F32)
        link_two = (doc_in(one) == last).astype(F32)
        link_three = (doc_in(two) == last).astype(F32)
        states = joined_state(decay, size, one, two, three, link_two, link_three)
        for h in range(heads):
            state[h] = states[h]

    cosine, sine = cos[...], -sin[...]
    for h in range(heads):
        mine = slice(h * KD, (h + 1) * KD)
        wide = slice(h * VD, (h + 1) * VD)
        lift = end[:, h : h + 1]
        grad_key = dk_in[:, mine] + lift * dot_nt(v[:, wide], state[h])
        dk_out[:, mine] = (turned(grad_key, cosine, sine) * KD ** (-0.5)).astype(BF)
        key_end = (k[:, mine].astype(F32) * lift).astype(BF)
        dv_out[:, wide] = (dv_in[:, wide] + dot(key_end, state[h])).astype(BF)
    part = (
        dot_nt(dq[...], wq[...])
        + dot_nt(dk_out[...], wk[...])
        + dot_nt(dv_out[...], wv[...])
        + dot_nt(dgate[...], wg[...])
    )
    count, width = part_out.shape[0], part_out.shape[2]
    for shard in range(count):
        part_out[shard] = part[:, shard * width : (shard + 1) * width].astype(BF)
    normed = (lanes(x).astype(F32) - stat[:, 0:1]) * stat[:, 1:2]
    scaled = part * vec[0:1, :]
    ones = jnp.ones((8, scaled.shape[1]), BF)
    rows_out[0, 0:8] = dot_nt(ones, scaled.astype(BF))
    rows_out[0, 8:16] = dot_nt(ones, (scaled * normed).astype(BF))
    sums = jnp.concatenate(
        [jnp.sum(part * normed, axis=0, keepdims=True), jnp.sum(part, axis=0, keepdims=True)],
        axis=0,
    )

    @pl.when(step == 0)
    def _():
        cols_out[...] = jnp.zeros_like(cols_out)

    cols_out[...] += sums


def feed_kernel(
    chunks, x, grads, vec, up_near, up_far, down_near, down_far, ln_out, grad_out, act_out,
    dup_out, part_out, stat_out, rows_out, cols_out, acc
):
    step = pl.program_id(0)
    count = x.shape[1]
    steps = count // TILE

    def at_rows(r):
        return pl.ds(pl.multiple_of(r * TILE, TILE), TILE)

    @pl.when(step == 0)
    def _():
        def start(r, carry):
            at = at_rows(r)
            rows = jnp.concatenate([x[i, at, :] for i in range(x.shape[0])], axis=1).astype(F32)
            mean = jnp.mean(rows, axis=1, keepdims=True)
            scale = lax.rsqrt(jnp.mean(rows * rows, axis=1, keepdims=True) - mean * mean + EPSILON)
            stat_out[at, :] = jnp.concatenate([mean, scale], axis=1)
            ln_out[at, :] = ((rows - mean) * scale * vec[2:3, :] + vec[3:4, :]).astype(BF)
            grad_out[at, :] = jnp.concatenate(
                [grads[i, at, :] for i in range(grads.shape[0])], axis=1
            )
            acc[at, :] = jnp.zeros((TILE, acc.shape[1]), F32)
            return carry

        lax.fori_loop(0, steps, start, 0)

    def units(up, down):
        def turn(r, carry):
            at = at_rows(r)
            lifted = dot(ln_out[at, :], up[...])
            share = 0.5 * (1.0 + lax.erf(lifted * 0.5**0.5))
            act_out[at, :] = (lifted * share).astype(BF)
            slope = share + lifted * jnp.exp(-0.5 * lifted * lifted) * 0.3989422804014327
            lowered = (slope * dot_nt(grad_out[at, :], down[...])).astype(BF)
            dup_out[at, :] = lowered
            acc[at, :] += dot_nt(lowered, up[...])
            return carry

        lax.fori_loop(0, steps, turn, 0)

    @pl.when(step < chunks)
    def _():
        units(up_near, down_near)

    @pl.when(step >= chunks)
    def _():
        units(up_far, down_far)

    @pl.when(step == pl.num_programs(0) - 1)
    def _():
        cols_out[...] = jnp.zeros_like(cols_out)
        sides, width = part_out.shape[1], part_out.shape[3]

        def finish(r, carry):
            at = at_rows(r)
            part = acc[at, :]
            for f in range(2):
                for side in range(sides):
                    first = (f * sides + side) * width
                    part_out[f, side, at, :] = part[:, first : first + width].astype(BF)
            rows = jnp.concatenate([x[i, at, :] for i in range(x.shape[0])], axis=1).astype(F32)
            normed = (rows - stat_out[at, 0:1]) * stat_out[at, 1:2]
            scaled = part * vec[2:3, :]
            rows_out[at, :] = jnp.concatenate(
                [
                    jnp.sum(scaled, axis=1, keepdims=True),
                    jnp.sum(scaled * normed, axis=1, keepdims=True),
                ],
                axis=1,
            )
            cols_out[...] += jnp.concatenate(
                [
                    jnp.sum(part * normed, axis=0, keepdims=True),
                    jnp.sum(part, axis=0, keepdims=True),
                ],
                axis=0,
            )
            return carry

        lax.fori_loop(0, steps, finish, 0)


def branch_kernel(full, mine, keep, other, hidden, grads, gain, stat, near, far, out):
    total_rows = (near[...] + far[...]) * (1.0 / full)
    upstream = keep[0, 0].astype(F32) + other[0, 0].astype(F32)
    scale = stat[:, 1:2]
    normed = (hidden[0] - stat[:, 0:1]) * scale
    out[0] = (
        grads[0].astype(F32)
        + scale
        * (upstream * gain[0] - total_rows[:, 0:1] - normed * total_rows[:, 1:2])
    ).astype(BF)


def lower_kernel(act, down_near, down_far, out):
    units = down_near.shape[0]
    part = (dot(act[:, :units], down_near[...]) + dot(act[:, units:], down_far[...])).astype(BF)
    sides, width = out.shape[1], out.shape[3]
    for f in range(2):
        for side in range(sides):
            first = (f * sides + side) * width
            out[f, side] = part[:, first : first + width]


def prefetched(kernel, grid, in_specs, out_specs, outs):
    return pl.pallas_call(
        kernel,
        grid_spec=pltpu.PrefetchScalarGridSpec(
            num_scalar_prefetch=1, grid=grid, in_specs=in_specs, out_specs=out_specs
        ),
        out_shape=[jax.ShapeDtypeStruct(shape, dtype) for shape, dtype in outs],
        cost_estimate=pl.CostEstimate(flops=0, bytes_accessed=0, transcendentals=0),
        compiler_params=pltpu.CompilerParams(vmem_limit_bytes=VMEM_LIMIT),
    )


def bit_value(bit):
    return my_bit("tok", bit)[None].astype(jnp.int32)


def split_source(groups, rows, block):
    per_half = rows // (2 * block)
    count = groups * per_half

    def source(i, mine):
        keeps = (i >= count).astype(jnp.int32)
        half = jnp.where(keeps == 1, mine[0], 1 - mine[0])
        j = i - keeps * count
        return (j // per_half) * (2 * per_half) + half * per_half + j % per_half

    give = lambda i, mine: (jnp.minimum(i, count - 1), 0)
    keep = lambda i, mine: (jnp.maximum(i - count, 0), 0)
    return count, source, give, keep


def weight_kernel(count, mine, left, *refs):
    give, keep = refs[-2:]

    def fill(out):
        first = 0
        for right in refs[:-2]:
            width = right.shape[1]
            out[:, first : first + width] = dot_tn(left[...], right[...]).astype(BF)
            first += width

    @pl.when(pl.program_id(0) < count)
    def _():
        fill(give)

    @pl.when(pl.program_id(0) >= count)
    def _():
        fill(keep)


def weight_grad(bit, groups, left, *rights):
    rows, columns = left.shape
    width = sum(right.shape[1] for right in rights)
    block = min(CHUNK, columns // groups // 2)
    count, source, give, keep = split_source(groups, columns // groups, block)
    half = (columns // 2, width)
    return prefetched(
        partial(weight_kernel, count),
        (2 * count,),
        [pl.BlockSpec((rows, block), lambda i, mine: (0, source(i, mine)))]
        + [
            pl.BlockSpec(right.shape, lambda i, mine: (0, 0), pipeline_mode=pl.Buffered(1))
            for right in rights
        ],
        [pl.BlockSpec((block, width), give), pl.BlockSpec((block, width), keep)],
        [(half, BF), (half, BF)],
    )(bit_value(bit), left, *rights)


def turned_place(i, order):
    place = 0
    for k, bit in enumerate(order):
        place = place + (((i >> (len(order) - 1 - k)) & 1) << bit)
    return place


def outer_kernel(mine, gated, grad, give, keep):
    part = dot_tn(gated[...], jnp.concatenate([grad[0, 0, 0], grad[1, 0, 0]], axis=0)).astype(BF)
    half = give.shape[0]

    @pl.when(mine[0] == 0)
    def _():
        keep[...] = part[:half]
        give[...] = part[half:]

    @pl.when(mine[0] == 1)
    def _():
        keep[...] = part[half:]
        give[...] = part[:half]


def fold_kernel(count, mine, one, two, give, keep):
    total = (one[...].astype(F32) + two[...].astype(F32)).astype(BF)

    @pl.when(pl.program_id(0) < count)
    def _():
        give[...] = total

    @pl.when(pl.program_id(0) >= count)
    def _():
        keep[...] = total


def fold(bit, groups, one, two):
    rows, columns = one.shape
    block = min(CHUNK // 2, rows // groups // 2)
    count, source, give, keep = split_source(groups, rows // groups, block)
    spec = pl.BlockSpec((block, columns), lambda i, mine: (source(i, mine), 0))
    half = (rows // 2, columns)
    return prefetched(
        partial(fold_kernel, count),
        (2 * count,),
        [spec, spec],
        [pl.BlockSpec((block, columns), give), pl.BlockSpec((block, columns), keep)],
        [(half, BF), (half, BF)],
    )(bit_value(bit), one, two)


def scatter_rest(give, keep, order, groups=1, waits=None):
    values, others = [], []
    for place, bit in enumerate(order):
        if waits and place in waits:
            give = after(give, *waits[place])
        other = swapped(give, "tok", 1 << bit)
        others.append(other)
        if place + 1 < len(order):
            give, keep = fold(order[place + 1], groups, keep, other)
            values.append(give)
        else:
            values.append((keep, other))
    return values, others


def total(pair):
    return pair[0].astype(F32) + pair[1].astype(F32)


def spread_kernel(per_half, mine, near, other, out):
    here = pl.program_id(0) // per_half == mine[0]

    @pl.when(here)
    def _():
        out[...] = near[...].astype(out.dtype)

    @pl.when(jnp.logical_not(here))
    def _():
        out[...] = other[...].astype(out.dtype)


def gather_one(value, bit):
    return joined(value, swapped(value, "tok", 1 << bit), my_bit("tok", bit) == 0, 0)


def gather_wide(value, order):
    for bit in order[:0:-1]:
        value = gather_one(value, bit)
    bit = order[0]
    other = swapped(value, "tok", 1 << bit)
    rows, columns = value.shape
    block = min(CHUNK // 2, rows)
    per_half = rows // block

    def spec(mirror):
        def index(i, mine):
            half = 1 - mine[0] if mirror else mine[0]
            return (jnp.clip(i - half * per_half, 0, per_half - 1), 0)

        return pl.BlockSpec((block, columns), index)

    return prefetched(
        partial(spread_kernel, per_half),
        (2 * per_half,),
        [spec(False), spec(True)],
        [pl.BlockSpec((block, columns), lambda i, mine: (i, 0))],
        [((2 * rows, columns), F32)],
    )(bit_value(bit), value, other)[0], value


def order_kernel(split, first, second, one_out, two_out, *rest):
    rows, columns = one_out.shape[0], first.shape[2]
    for i in range(first.shape[1] // rows):
        at = slice(i * columns, (i + 1) * columns)
        one_out[:, at] = first[0, i * rows : (i + 1) * rows].astype(F32)
    if rest:
        two_out[...] = second[0, :, :split].astype(F32)
        rest[0][...] = second[0, :, split:].astype(F32)
    else:
        two_out[...] = second[0].astype(F32)


def packed_pieces(first, second):
    columns = second.shape[1]
    parts = [first[:, i : i + columns] for i in range(0, first.shape[1], columns)]
    return jnp.concatenate([*parts, second], axis=0)


def in_order(pieces, first, order_one, order_two, split=None):
    count, rows, columns = pieces.shape
    half = rows // 2

    def spec(order, which):
        return pl.BlockSpec(
            (1, half, columns), lambda i: (turned_place(i, order), which, 0)
        )

    shapes = [first]
    if split:
        shapes += [(half, split), (half, columns - split)]
    else:
        shapes += [(half, columns)]
    return pl.pallas_call(
        partial(order_kernel, split),
        grid=(count,),
        in_specs=[spec(order_one, 0), spec(order_two, 1)],
        out_specs=[pl.BlockSpec(shape, lambda i: (i, 0)) for shape in shapes],
        out_shape=[jax.ShapeDtypeStruct((count * high, wide), F32) for high, wide in shapes],
        cost_estimate=pl.CostEstimate(flops=0, bytes_accessed=0, transcendentals=0),
        compiler_params=pltpu.CompilerParams(vmem_limit_bytes=VMEM_LIMIT),
    )(pieces, pieces)


def body(
    tokens,
    mix_gain,
    mix_bias,
    query_weight,
    key_weight,
    value_weight,
    gate_weight,
    output_weight,
    feed_gain,
    feed_bias,
    up_weight,
    down_weight,
    doc_ids,
    pad_mask,
    out_grad,
):
    row_count, width = tokens.shape
    heads_here = query_weight.shape[1] // KD
    shards = lax.axis_size("head")
    full_width = width * shards
    sides = shards // 2
    spread = lax.axis_index("head") // sides
    side = lax.axis_index("head") % sides
    half_rows = row_count // 2
    block = lax.axis_index("tok")

    packed = pl.pallas_call(
        entry_kernel,
        out_shape=jax.ShapeDtypeStruct((row_count + EXTRA, width), BF),
        compiler_params=pltpu.CompilerParams(vmem_limit_bytes=VMEM_LIMIT),
    )(tokens, mix_gain[None], mix_bias[None], feed_gain[None], feed_bias[None])
    rows_raw = lax.all_gather(packed, "head", axis=0)
    vector_rows = rows_raw[:, row_count:, :].astype(F32)
    vectors = (vector_rows[:, 0:12:3] + vector_rows[:, 1:12:3] + vector_rows[:, 2:12:3]).transpose(
        1, 0, 2
    )
    side_vectors = lax.dynamic_index_in_dim(
        vectors.reshape(4, 2, sides, width), side, 2, keepdims=False
    )
    vectors = vectors.reshape(4, full_width)

    order_one, order_two = bit_orders()
    late_grad = after(out_grad, rows_raw)
    grad_keep, grad_give = halves(late_grad, "head", shards.bit_length() - 2, 0)
    grad_seen = swapped(grad_give, "head", sides)
    up_piece, down_piece = own_piece(up_weight, order_one), own_piece(down_weight, order_two)
    both_pieces = jnp.concatenate([up_piece, down_piece.reshape(up_piece.shape)], axis=0)

    first_head = lax.axis_index("head") * heads_here
    log_decay = jnp.log(
        1.0 - 2.0 ** (-5.0 - (first_head + jnp.arange(heads_here, dtype=jnp.int32)).astype(F32))
    )
    position = jnp.arange(row_count, dtype=jnp.int32)
    frequency = 10000.0 ** (-2.0 * jnp.arange(KD // 2, dtype=jnp.int32).astype(F32) / KD)
    angles = (block * row_count + position).astype(F32)[:, None] * frequency[None, :]
    cosine, sine = jnp.cos(angles), jnp.sin(angles)
    padding = pad_mask.astype(F32)
    last_doc = doc_ids[row_count - 1]

    end_factor = (padding * (doc_ids == last_doc).astype(F32))[:, None] * jnp.exp(
        (row_count - 1 - position).astype(F32)[:, None] * log_decay[None, :]
    )

    docs_col, docs_row = doc_ids[:, None], doc_ids[None, :]
    pads_col, pads_row = padding[:, None], padding[None, :]
    inner_width, value_width = heads_here * KD, heads_here * VD
    states = pltpu.VMEM((heads_here, KD, VD), F32)
    state_shape = (heads_here, KD, VD)
    sent_shape = (heads_here, KD + EXTRA, VD)
    shard_tiles = pl.BlockSpec((shards, TILE, width), lambda i: (0, i, 0))
    per_half = half_rows // TILE
    split_tiles = pl.BlockSpec(
        (1, sides, 2, TILE, width), lambda i: (i // per_half, 0, 0, i % per_half, 0)
    )
    last_docs = doc_ids[row_count - 1 :]
    rows_first, query_rot, key_rot, values, stats, summary = call(
        partial(project_kernel, heads_here),
        row_count,
        [
            SCALARS,
            shard_tiles,
            pl.BlockSpec((shards, EXTRA, width), lambda i: (0, row_count // EXTRA, 0)),
            whole(full_width, inner_width),
            whole(full_width, inner_width),
            whole(full_width, value_width),
            tiles(KD // 2),
            tiles(KD // 2),
            tiles(heads_here),
        ],
        [
            ((row_count, full_width), BF),
            ((row_count, inner_width), BF),
            ((row_count, inner_width), BF),
            ((row_count, value_width), BF),
            ((row_count, 2), F32),
            (sent_shape, BF),
        ],
        [
            tiles(full_width),
            tiles(inner_width),
            tiles(inner_width),
            tiles(value_width),
            tiles(2),
            held(*sent_shape),
        ],
        [states],
    )(
        last_docs,
        rows_raw,
        rows_raw,
        query_weight,
        key_weight,
        value_weight,
        cosine,
        sine,
        end_factor,
    )
    one_back, two_back, three_back = (shifted(summary, by) for by in (1, 2, 3))
    grad_seen = after(grad_seen, summary)
    side_grads = joined(grad_keep[None], grad_seen[None], spread == 0, 0)
    grad_rows = gather_side(side_grads[:, None]).reshape(shards, half_rows, width)
    (both_seen,) = far_swap(after(both_pieces, grad_seen))
    up_seen = both_seen[: up_piece.shape[0]]
    down_seen = both_seen[up_piece.shape[0] :].reshape(down_piece.shape)
    up_other = gather_back(up_seen, order_one)
    down_other = gather_back(down_seen, order_two)
    gate_pre, inner_part = call(
        partial(inner_kernel, heads_here),
        row_count,
        [
            SCALARS,
            tiles(full_width),
            whole(full_width, value_width),
            tiles(inner_width),
            whole(row_count, inner_width),
            whole(row_count, value_width),
            tiles(1),
            whole(1, row_count),
            whole(1, row_count),
        ],
        [((row_count, value_width), F32)] * 2,
        [tiles(value_width)] * 2,
    )(
        after(log_decay, side_grads),
        rows_first,
        gate_weight,
        query_rot,
        key_rot,
        values,
        docs_col,
        docs_row,
        pads_row,
    )
    flat_group, group_scale, gated, mix_part, state_low, carry_factor = call(
        partial(mix_kernel, heads_here, row_count),
        row_count,
        [
            SCALARS,
            tiles(value_width),
            tiles(inner_width),
            whole(*sent_shape),
            whole(*sent_shape),
            whole(*sent_shape),
            tiles(value_width),
            tiles(1),
            tiles(1),
            whole(value_width, full_width),
        ],
        [
            ((row_count, value_width), F32),
            ((row_count, heads_here), F32),
            ((row_count, value_width), BF),
            ((2, sides, 2, half_rows, width), BF),
            (state_shape, BF),
            ((row_count, heads_here), F32),
        ],
        [
            tiles(value_width),
            tiles(heads_here),
            tiles(value_width),
            split_tiles,
            held(*state_shape),
            tiles(heads_here),
        ],
    )(
        log_decay,
        inner_part,
        query_rot,
        one_back,
        two_back,
        three_back,
        gate_pre,
        docs_col,
        pads_col,
        output_weight,
    )
    mix_part = after(mix_part, grad_rows, both_seen)
    side_tokens = lax.dynamic_index_in_dim(
        lax.dynamic_slice_in_dim(rows_raw, spread * half_rows, half_rows, axis=1).reshape(
            2, sides, half_rows, width
        ),
        side,
        1,
        keepdims=False,
    )
    mixed_sum = lax.psum_scatter(
        mix_part.reshape(shards, 2, half_rows, width), "head", scatter_dimension=0
    )
    hidden = lax.optimization_barrier(side_tokens.astype(F32) + mixed_sum.astype(F32))
    hidden_rows = gather_side(hidden.astype(BF)[:, None]).reshape(shards, half_rows, width)
    units = up_weight.shape[1]
    chunks = units // CHUNK
    rows_second, grad_plain, act_low, grad_up, feed_part, stats_second, row_second, cols_second = (
        pl.pallas_call(
            partial(feed_kernel, chunks),
            grid=(2 * chunks,),
            in_specs=[
                whole(shards, half_rows, width),
                whole(shards, half_rows, width),
                whole(4, full_width),
                pl.BlockSpec((full_width, CHUNK), lambda i: (0, jnp.minimum(i, chunks - 1))),
                pl.BlockSpec((full_width, CHUNK), lambda i: (0, jnp.maximum(i - chunks, 0))),
                pl.BlockSpec((CHUNK, full_width), lambda i: (jnp.minimum(i, chunks - 1), 0)),
                pl.BlockSpec((CHUNK, full_width), lambda i: (jnp.maximum(i - chunks, 0), 0)),
            ],
            out_specs=[
                held(half_rows, full_width),
                held(half_rows, full_width),
                pl.BlockSpec((half_rows, CHUNK), lambda i: (0, i)),
                pl.BlockSpec((half_rows, CHUNK), lambda i: (0, i)),
                held(2, sides, half_rows, width),
                held(half_rows, 2),
                held(half_rows, 2),
                held(2, full_width),
            ],
            out_shape=[
                jax.ShapeDtypeStruct((half_rows, full_width), BF),
                jax.ShapeDtypeStruct((half_rows, full_width), BF),
                jax.ShapeDtypeStruct((half_rows, 2 * units), BF),
                jax.ShapeDtypeStruct((half_rows, 2 * units), BF),
                jax.ShapeDtypeStruct((2, sides, half_rows, width), BF),
                jax.ShapeDtypeStruct((half_rows, 2), F32),
                jax.ShapeDtypeStruct((half_rows, 2), F32),
                jax.ShapeDtypeStruct((2, full_width), F32),
            ],
            scratch_shapes=[pltpu.VMEM((half_rows, full_width), F32)],
            cost_estimate=pl.CostEstimate(flops=0, bytes_accessed=0, transcendentals=0),
            compiler_params=pltpu.CompilerParams(vmem_limit_bytes=VMEM_LIMIT),
        )(hidden_rows, grad_rows, vectors, up_weight, up_other, down_weight, down_other)
    )
    feed_value, feed_seen = scatter_side_start(feed_part)
    for bit in list(side_bits())[:0:-1]:
        row_second = row_second + swapped(row_second, "head", 1 << bit)
    row_seen = swapped(row_second, "head", 1)
    down_give, down_keep = weight_grad(order_one[0], 2, act_low, grad_plain)
    up_give, up_keep = weight_grad(order_two[0], 1, rows_second, grad_up)
    row_seen = after(row_seen, down_give, up_give)
    half_block = pl.BlockSpec((1, TILE, width), lambda f, i, mine: (f, i, 0))
    row_block = pl.BlockSpec((TILE, 2), lambda f, i, mine: (i, 0))
    (branch,) = prefetched(
        partial(branch_kernel, full_width),
        (2, half_rows // TILE),
        [
            pl.BlockSpec((1, 1, TILE, width), lambda f, i, mine: (f, mine[0], i, 0)),
            pl.BlockSpec((1, 1, TILE, width), lambda f, i, mine: (f, 0, i, 0)),
            half_block,
            half_block,
            pl.BlockSpec((1, 1, width), lambda f, i, mine: (f, 0, 0)),
            row_block,
            row_block,
            row_block,
        ],
        [half_block],
        [((2, half_rows, width), BF)],
    )(
        my_bit("head", 0)[None].astype(jnp.int32),
        feed_value,
        feed_seen[:, None] if feed_seen.ndim == 3 else feed_seen,
        hidden,
        side_grads,
        side_vectors[2][:, None, :],
        stats_second,
        row_second,
        row_seen,
    )
    grad_branch = lax.all_gather(branch, "head", axis=0).reshape(
        2, sides, 2, half_rows, width
    )

    down_part = pl.pallas_call(
        lower_kernel,
        grid=(half_rows // TILE,),
        in_specs=[tiles(2 * units), whole(units, full_width), whole(units, full_width)],
        out_specs=pl.BlockSpec((2, sides, TILE, width), lambda i: (0, 0, i, 0)),
        out_shape=jax.ShapeDtypeStruct((2, sides, half_rows, width), BF),
        cost_estimate=pl.CostEstimate(flops=0, bytes_accessed=0, transcendentals=0),
        compiler_params=pltpu.CompilerParams(vmem_limit_bytes=VMEM_LIMIT),
    )(after(act_low, branch), down_weight, down_other)

    down_sum, _ = scatter_rest(
        down_give, down_keep, order_one, 2, {0: (branch,), len(order_one) - 1: (down_part,)}
    )
    up_sum, _ = scatter_rest(up_give, up_keep, order_two, 1, {0: (branch,)})

    dgate, grad_mixed = call(
        partial(gate_kernel, heads_here),
        row_count,
        [
            split_tiles,
            whole(value_width, full_width),
            tiles(value_width),
            tiles(value_width),
            tiles(heads_here),
            tiles(1),
        ],
        [((row_count, value_width), BF), ((row_count, value_width), BF)],
        [tiles(value_width), tiles(value_width)],
    )(
        grad_branch,
        output_weight,
        gate_pre,
        flat_group,
        group_scale,
        pads_col,
    )
    half_down = down_sum[-1][0].shape[0] // 2
    up_pair = lax.optimization_barrier((*up_sum[-1], dgate))[:2]
    down_pair = lax.optimization_barrier((*down_sum[-1], dgate))[:2]
    up_give = total([part[:, units:] for part in up_pair]).astype(BF)
    down_give = total([part[half_down:] for part in down_pair]).astype(BF)
    up_far, down_far = far_swap(up_give, down_give)
    up_near = total([part[:, :units] for part in up_pair]) + up_far.astype(F32)
    down_near = total([part[:half_down] for part in down_pair]) + down_far.astype(F32)
    dq, dk_part, dv_part, grad_state = call(
        partial(back_kernel, heads_here),
        row_count,
        [
            SCALARS,
            SCALARS,
            tiles(value_width),
            tiles(inner_width),
            whole(row_count, inner_width),
            whole(row_count, value_width),
            tiles(heads_here),
            whole(*state_shape),
            tiles(1),
            whole(1, row_count),
            whole(1, row_count),
            tiles(KD // 2),
            tiles(KD // 2),
        ],
        [
            ((row_count, inner_width), BF),
            ((row_count, inner_width), F32),
            ((row_count, value_width), F32),
            (sent_shape, BF),
        ],
        [
            tiles(inner_width),
            held(row_count, inner_width),
            held(row_count, value_width),
            held(*sent_shape),
        ],
        [states],
        10 * row_count * full_width * value_width,
    )(
        last_docs,
        after(log_decay, down_part, up_give, down_give),
        grad_mixed,
        query_rot,
        key_rot,
        values,
        carry_factor,
        state_low,
        docs_col,
        docs_row,
        pads_row,
        cosine,
        sine,
    )
    width_out = (value_width // 2, full_width)
    outw_give, outw_keep = prefetched(
        outer_kernel,
        (shards,),
        [
            pl.BlockSpec(
                (row_count, value_width), lambda i, mine: (0, 0), pipeline_mode=pl.Buffered(1)
            ),
            pl.BlockSpec(
                (2, 1, 1, half_rows, width), lambda i, mine: (0, i % sides, i // sides, 0, 0)
            ),
        ],
        [pl.BlockSpec((value_width // 2, width), lambda i, mine: (0, i))] * 2,
        [(width_out, BF), (width_out, BF)],
    )(bit_value(order_one[0]), after(gated, dq), grad_branch)
    outw_sum, outw_seen = scatter_rest(outw_give, outw_keep, order_one)
    gw_give, gw_keep = weight_grad(order_two[0], 1, rows_first, after(dgate, dq))
    gw_sum, gw_seen = scatter_rest(gw_give, gw_keep, order_two)
    one_on, two_on, three_on = (shifted(grad_state, -by) for by in (1, 2, 3))
    dk, dv, last_part, row_sums, column_first = call(
        partial(finish_kernel, heads_here, row_count),
        row_count,
        [
            SCALARS,
            SCALARS,
            tiles(inner_width),
            tiles(value_width),
            tiles(inner_width),
            tiles(value_width),
            tiles(heads_here),
            whole(*sent_shape),
            whole(*sent_shape),
            whole(*sent_shape),
            tiles(inner_width),
            tiles(value_width),
            whole(full_width, inner_width),
            whole(full_width, inner_width),
            whole(full_width, value_width),
            whole(full_width, value_width),
            tiles(KD // 2),
            tiles(KD // 2),
            shard_tiles,
            tiles(2),
            whole(4, full_width),
        ],
        [
            ((row_count, inner_width), BF),
            ((row_count, value_width), BF),
            ((shards, row_count + EXTRA, width), BF),
            ((row_count // TILE, 16, TILE), F32),
            ((2, full_width), F32),
        ],
        [
            tiles(inner_width),
            tiles(value_width),
            shard_tiles,
            pl.BlockSpec((1, 16, TILE), lambda i: (i, 0, 0)),
            held(2, full_width),
        ],
        [pltpu.VMEM(state_shape, BF)],
        12 * row_count * full_width * value_width,
    )(
        last_docs,
        after(log_decay, outw_sum[0], gw_give),
        dk_part,
        dv_part,
        key_rot,
        values,
        end_factor,
        one_on,
        two_on,
        three_on,
        dq,
        dgate,
        query_weight,
        key_weight,
        value_weight,
        gate_weight,
        cosine,
        sine,
        rows_raw,
        stats,
        vectors,
    )
    count = row_count // TILE
    line = jnp.concatenate([row_sums[:, 0], row_sums[:, 8]], axis=0)
    line = jnp.pad(line, ((0, EXTRA - 2 * count - 4), (0, width - TILE)))
    columns = jnp.concatenate([column_first, cols_second]).reshape(4, shards, width)
    extra = jnp.concatenate(
        [jnp.broadcast_to(line[None], (shards, *line.shape)), columns.transpose(1, 0, 2)], axis=1
    )
    last_part = lax.dynamic_update_slice_in_dim(last_part, extra.astype(BF), row_count, axis=1)
    down_low, up_low = down_near.astype(BF), up_near.astype(BF)
    down_next = swapped(down_low, "tok", 1 << order_one[-1])
    up_next = swapped(up_low, "tok", 1 << order_two[-1])
    last_part = after(last_part, down_far, up_far, outw_seen[1], gw_seen[0])
    down_back = joined(down_low, down_next, my_bit("tok", order_one[-1]) == 0, 0)
    up_back = joined(up_low, up_next, my_bit("tok", order_two[-1]) == 0, 0)
    last_sum = lax.psum_scatter(last_part, "head", scatter_dimension=0).astype(F32)
    grad_ln1 = last_sum[:row_count]
    sums_first = last_sum[row_count:, :TILE] / full_width
    sums_first = jnp.stack(
        [sums_first[:count].reshape(row_count), sums_first[count : 2 * count].reshape(row_count)],
        axis=1,
    )
    columns = lax.psum(last_sum[row_count + EXTRA - 4 :], "tok")
    result = (hidden + scatter_side(after(down_part, last_sum))).astype(BF)
    result_keep = lax.dynamic_index_in_dim(result, spread, 0, keepdims=False)
    result_give = lax.dynamic_index_in_dim(result, 1 - spread, 0, keepdims=False)
    layer_out = joined(result_keep, swapped(result_give, "head", sides), spread == 0, 0)

    vw_give, vw_keep = weight_grad(order_one[0], 1, rows_first, dv)
    qkw_give, qkw_keep = weight_grad(order_two[0], 1, rows_first, dq, dk)
    grad_down, down_back = gather_wide(down_back, order_one[:-1])
    grad_upw, up_back = gather_wide(up_back, order_two[:-1])
    outw_low, gw_low = total(outw_sum[-1]).astype(BF), total(gw_sum[-1]).astype(BF)
    waits = {1: (gw_sum[0],), 2: (outw_sum[1], gw_sum[1])}
    vw_sum, _ = scatter_rest(vw_give, vw_keep, order_one, 1, waits)
    qkw_sum, _ = scatter_rest(qkw_give, qkw_keep, order_two, 1, waits)
    gates = (last_sum, vw_sum[0], qkw_sum[0], down_back, up_back)
    middle = lax.all_gather(after(packed_pieces(outw_low, gw_low), *gates), "tok", axis=0)
    grad_outw, grad_gw = in_order(middle, outw_low.shape, order_one, order_two)
    vw_low, qkw_low = total(vw_sum[-1]).astype(BF), total(qkw_sum[-1]).astype(BF)
    pieces = after(packed_pieces(vw_low, qkw_low), grad_down, grad_upw, middle, result)
    pieces = lax.all_gather(pieces, "tok", axis=0)
    grad_vw, grad_qw, grad_kw = in_order(
        pieces, vw_low.shape, order_one, order_two, inner_width
    )

    norm_first = (tokens.astype(F32) - stats[:, 0:1]) * stats[:, 1:2]
    branch_rows = lax.dynamic_index_in_dim(
        lax.dynamic_index_in_dim(grad_branch, side, 1, keepdims=False), spread, 1, keepdims=False
    ).reshape(row_count, width)
    tokens_grad = branch_rows.astype(F32) + stats[:, 1:2] * (
        grad_ln1 * mix_gain - sums_first[:, 0:1] - norm_first * sums_first[:, 1:2]
    )
    return (
        layer_out,
        tokens_grad,
        columns[0],
        columns[1],
        grad_qw,
        grad_kw,
        grad_vw,
        grad_gw,
        grad_outw,
        columns[2],
        columns[3],
        grad_upw,
        grad_down,
    )


def solution(mesh):
    rows = P("tok", "head")
    columns = P(None, "head")
    return jax.shard_map(
        body,
        mesh=mesh,
        in_specs=(
            rows,
            P("head"),
            P("head"),
            columns,
            columns,
            columns,
            columns,
            P("head", None),
            P("head"),
            P("head"),
            columns,
            P("head", None),
            P("tok"),
            P("tok"),
            rows,
        ),
        out_specs=(
            rows,
            rows,
            P("head"),
            P("head"),
            columns,
            columns,
            columns,
            columns,
            P("head", None),
            P("head"),
            P("head"),
            columns,
            P("head", None),
        ),
        check_vma=False,
    )
```

```python
from functools import partial

import jax
import jax.numpy as jnp
from jax import lax
from jax.experimental import pallas as pl
from jax.experimental.pallas import tpu as pltpu
from jax.sharding import PartitionSpec as P

KD = 256
VD = 512
EPSILON = 1e-05
BF = jnp.bfloat16
F32 = jnp.float32


def after(value, *others):
    return lax.optimization_barrier((value, *others))[0]


def shifted(value, by):
    length = lax.axis_size("tok")
    pairs = [(i, i + by) for i in range(length) if 0 <= i + by < length]
    return lax.ppermute(value, "tok", pairs)


def swapped(value, axis, mask):
    return lax.ppermute(value, axis, [(i, i ^ mask) for i in range(lax.axis_size(axis))])


def my_bit(axis, bit):
    return (lax.axis_index(axis) >> bit) & 1


def joined(value, other, first, axis):
    return jnp.where(
        first,
        jnp.concatenate([value, other], axis=axis),
        jnp.concatenate([other, value], axis=axis),
    )


def bit_orders():
    bits = lax.axis_size("tok").bit_length() - 1
    first = list(range(bits))
    second = [0, 2, 1] if bits == 3 else first[bits // 2 :] + first[: bits // 2]
    return first, second


def halves(value, axis, bit, dim):
    shape = value.shape
    pieces = value.reshape(*shape[:dim], 2, shape[dim] // 2, *shape[dim + 1 :])
    mine = my_bit(axis, bit)
    keep = lax.dynamic_index_in_dim(pieces, mine, dim, keepdims=False)
    give = lax.dynamic_index_in_dim(pieces, 1 - mine, dim, keepdims=False)
    return keep, give


def own_piece(value, order, dim=0):
    for bit in order:
        value = halves(value, "tok", bit, dim)[0]
    return value


def gather_back(value, order):
    for bit in order[::-1]:
        other = swapped(value, "tok", 1 << bit)
        value = joined(value, other, my_bit("tok", bit) == 0, 0)
    return value


def far_swap(*values):
    return [swapped(value, "head", lax.axis_size("head") // 2) for value in values]


def side_bits():
    return range(lax.axis_size("head").bit_length() - 2)


def gather_side(value):
    for bit in side_bits():
        other = swapped(value, "head", 1 << bit)
        value = joined(value, other, my_bit("head", bit) == 0, 1)
    return value, other


def scatter_side_start(value):
    for bit in list(side_bits())[:0:-1]:
        keep, give = halves(value, "head", bit, 1)
        value = keep.astype(F32) + swapped(give.astype(BF), "head", 1 << bit).astype(F32)
    give = halves(value, "head", 0, 1)[1]
    return value, swapped(give.astype(BF), "head", 1)


def scatter_side(value):
    for bit in list(side_bits())[::-1]:
        keep, give = halves(value, "head", bit, 1)
        value = keep.astype(F32) + swapped(give.astype(BF), "head", 1 << bit).astype(F32)
    return value[:, 0]


def sum_side(value):
    for bit in side_bits():
        value = value + swapped(value, "head", 1 << bit)
    return value


TILE = 256
EXTRA = 16
CHUNK = 512
VMEM_LIMIT = 58 << 20


def dot(left, right):
    return jnp.dot(left, right, preferred_element_type=F32)


def dot_nt(left, right):
    return lax.dot_general(left, right, (((1,), (1,)), ((), ())), preferred_element_type=F32)


def dot_tn(left, right):
    return lax.dot_general(left, right, (((0,), (0,)), ((), ())), preferred_element_type=F32)


def tiles(columns):
    return pl.BlockSpec((TILE, columns), lambda i: (i, 0))


def whole(*shape):
    zeros = (0,) * len(shape)
    return pl.BlockSpec(shape, lambda i: zeros, pipeline_mode=pl.Buffered(1))


def held(*shape):
    zeros = (0,) * len(shape)
    return pl.BlockSpec(shape, lambda i: zeros)


SCALARS = pl.BlockSpec(memory_space=pltpu.SMEM)


def call(kernel, rows, in_specs, outs, out_specs, scratch=(), flops=0):
    return pl.pallas_call(
        kernel,
        grid=(rows // TILE,),
        in_specs=in_specs,
        out_specs=out_specs,
        out_shape=[jax.ShapeDtypeStruct(shape, dtype) for shape, dtype in outs],
        scratch_shapes=list(scratch),
        cost_estimate=pl.CostEstimate(flops=flops, bytes_accessed=0, transcendentals=0),
        compiler_params=pltpu.CompilerParams(vmem_limit_bytes=VMEM_LIMIT),
    )


def turned(value, cosine, sine):
    half_dim = KD // 2
    front, back = value[:, :half_dim], value[:, half_dim:]
    return jnp.concatenate([front * cosine - back * sine, back * cosine + front * sine], axis=1)


def tile_decay(log_decay, behind, docs_col, docs_row, pads_row):
    rows = lax.broadcasted_iota(jnp.int32, (TILE, 1), 0)
    cols = lax.broadcasted_iota(jnp.int32, (1, TILE), 1)
    allowed = (docs_col == docs_row) & (rows + behind >= cols) & (pads_row > 0)
    rise = jnp.exp(rows.astype(F32) * log_decay)
    fall = jnp.exp((behind - cols).astype(F32) * log_decay)
    return jnp.where(allowed, rise * fall, 0.0)


def send_state(docs, acc, sum_out):
    sum_out[:, :KD, :] = acc[...].astype(BF)
    sum_out[:, KD:, :] = jnp.full((acc.shape[0], EXTRA, VD), docs[0].astype(F32), F32).astype(BF)


def lanes(shards):
    return jnp.concatenate([shards[i] for i in range(shards.shape[0])], axis=1)


def vector_of(rows, index):
    return rows[3 * index : 3 * index + 1] + rows[3 * index + 1 : 3 * index + 2] + rows[
        3 * index + 2 : 3 * index + 3
    ]


def entry_kernel(x, one, two, three, four, out):
    rows = x.shape[0]
    out[:rows] = x[...]
    pieces = []
    for vector in (one, two, three, four):
        value = vector[...]
        for _ in range(3):
            piece = value.astype(BF)
            pieces.append(piece.astype(F32))
            value = value - piece.astype(F32)
    pieces.append(jnp.zeros((EXTRA - len(pieces), x.shape[1]), F32))
    out[rows:] = jnp.concatenate(pieces, axis=0).astype(BF)


def project_kernel(
    heads, docs, x, vec, wq, wk, wv, cos, sin, end, ln_out, q_out, k_out, v_out, stat_out,
    sum_out, acc
):
    step = pl.program_id(0)
    rows = lanes(x).astype(F32)
    vectors = lanes(vec).astype(F32)
    mean = jnp.mean(rows, axis=1, keepdims=True)
    scale = lax.rsqrt(jnp.mean(rows * rows, axis=1, keepdims=True) - mean * mean + EPSILON)
    low = ((rows - mean) * scale * vector_of(vectors, 0) + vector_of(vectors, 1)).astype(BF)
    ln_out[...] = low
    stat_out[...] = jnp.concatenate([mean, scale], axis=1)
    values = dot(low, wv[...]).astype(BF)
    v_out[...] = values
    queries = dot(low, wq[...])
    keys = dot(low, wk[...])
    cosine, sine = cos[...], sin[...]

    @pl.when(step == 0)
    def _():
        acc[...] = jnp.zeros_like(acc)

    for h in range(heads):
        mine = slice(h * KD, (h + 1) * KD)
        q_out[:, mine] = turned(queries[:, mine], cosine, sine).astype(BF)
        key = (turned(keys[:, mine], cosine, sine) * KD ** (-0.5)).astype(BF)
        k_out[:, mine] = key
        key_end = (key.astype(F32) * end[:, h : h + 1]).astype(BF)
        acc[h] += dot_tn(key_end, values[:, h * VD : (h + 1) * VD])

    @pl.when(step == pl.num_programs(0) - 1)
    def _():
        send_state(docs, acc, sum_out)


def inner_kernel(heads, decay, low, wg, q, k, v, dcol, drow, prow, gate_out, inner_out):
    step = pl.program_id(0)
    gate_out[...] = dot(low[...], wg[...])
    docs_col = dcol[...]

    def turn(j, totals):
        at = pl.ds(pl.multiple_of(j * TILE, TILE), TILE)
        sums = []
        for h in range(heads):
            mine = slice(h * KD, (h + 1) * KD)
            wide = slice(h * VD, (h + 1) * VD)
            factor = tile_decay(decay[h], (step - j) * TILE, docs_col, drow[:, at], prow[:, at])
            weights = (dot_nt(q[:, mine], k[at, mine]) * factor).astype(BF)
            sums.append(totals[h] + dot(weights, v[at, wide]))
        return tuple(sums)

    zeros = tuple(jnp.zeros((TILE, VD), F32) for _ in range(heads))
    totals = lax.fori_loop(0, step + 1, turn, zeros)
    for h in range(heads):
        inner_out[:, h * VD : (h + 1) * VD] = totals[h]


def joined_state(decay, rows, one, two, three, link_two, link_three):
    states = []
    for h in range(one.shape[0]):
        far = jnp.exp(jnp.full((1, 1), rows, F32) * decay[h])
        states.append(
            (
                one[h, :KD].astype(F32)
                + two[h, :KD].astype(F32) * (link_two * far)
                + three[h, :KD].astype(F32) * (link_three * far * far)
            ).astype(BF)
        )
    return states


def doc_in(payload):
    return payload[0, KD : KD + 1, 0:1].astype(F32)


def mix_kernel(
    heads, rows, decay, inner, q, one, two, three, gate, dcol, pcol, wo, group_out, scale_out,
    gated_out, part_out, state_out, carry_out
):
    step = pl.program_id(0)
    before = doc_in(one)

    @pl.when(step == 0)
    def _():
        link_two = (doc_in(two) == before).astype(F32)
        link_three = (doc_in(three) == before).astype(F32)
        states = joined_state(decay, rows, one, two, three, link_two, link_three)
        for h in range(heads):
            state_out[h] = states[h]

    same = (dcol[...].astype(F32) == before).astype(F32)
    place = (step * TILE + 1 + lax.broadcasted_iota(jnp.int32, (TILE, 1), 0)).astype(F32)
    for h in range(heads):
        mine = slice(h * KD, (h + 1) * KD)
        wide = slice(h * VD, (h + 1) * VD)
        carry = same * jnp.exp(place * decay[h])
        carry_out[:, h : h + 1] = carry
        carried = (q[:, mine].astype(F32) * carry).astype(BF)
        mixed = inner[:, wide] + dot(carried, state_out[h])
        mean = jnp.mean(mixed, axis=1, keepdims=True)
        scale = lax.rsqrt(jnp.mean(mixed * mixed, axis=1, keepdims=True) - mean * mean + 1.0)
        grouped = (mixed - mean) * scale
        group_out[:, wide] = grouped
        scale_out[:, h : h + 1] = scale
        gate_h = gate[:, wide]
        gated_out[:, wide] = (pcol[...] * gate_h * jax.nn.sigmoid(gate_h) * grouped).astype(BF)
    part = dot(gated_out[...], wo[...]).astype(BF)
    sides, width = part_out.shape[1], part_out.shape[4]
    for side in range(sides):
        for f in range(2):
            first = (f * sides + side) * width
            part_out[0, side, f] = part[:, first : first + width]


def gate_kernel(heads, grad, wo, gate, group, scale, pcol, dgate_out, mix_out):
    sides = grad.shape[1]
    rows = jnp.concatenate(
        [grad[0, side, f] for f in range(2) for side in range(sides)], axis=1
    )
    passed = dot_nt(rows, wo[...]) * pcol[...]
    for h in range(heads):
        wide = slice(h * VD, (h + 1) * VD)
        gate_h, grouped = gate[:, wide], group[:, wide]
        squash = jax.nn.sigmoid(gate_h)
        upstream = passed[:, wide]
        dgate_out[:, wide] = (
            upstream * grouped * (squash + gate_h * squash * (1.0 - squash))
        ).astype(BF)
        grad_group = upstream * gate_h * squash
        mean = jnp.mean(grad_group, axis=1, keepdims=True)
        cross = jnp.mean(grad_group * grouped, axis=1, keepdims=True)
        mix_out[:, wide] = (scale[:, h : h + 1] * (grad_group - mean - grouped * cross)).astype(BF)


def back_kernel(
    heads, docs, decay, mix, q, k, v, carry, state, dcol, drow, prow, cos, sin, dq_out, dk_out,
    dv_out, sum_out, acc
):
    step = pl.program_id(0)

    @pl.when(step == 0)
    def _():
        acc[...] = jnp.zeros_like(acc)
        dk_out[...] = jnp.zeros_like(dk_out)
        dv_out[...] = jnp.zeros_like(dv_out)

    docs_col = dcol[...]

    def turn(j, totals):
        at = pl.ds(pl.multiple_of(j * TILE, TILE), TILE)
        sums = []
        for h in range(heads):
            mine = slice(h * KD, (h + 1) * KD)
            wide = slice(h * VD, (h + 1) * VD)
            query, grad_mixed, key = q[:, mine], mix[:, wide], k[at, mine]
            factor = tile_decay(decay[h], (step - j) * TILE, docs_col, drow[:, at], prow[:, at])
            weights = (dot_nt(query, key) * factor).astype(BF)
            grads = (dot_nt(grad_mixed, v[at, wide]) * factor).astype(BF)
            dk_out[at, mine] += dot_tn(grads, query)
            dv_out[at, wide] += dot_tn(weights, grad_mixed)
            sums.append(totals[h] + dot(grads, key))
        return tuple(sums)

    zeros = tuple(jnp.zeros((TILE, KD), F32) for _ in range(heads))
    totals = lax.fori_loop(0, step + 1, turn, zeros)
    for h in range(heads):
        mine = slice(h * KD, (h + 1) * KD)
        wide = slice(h * VD, (h + 1) * VD)
        lift = carry[:, h : h + 1]
        total = totals[h] + lift * dot_nt(mix[:, wide], state[h])
        dq_out[:, mine] = turned(total, cos[...], -sin[...]).astype(BF)
        acc[h] += dot_tn((q[:, mine].astype(F32) * lift).astype(BF), mix[:, wide])

    @pl.when(step == pl.num_programs(0) - 1)
    def _():
        send_state(docs, acc, sum_out)


def finish_kernel(
    heads, size, docs, decay, dk_in, dv_in, k, v, end, one, two, three, dq, dgate, wq, wk, wv, wg,
    cos, sin, x, stat, vec, dk_out, dv_out, part_out, rows_out, cols_out, state
):
    step = pl.program_id(0)

    @pl.when(step == 0)
    def _():
        last = docs[0].astype(F32)
        link_two = (doc_in(one) == last).astype(F32)
        link_three = (doc_in(two) == last).astype(F32)
        states = joined_state(decay, size, one, two, three, link_two, link_three)
        for h in range(heads):
            state[h] = states[h]

    cosine, sine = cos[...], -sin[...]
    for h in range(heads):
        mine = slice(h * KD, (h + 1) * KD)
        wide = slice(h * VD, (h + 1) * VD)
        lift = end[:, h : h + 1]
        grad_key = dk_in[:, mine] + lift * dot_nt(v[:, wide], state[h])
        dk_out[:, mine] = (turned(grad_key, cosine, sine) * KD ** (-0.5)).astype(BF)
        key_end = (k[:, mine].astype(F32) * lift).astype(BF)
        dv_out[:, wide] = (dv_in[:, wide] + dot(key_end, state[h])).astype(BF)
    part = (
        dot_nt(dq[...], wq[...])
        + dot_nt(dk_out[...], wk[...])
        + dot_nt(dv_out[...], wv[...])
        + dot_nt(dgate[...], wg[...])
    )
    count, width = part_out.shape[0], part_out.shape[2]
    for shard in range(count):
        part_out[shard] = part[:, shard * width : (shard + 1) * width].astype(BF)
    normed = (lanes(x).astype(F32) - stat[:, 0:1]) * stat[:, 1:2]
    scaled = part * vec[0:1, :]
    ones = jnp.ones((8, scaled.shape[1]), BF)
    rows_out[0, 0:8] = dot_nt(ones, scaled.astype(BF))
    rows_out[0, 8:16] = dot_nt(ones, (scaled * normed).astype(BF))
    sums = jnp.concatenate(
        [jnp.sum(part * normed, axis=0, keepdims=True), jnp.sum(part, axis=0, keepdims=True)],
        axis=0,
    )

    @pl.when(step == 0)
    def _():
        cols_out[...] = jnp.zeros_like(cols_out)

    cols_out[...] += sums


def feed_kernel(
    chunks, x, grads, vec, up_near, up_far, down_near, down_far, ln_out, grad_out, act_out,
    dup_out, part_out, stat_out, rows_out, cols_out, acc
):
    step = pl.program_id(0)
    count = x.shape[1]
    steps = count // TILE

    def at_rows(r):
        return pl.ds(pl.multiple_of(r * TILE, TILE), TILE)

    @pl.when(step == 0)
    def _():
        def start(r, carry):
            at = at_rows(r)
            rows = jnp.concatenate([x[i, at, :] for i in range(x.shape[0])], axis=1).astype(F32)
            mean = jnp.mean(rows, axis=1, keepdims=True)
            scale = lax.rsqrt(jnp.mean(rows * rows, axis=1, keepdims=True) - mean * mean + EPSILON)
            stat_out[at, :] = jnp.concatenate([mean, scale], axis=1)
            ln_out[at, :] = ((rows - mean) * scale * vec[2:3, :] + vec[3:4, :]).astype(BF)
            grad_out[at, :] = jnp.concatenate(
                [grads[i, at, :] for i in range(grads.shape[0])], axis=1
            )
            acc[at, :] = jnp.zeros((TILE, acc.shape[1]), F32)
            return carry

        lax.fori_loop(0, steps, start, 0)

    def units(up, down):
        def turn(r, carry):
            at = at_rows(r)
            lifted = dot(ln_out[at, :], up[...])
            share = 0.5 * (1.0 + lax.erf(lifted * 0.5**0.5))
            act_out[at, :] = (lifted * share).astype(BF)
            slope = share + lifted * jnp.exp(-0.5 * lifted * lifted) * 0.3989422804014327
            lowered = (slope * dot_nt(grad_out[at, :], down[...])).astype(BF)
            dup_out[at, :] = lowered
            acc[at, :] += dot_nt(lowered, up[...])
            return carry

        lax.fori_loop(0, steps, turn, 0)

    @pl.when(step < chunks)
    def _():
        units(up_near, down_near)

    @pl.when(step >= chunks)
    def _():
        units(up_far, down_far)

    @pl.when(step == pl.num_programs(0) - 1)
    def _():
        cols_out[...] = jnp.zeros_like(cols_out)
        sides, width = part_out.shape[1], part_out.shape[3]

        def finish(r, carry):
            at = at_rows(r)
            part = acc[at, :]
            for f in range(2):
                for side in range(sides):
                    first = (f * sides + side) * width
                    part_out[f, side, at, :] = part[:, first : first + width].astype(BF)
            rows = jnp.concatenate([x[i, at, :] for i in range(x.shape[0])], axis=1).astype(F32)
            normed = (rows - stat_out[at, 0:1]) * stat_out[at, 1:2]
            scaled = part * vec[2:3, :]
            ones = jnp.ones((8, scaled.shape[1]), BF)
            rows_out[r, 0:8] = dot_nt(ones, scaled.astype(BF))
            rows_out[r, 8:16] = dot_nt(ones, (scaled * normed).astype(BF))
            cols_out[...] += jnp.concatenate(
                [
                    jnp.sum(part * normed, axis=0, keepdims=True),
                    jnp.sum(part, axis=0, keepdims=True),
                ],
                axis=0,
            )
            return carry

        lax.fori_loop(0, steps, finish, 0)


def branch_kernel(full, mine, keep, other, hidden, grads, gain, stat, near, far, out):
    sums = (near[0] + far[0]) * (1.0 / full)
    one, two = (
        sums[at : at + 8].T[:, 0:1] for at in (0, 8)
    )
    upstream = keep[0, 0].astype(F32) + other[0, 0].astype(F32)
    scale = stat[:, 1:2]
    normed = (hidden[0] - stat[:, 0:1]) * scale
    out[0] = (
        grads[0].astype(F32)
        + scale
        * (upstream * gain[0] - one - normed * two)
    ).astype(BF)


def lower_kernel(act, down_near, down_far, out):
    units = down_near.shape[0]
    part = (dot(act[:, :units], down_near[...]) + dot(act[:, units:], down_far[...])).astype(BF)
    sides, width = out.shape[1], out.shape[3]
    for f in range(2):
        for side in range(sides):
            first = (f * sides + side) * width
            out[f, side] = part[:, first : first + width]


def prefetched(kernel, grid, in_specs, out_specs, outs, flops=0):
    return pl.pallas_call(
        kernel,
        grid_spec=pltpu.PrefetchScalarGridSpec(
            num_scalar_prefetch=1, grid=grid, in_specs=in_specs, out_specs=out_specs
        ),
        out_shape=[jax.ShapeDtypeStruct(shape, dtype) for shape, dtype in outs],
        cost_estimate=pl.CostEstimate(flops=flops, bytes_accessed=0, transcendentals=0),
        compiler_params=pltpu.CompilerParams(vmem_limit_bytes=VMEM_LIMIT),
    )


def bit_value(bit):
    return my_bit("tok", bit)[None].astype(jnp.int32)


def split_source(groups, rows, block):
    per_half = rows // (2 * block)
    count = groups * per_half

    def source(i, mine):
        keeps = (i >= count).astype(jnp.int32)
        half = jnp.where(keeps == 1, mine[0], 1 - mine[0])
        j = i - keeps * count
        return (j // per_half) * (2 * per_half) + half * per_half + j % per_half

    give = lambda i, mine: (jnp.minimum(i, count - 1), 0)
    keep = lambda i, mine: (jnp.maximum(i - count, 0), 0)
    return count, source, give, keep


def weight_kernel(count, mine, left, *refs):
    give, keep = refs[-2:]

    def fill(out):
        first = 0
        for right in refs[:-2]:
            width = right.shape[1]
            out[:, first : first + width] = dot_tn(left[...], right[...]).astype(BF)
            first += width

    @pl.when(pl.program_id(0) < count)
    def _():
        fill(give)

    @pl.when(pl.program_id(0) >= count)
    def _():
        fill(keep)


def weight_grad(bit, groups, left, *rights):
    rows, columns = left.shape
    width = sum(right.shape[1] for right in rights)
    block = min(CHUNK, columns // groups // 2)
    count, source, give, keep = split_source(groups, columns // groups, block)
    half = (columns // 2, width)
    return prefetched(
        partial(weight_kernel, count),
        (2 * count,),
        [pl.BlockSpec((rows, block), lambda i, mine: (0, source(i, mine)))]
        + [
            pl.BlockSpec(right.shape, lambda i, mine: (0, 0), pipeline_mode=pl.Buffered(1))
            for right in rights
        ],
        [pl.BlockSpec((block, width), give), pl.BlockSpec((block, width), keep)],
        [(half, BF), (half, BF)],
        4 * rows * columns * width,
    )(bit_value(bit), left, *rights)


def turned_place(i, order):
    place = 0
    for k, bit in enumerate(order):
        place = place + (((i >> (len(order) - 1 - k)) & 1) << bit)
    return place


def outer_kernel(mine, gated, grad, give, keep):
    part = dot_tn(gated[...], jnp.concatenate([grad[0, 0, 0], grad[1, 0, 0]], axis=0)).astype(BF)
    half = give.shape[0]

    @pl.when(mine[0] == 0)
    def _():
        keep[...] = part[:half]
        give[...] = part[half:]

    @pl.when(mine[0] == 1)
    def _():
        keep[...] = part[half:]
        give[...] = part[:half]


def fold_kernel(count, mine, one, two, give, keep):
    total = (one[...].astype(F32) + two[...].astype(F32)).astype(BF)

    @pl.when(pl.program_id(0) < count)
    def _():
        give[...] = total

    @pl.when(pl.program_id(0) >= count)
    def _():
        keep[...] = total


def fold(bit, groups, one, two):
    rows, columns = one.shape
    block = min(CHUNK // 2, rows // groups // 2)
    count, source, give, keep = split_source(groups, rows // groups, block)
    spec = pl.BlockSpec((block, columns), lambda i, mine: (source(i, mine), 0))
    half = (rows // 2, columns)
    return prefetched(
        partial(fold_kernel, count),
        (2 * count,),
        [spec, spec],
        [pl.BlockSpec((block, columns), give), pl.BlockSpec((block, columns), keep)],
        [(half, BF), (half, BF)],
    )(bit_value(bit), one, two)


def scatter_rest(give, keep, order, groups=1, waits=None):
    values, others = [], []
    for place, bit in enumerate(order):
        if waits and place in waits:
            give = after(give, *waits[place])
        other = swapped(give, "tok", 1 << bit)
        if waits and ("seen", place) in waits:
            other = after(other, *waits["seen", place])
        others.append(other)
        if place + 1 < len(order):
            give, keep = fold(order[place + 1], groups, keep, other)
            values.append(give)
        else:
            values.append((keep, other))
    return values, others


def total(pair):
    return pair[0].astype(F32) + pair[1].astype(F32)


def spread_kernel(per_half, mine, near, other, out):
    here = pl.program_id(0) // per_half == mine[0]

    @pl.when(here)
    def _():
        out[...] = near[...].astype(out.dtype)

    @pl.when(jnp.logical_not(here))
    def _():
        out[...] = other[...].astype(out.dtype)


def gather_one(value, bit):
    return joined(value, swapped(value, "tok", 1 << bit), my_bit("tok", bit) == 0, 0)


def gather_wide(value, order):
    for bit in order[:0:-1]:
        value = gather_one(value, bit)
    bit = order[0]
    other = swapped(value, "tok", 1 << bit)
    rows, columns = value.shape
    block = min(CHUNK // 2, rows)
    per_half = rows // block

    def spec(mirror):
        def index(i, mine):
            half = 1 - mine[0] if mirror else mine[0]
            return (jnp.clip(i - half * per_half, 0, per_half - 1), 0)

        return pl.BlockSpec((block, columns), index)

    return prefetched(
        partial(spread_kernel, per_half),
        (2 * per_half,),
        [spec(False), spec(True)],
        [pl.BlockSpec((block, columns), lambda i, mine: (i, 0))],
        [((2 * rows, columns), F32)],
    )(bit_value(bit), value, other)[0], value


def order_kernel(plan, *refs):
    outs = list(refs[len(plan) :])
    for part, count in zip(refs, plan, strict=False):
        if count == 1:
            out = outs.pop(0)
            rows, columns = out.shape[0], part.shape[2]
            for i in range(part.shape[1] // rows):
                at = slice(i * columns, (i + 1) * columns)
                out[:, at] = part[0, i * rows : (i + 1) * rows].astype(F32)
            continue
        first = 0
        for _ in range(count):
            out = outs.pop(0)
            out[...] = part[0, :, first : first + out.shape[1]].astype(F32)
            first += out.shape[1]


def packed_pieces(first, *others):
    columns = others[0].shape[1]
    parts = [first[:, i : i + columns] for i in range(0, first.shape[1], columns)]
    return jnp.concatenate([*parts, *others], axis=0)


def in_order(pieces, plan):
    count, rows, columns = pieces.shape
    part = rows // len(plan)

    def spec(which, order):
        return pl.BlockSpec(
            (1, part, columns), lambda i: (turned_place(i, order), which, 0)
        )

    shapes = [shape for _, parts in plan for shape in parts]
    return pl.pallas_call(
        partial(order_kernel, [len(parts) for _, parts in plan]),
        grid=(count,),
        in_specs=[spec(which, order) for which, (order, _) in enumerate(plan)],
        out_specs=[pl.BlockSpec(shape, lambda i: (i, 0)) for shape in shapes],
        out_shape=[jax.ShapeDtypeStruct((count * high, wide), F32) for high, wide in shapes],
        cost_estimate=pl.CostEstimate(flops=0, bytes_accessed=0, transcendentals=0),
        compiler_params=pltpu.CompilerParams(vmem_limit_bytes=VMEM_LIMIT),
    )(*[pieces] * len(plan))


def body(
    tokens,
    mix_gain,
    mix_bias,
    query_weight,
    key_weight,
    value_weight,
    gate_weight,
    output_weight,
    feed_gain,
    feed_bias,
    up_weight,
    down_weight,
    doc_ids,
    pad_mask,
    out_grad,
):
    row_count, width = tokens.shape
    heads_here = query_weight.shape[1] // KD
    shards = lax.axis_size("head")
    full_width = width * shards
    sides = shards // 2
    spread = lax.axis_index("head") // sides
    side = lax.axis_index("head") % sides
    half_rows = row_count // 2
    block = lax.axis_index("tok")

    packed = pl.pallas_call(
        entry_kernel,
        out_shape=jax.ShapeDtypeStruct((row_count + EXTRA, width), BF),
        compiler_params=pltpu.CompilerParams(vmem_limit_bytes=VMEM_LIMIT),
    )(tokens, mix_gain[None], mix_bias[None], feed_gain[None], feed_bias[None])
    rows_raw = lax.all_gather(packed, "head", axis=0)
    vector_rows = rows_raw[:, row_count:, :].astype(F32)
    vectors = (vector_rows[:, 0:12:3] + vector_rows[:, 1:12:3] + vector_rows[:, 2:12:3]).transpose(
        1, 0, 2
    )
    side_vectors = lax.dynamic_index_in_dim(
        vectors.reshape(4, 2, sides, width), side, 2, keepdims=False
    )
    vectors = vectors.reshape(4, full_width)

    order_one, order_two = bit_orders()
    first_head = lax.axis_index("head") * heads_here
    log_decay = jnp.log(
        1.0 - 2.0 ** (-5.0 - (first_head + jnp.arange(heads_here, dtype=jnp.int32)).astype(F32))
    )
    position = jnp.arange(row_count, dtype=jnp.int32)
    frequency = 10000.0 ** (-2.0 * jnp.arange(KD // 2, dtype=jnp.int32).astype(F32) / KD)
    angles = (block * row_count + position).astype(F32)[:, None] * frequency[None, :]
    cosine, sine = jnp.cos(angles), jnp.sin(angles)
    padding = pad_mask.astype(F32)
    last_doc = doc_ids[row_count - 1]

    end_factor = (padding * (doc_ids == last_doc).astype(F32))[:, None] * jnp.exp(
        (row_count - 1 - position).astype(F32)[:, None] * log_decay[None, :]
    )

    late_grad = after(out_grad, rows_raw, cosine, sine, end_factor)
    grad_keep, grad_give = halves(late_grad, "head", shards.bit_length() - 2, 0)
    grad_seen = swapped(grad_give, "head", sides)
    up_piece, down_piece = own_piece(up_weight, order_one), own_piece(down_weight, order_two)
    both_pieces = jnp.concatenate([up_piece, down_piece.reshape(up_piece.shape)], axis=0)

    docs_col, docs_row = doc_ids[:, None], doc_ids[None, :]
    pads_col, pads_row = padding[:, None], padding[None, :]
    inner_width, value_width = heads_here * KD, heads_here * VD
    states = pltpu.VMEM((heads_here, KD, VD), F32)
    state_shape = (heads_here, KD, VD)
    sent_shape = (heads_here, KD + EXTRA, VD)
    shard_tiles = pl.BlockSpec((shards, TILE, width), lambda i: (0, i, 0))
    per_half = half_rows // TILE
    split_tiles = pl.BlockSpec(
        (1, sides, 2, TILE, width), lambda i: (i // per_half, 0, 0, i % per_half, 0)
    )
    last_docs = doc_ids[row_count - 1 :]
    rows_first, query_rot, key_rot, values, stats, summary = call(
        partial(project_kernel, heads_here),
        row_count,
        [
            SCALARS,
            shard_tiles,
            pl.BlockSpec((shards, EXTRA, width), lambda i: (0, row_count // EXTRA, 0)),
            whole(full_width, inner_width),
            whole(full_width, inner_width),
            whole(full_width, value_width),
            tiles(KD // 2),
            tiles(KD // 2),
            tiles(heads_here),
        ],
        [
            ((row_count, full_width), BF),
            ((row_count, inner_width), BF),
            ((row_count, inner_width), BF),
            ((row_count, value_width), BF),
            ((row_count, 2), F32),
            (sent_shape, BF),
        ],
        [
            tiles(full_width),
            tiles(inner_width),
            tiles(inner_width),
            tiles(value_width),
            tiles(2),
            held(*sent_shape),
        ],
        [states],
    )(
        last_docs,
        rows_raw,
        rows_raw,
        query_weight,
        key_weight,
        value_weight,
        cosine,
        sine,
        end_factor,
    )
    one_back, two_back, three_back = (shifted(summary, by) for by in (1, 2, 3))
    grad_seen = after(grad_seen, summary)
    side_grads = joined(grad_keep[None], grad_seen[None], spread == 0, 0)
    grad_rows, grads_last = gather_side(side_grads[:, None])
    grad_rows = grad_rows.reshape(shards, half_rows, width)
    (both_seen,) = far_swap(after(both_pieces, grad_seen))
    up_seen = both_seen[: up_piece.shape[0]]
    down_seen = both_seen[up_piece.shape[0] :].reshape(down_piece.shape)
    up_other = gather_back(up_seen, order_one)
    down_other = gather_back(down_seen, order_two)
    gate_pre, inner_part = call(
        partial(inner_kernel, heads_here),
        row_count,
        [
            SCALARS,
            tiles(full_width),
            whole(full_width, value_width),
            tiles(inner_width),
            whole(row_count, inner_width),
            whole(row_count, value_width),
            tiles(1),
            whole(1, row_count),
            whole(1, row_count),
        ],
        [((row_count, value_width), F32)] * 2,
        [tiles(value_width)] * 2,
    )(
        after(log_decay, side_grads),
        rows_first,
        gate_weight,
        query_rot,
        key_rot,
        values,
        docs_col,
        docs_row,
        pads_row,
    )
    flat_group, group_scale, gated, mix_part, state_low, carry_factor = call(
        partial(mix_kernel, heads_here, row_count),
        row_count,
        [
            SCALARS,
            tiles(value_width),
            tiles(inner_width),
            whole(*sent_shape),
            whole(*sent_shape),
            whole(*sent_shape),
            tiles(value_width),
            tiles(1),
            tiles(1),
            whole(value_width, full_width),
        ],
        [
            ((row_count, value_width), F32),
            ((row_count, heads_here), F32),
            ((row_count, value_width), BF),
            ((2, sides, 2, half_rows, width), BF),
            (state_shape, BF),
            ((row_count, heads_here), F32),
        ],
        [
            tiles(value_width),
            tiles(heads_here),
            tiles(value_width),
            split_tiles,
            held(*state_shape),
            tiles(heads_here),
        ],
    )(
        log_decay,
        inner_part,
        query_rot,
        one_back,
        two_back,
        three_back,
        gate_pre,
        docs_col,
        pads_col,
        output_weight,
    )
    mix_part = after(mix_part, grads_last, both_seen)
    side_tokens = lax.dynamic_index_in_dim(
        lax.dynamic_slice_in_dim(rows_raw, spread * half_rows, half_rows, axis=1).reshape(
            2, sides, half_rows, width
        ),
        side,
        1,
        keepdims=False,
    )
    mixed_sum = lax.psum_scatter(
        mix_part.reshape(shards, 2, half_rows, width), "head", scatter_dimension=0
    )
    hidden = lax.optimization_barrier(side_tokens.astype(F32) + mixed_sum.astype(F32))
    hidden_rows = gather_side(hidden.astype(BF)[:, None])[0].reshape(shards, half_rows, width)
    units = up_weight.shape[1]
    chunks = units // CHUNK
    rows_second, grad_plain, act_low, grad_up, feed_part, stats_second, row_second, cols_second = (
        pl.pallas_call(
            partial(feed_kernel, chunks),
            grid=(2 * chunks,),
            in_specs=[
                whole(shards, half_rows, width),
                whole(shards, half_rows, width),
                whole(4, full_width),
                pl.BlockSpec((full_width, CHUNK), lambda i: (0, jnp.minimum(i, chunks - 1))),
                pl.BlockSpec((full_width, CHUNK), lambda i: (0, jnp.maximum(i - chunks, 0))),
                pl.BlockSpec((CHUNK, full_width), lambda i: (jnp.minimum(i, chunks - 1), 0)),
                pl.BlockSpec((CHUNK, full_width), lambda i: (jnp.maximum(i - chunks, 0), 0)),
            ],
            out_specs=[
                held(half_rows, full_width),
                held(half_rows, full_width),
                pl.BlockSpec((half_rows, CHUNK), lambda i: (0, i)),
                pl.BlockSpec((half_rows, CHUNK), lambda i: (0, i)),
                held(2, sides, half_rows, width),
                held(half_rows, 2),
                held(half_rows // TILE, 16, TILE),
                held(2, full_width),
            ],
            out_shape=[
                jax.ShapeDtypeStruct((half_rows, full_width), BF),
                jax.ShapeDtypeStruct((half_rows, full_width), BF),
                jax.ShapeDtypeStruct((half_rows, 2 * units), BF),
                jax.ShapeDtypeStruct((half_rows, 2 * units), BF),
                jax.ShapeDtypeStruct((2, sides, half_rows, width), BF),
                jax.ShapeDtypeStruct((half_rows, 2), F32),
                jax.ShapeDtypeStruct((half_rows // TILE, 16, TILE), F32),
                jax.ShapeDtypeStruct((2, full_width), F32),
            ],
            scratch_shapes=[pltpu.VMEM((half_rows, full_width), F32)],
            cost_estimate=pl.CostEstimate(flops=0, bytes_accessed=0, transcendentals=0),
            compiler_params=pltpu.CompilerParams(vmem_limit_bytes=VMEM_LIMIT),
        )(hidden_rows, grad_rows, vectors, up_weight, up_other, down_weight, down_other)
    )
    feed_value, feed_seen = scatter_side_start(feed_part)
    for bit in list(side_bits())[:0:-1]:
        row_second = row_second + swapped(row_second, "head", 1 << bit)
    row_seen = swapped(row_second, "head", 1)
    down_give, down_keep = weight_grad(order_one[0], 2, act_low, grad_plain)
    up_give, up_keep = weight_grad(order_two[0], 1, rows_second, grad_up)
    row_seen = after(row_seen, down_give, up_give)
    half_block = pl.BlockSpec((1, TILE, width), lambda f, i, mine: (f, i, 0))
    row_block = pl.BlockSpec((TILE, 2), lambda f, i, mine: (i, 0))
    sum_block = pl.BlockSpec((1, 16, TILE), lambda f, i, mine: (i, 0, 0))
    (branch,) = prefetched(
        partial(branch_kernel, full_width),
        (2, half_rows // TILE),
        [
            pl.BlockSpec((1, 1, TILE, width), lambda f, i, mine: (f, mine[0], i, 0)),
            pl.BlockSpec((1, 1, TILE, width), lambda f, i, mine: (f, 0, i, 0)),
            half_block,
            half_block,
            pl.BlockSpec((1, 1, width), lambda f, i, mine: (f, 0, 0)),
            row_block,
            sum_block,
            sum_block,
        ],
        [half_block],
        [((2, half_rows, width), BF)],
    )(
        my_bit("head", 0)[None].astype(jnp.int32),
        feed_value,
        feed_seen[:, None] if feed_seen.ndim == 3 else feed_seen,
        hidden,
        side_grads,
        side_vectors[2][:, None, :],
        stats_second,
        row_second,
        row_seen,
    )
    grad_branch = lax.all_gather(branch, "head", axis=0).reshape(
        2, sides, 2, half_rows, width
    )

    down_part = pl.pallas_call(
        lower_kernel,
        grid=(half_rows // TILE,),
        in_specs=[tiles(2 * units), whole(units, full_width), whole(units, full_width)],
        out_specs=pl.BlockSpec((2, sides, TILE, width), lambda i: (0, 0, i, 0)),
        out_shape=jax.ShapeDtypeStruct((2, sides, half_rows, width), BF),
        cost_estimate=pl.CostEstimate(flops=0, bytes_accessed=0, transcendentals=0),
        compiler_params=pltpu.CompilerParams(vmem_limit_bytes=VMEM_LIMIT),
    )(after(act_low, branch), down_weight, down_other)

    down_sum, down_seen_all = scatter_rest(
        down_give, down_keep, order_one, 2, {0: (branch,), ("seen", 1): (down_part,)}
    )
    up_sum, up_seen_all = scatter_rest(
        up_give, up_keep, order_two, 1, {0: (branch,), ("seen", 1): (down_part,)}
    )

    dgate, grad_mixed = call(
        partial(gate_kernel, heads_here),
        row_count,
        [
            split_tiles,
            whole(value_width, full_width),
            tiles(value_width),
            tiles(value_width),
            tiles(heads_here),
            tiles(1),
        ],
        [((row_count, value_width), BF), ((row_count, value_width), BF)],
        [tiles(value_width), tiles(value_width)],
    )(
        grad_branch,
        output_weight,
        gate_pre,
        flat_group,
        group_scale,
        after(pads_col, down_sum[1], up_sum[1]),
    )
    half_down = down_sum[-1][0].shape[0] // 2
    up_pair = lax.optimization_barrier((*up_sum[-1], dgate))[:2]
    down_pair = lax.optimization_barrier((*down_sum[-1], dgate))[:2]
    up_give = total([part[:, units:] for part in up_pair]).astype(BF)
    down_give = total([part[half_down:] for part in down_pair]).astype(BF)
    dq, dk_part, dv_part, grad_state = call(
        partial(back_kernel, heads_here),
        row_count,
        [
            SCALARS,
            SCALARS,
            tiles(value_width),
            tiles(inner_width),
            whole(row_count, inner_width),
            whole(row_count, value_width),
            tiles(heads_here),
            whole(*state_shape),
            tiles(1),
            whole(1, row_count),
            whole(1, row_count),
            tiles(KD // 2),
            tiles(KD // 2),
        ],
        [
            ((row_count, inner_width), BF),
            ((row_count, inner_width), F32),
            ((row_count, value_width), F32),
            (sent_shape, BF),
        ],
        [
            tiles(inner_width),
            held(row_count, inner_width),
            held(row_count, value_width),
            held(*sent_shape),
        ],
        [states],
        10 * row_count * full_width * value_width,
    )(
        last_docs,
        after(log_decay, down_part, up_give, down_give),
        grad_mixed,
        query_rot,
        key_rot,
        values,
        carry_factor,
        state_low,
        docs_col,
        docs_row,
        pads_row,
        cosine,
        sine,
    )
    width_out = (value_width // 2, full_width)
    outw_give, outw_keep = prefetched(
        outer_kernel,
        (shards,),
        [
            pl.BlockSpec(
                (row_count, value_width), lambda i, mine: (0, 0), pipeline_mode=pl.Buffered(1)
            ),
            pl.BlockSpec(
                (2, 1, 1, half_rows, width), lambda i, mine: (0, i % sides, i // sides, 0, 0)
            ),
        ],
        [pl.BlockSpec((value_width // 2, width), lambda i, mine: (0, i))] * 2,
        [(width_out, BF), (width_out, BF)],
        4 * row_count * value_width * full_width,
    )(bit_value(order_one[0]), after(gated, dq, up_give, down_give), grad_branch)
    outw_sum, outw_seen = scatter_rest(outw_give, outw_keep, order_one)
    gw_give, gw_keep = weight_grad(order_two[0], 1, rows_first, after(dgate, dq))
    gw_sum, gw_seen = scatter_rest(gw_give, gw_keep, order_two)
    one_on, two_on, three_on = (shifted(grad_state, -by) for by in (1, 2, 3))
    up_far, down_far = far_swap(up_give, down_give)
    up_far, down_far = after(up_far, gw_give, outw_give), after(down_far, gw_give, outw_give)
    up_near = total([part[:, :units] for part in up_pair]) + up_far.astype(F32)
    down_near = total([part[:half_down] for part in down_pair]) + down_far.astype(F32)
    down_low, up_low = down_near.astype(BF), up_near.astype(BF)
    feed_pieces = after(packed_pieces(down_low, up_low), one_on, two_on, three_on)
    feed_pieces = lax.all_gather(feed_pieces, "tok", axis=0)
    grad_down, grad_upw = in_order(
        feed_pieces, ((order_one, [down_low.shape]), (order_two, [up_low.shape]))
    )
    dk, dv, last_part, row_sums, column_first = call(
        partial(finish_kernel, heads_here, row_count),
        row_count,
        [
            SCALARS,
            SCALARS,
            tiles(inner_width),
            tiles(value_width),
            tiles(inner_width),
            tiles(value_width),
            tiles(heads_here),
            whole(*sent_shape),
            whole(*sent_shape),
            whole(*sent_shape),
            tiles(inner_width),
            tiles(value_width),
            whole(full_width, inner_width),
            whole(full_width, inner_width),
            whole(full_width, value_width),
            whole(full_width, value_width),
            tiles(KD // 2),
            tiles(KD // 2),
            shard_tiles,
            tiles(2),
            whole(4, full_width),
        ],
        [
            ((row_count, inner_width), BF),
            ((row_count, value_width), BF),
            ((shards, row_count + EXTRA, width), BF),
            ((row_count // TILE, 16, TILE), F32),
            ((2, full_width), F32),
        ],
        [
            tiles(inner_width),
            tiles(value_width),
            shard_tiles,
            pl.BlockSpec((1, 16, TILE), lambda i: (i, 0, 0)),
            held(2, full_width),
        ],
        [pltpu.VMEM(state_shape, BF)],
        12 * row_count * full_width * value_width,
    )(
        last_docs,
        after(log_decay, up_near, down_near),
        dk_part,
        dv_part,
        key_rot,
        values,
        end_factor,
        one_on,
        two_on,
        three_on,
        dq,
        dgate,
        query_weight,
        key_weight,
        value_weight,
        gate_weight,
        cosine,
        sine,
        rows_raw,
        stats,
        vectors,
    )
    count = row_count // TILE
    line = jnp.concatenate([row_sums[:, 0], row_sums[:, 8]], axis=0)
    line = jnp.pad(line, ((0, EXTRA - 2 * count - 4), (0, width - TILE)))
    columns = jnp.concatenate([column_first, cols_second]).reshape(4, shards, width)
    extra = jnp.concatenate(
        [jnp.broadcast_to(line[None], (shards, *line.shape)), columns.transpose(1, 0, 2)], axis=1
    )
    last_part = lax.dynamic_update_slice_in_dim(last_part, extra.astype(BF), row_count, axis=1)
    vw_give, vw_keep = weight_grad(order_one[0], 1, rows_first, dv)
    qkw_give, qkw_keep = weight_grad(order_two[0], 1, rows_first, dq, dk)
    last_part = after(last_part, feed_pieces, vw_give, qkw_give, outw_sum[0], gw_seen[0])
    last_sum = lax.psum_scatter(last_part, "head", scatter_dimension=0).astype(F32)
    grad_ln1 = last_sum[:row_count]
    sums_first = last_sum[row_count:, :TILE] / full_width
    sums_first = jnp.stack(
        [sums_first[:count].reshape(row_count), sums_first[count : 2 * count].reshape(row_count)],
        axis=1,
    )
    columns = lax.psum(last_sum[row_count + EXTRA - 4 :], "tok")
    result = (hidden + scatter_side(after(down_part, last_sum))).astype(BF)
    result_keep = lax.dynamic_index_in_dim(result, spread, 0, keepdims=False)
    result_give = lax.dynamic_index_in_dim(result, 1 - spread, 0, keepdims=False)
    layer_out = joined(result_keep, swapped(result_give, "head", sides), spread == 0, 0)

    outw_low, gw_low = total(outw_sum[-1]).astype(BF), total(gw_sum[-1]).astype(BF)
    waits = {1: (gw_sum[0],), 2: (outw_sum[1], gw_sum[1])}
    vw_sum, _ = scatter_rest(vw_give, vw_keep, order_one, 1, waits)
    qkw_sum, _ = scatter_rest(qkw_give, qkw_keep, order_two, 1, waits)
    vw_low, qkw_low = total(vw_sum[-1]).astype(BF), total(qkw_sum[-1]).astype(BF)
    pieces = packed_pieces(outw_low, gw_low, vw_low, qkw_low)
    pieces = lax.all_gather(pieces, "tok", axis=0)
    high = qkw_low.shape[0]
    grad_outw, grad_gw, grad_vw, grad_qw, grad_kw = in_order(
        pieces,
        (
            (order_one, [outw_low.shape]),
            (order_two, [gw_low.shape]),
            (order_one, [vw_low.shape]),
            (order_two, [(high, inner_width), (high, inner_width)]),
        ),
    )

    norm_first = (tokens.astype(F32) - stats[:, 0:1]) * stats[:, 1:2]
    branch_rows = lax.dynamic_index_in_dim(
        lax.dynamic_index_in_dim(grad_branch, side, 1, keepdims=False), spread, 1, keepdims=False
    ).reshape(row_count, width)
    tokens_grad = branch_rows.astype(F32) + stats[:, 1:2] * (
        grad_ln1 * mix_gain - sums_first[:, 0:1] - norm_first * sums_first[:, 1:2]
    )
    return (
        layer_out,
        tokens_grad,
        columns[0],
        columns[1],
        grad_qw,
        grad_kw,
        grad_vw,
        grad_gw,
        grad_outw,
        columns[2],
        columns[3],
        grad_upw,
        grad_down,
    )


def solution(mesh):
    rows = P("tok", "head")
    columns = P(None, "head")
    return jax.shard_map(
        body,
        mesh=mesh,
        in_specs=(
            rows,
            P("head"),
            P("head"),
            columns,
            columns,
            columns,
            columns,
            P("head", None),
            P("head"),
            P("head"),
            columns,
            P("head", None),
            P("tok"),
            P("tok"),
            rows,
        ),
        out_specs=(
            rows,
            rows,
            P("head"),
            P("head"),
            columns,
            columns,
            columns,
            columns,
            P("head", None),
            P("head"),
            P("head"),
            columns,
            P("head", None),
        ),
        check_vma=False,
    )
```

```python
from functools import partial

import jax
import jax.numpy as jnp
from jax import lax
from jax.experimental import pallas as pl
from jax.experimental.pallas import tpu as pltpu
from jax.sharding import PartitionSpec as P

KD = 256
VD = 512
EPSILON = 1e-05
BF = jnp.bfloat16
F32 = jnp.float32


def after(value, *others):
    return lax.optimization_barrier((value, *others))[0]


def shifted(value, by):
    length = lax.axis_size("tok")
    pairs = [(i, i + by) for i in range(length) if 0 <= i + by < length]
    return lax.ppermute(value, "tok", pairs)


def swapped(value, axis, mask):
    return lax.ppermute(value, axis, [(i, i ^ mask) for i in range(lax.axis_size(axis))])


def my_bit(axis, bit):
    return (lax.axis_index(axis) >> bit) & 1


def joined(value, other, first, axis):
    return jnp.where(
        first,
        jnp.concatenate([value, other], axis=axis),
        jnp.concatenate([other, value], axis=axis),
    )


def bit_orders():
    bits = lax.axis_size("tok").bit_length() - 1
    first = list(range(bits))
    second = [0, 2, 1] if bits == 3 else first[bits // 2 :] + first[: bits // 2]
    return first, second


def halves(value, axis, bit, dim):
    shape = value.shape
    pieces = value.reshape(*shape[:dim], 2, shape[dim] // 2, *shape[dim + 1 :])
    mine = my_bit(axis, bit)
    keep = lax.dynamic_index_in_dim(pieces, mine, dim, keepdims=False)
    give = lax.dynamic_index_in_dim(pieces, 1 - mine, dim, keepdims=False)
    return keep, give


def own_piece(value, order, dim=0):
    for bit in order:
        value = halves(value, "tok", bit, dim)[0]
    return value


def gather_back(value, order):
    for bit in order[::-1]:
        other = swapped(value, "tok", 1 << bit)
        value = joined(value, other, my_bit("tok", bit) == 0, 0)
    return value


def far_swap(*values):
    return [swapped(value, "head", lax.axis_size("head") // 2) for value in values]


def side_bits():
    return range(lax.axis_size("head").bit_length() - 2)


def gather_side(value):
    for bit in side_bits():
        other = swapped(value, "head", 1 << bit)
        value = joined(value, other, my_bit("head", bit) == 0, 1)
    return value, other


def scatter_side_start(value):
    for bit in list(side_bits())[:0:-1]:
        keep, give = halves(value, "head", bit, 1)
        value = keep.astype(F32) + swapped(give.astype(BF), "head", 1 << bit).astype(F32)
    give = halves(value, "head", 0, 1)[1]
    return value, swapped(give.astype(BF), "head", 1)


def scatter_side(value):
    for bit in list(side_bits())[::-1]:
        keep, give = halves(value, "head", bit, 1)
        value = keep.astype(F32) + swapped(give.astype(BF), "head", 1 << bit).astype(F32)
    return value[:, 0]


def sum_side(value):
    for bit in side_bits():
        value = value + swapped(value, "head", 1 << bit)
    return value


TILE = 256
EXTRA = 16
CHUNK = 512
WIDE = 512
VMEM_LIMIT = 58 << 20


def dot(left, right):
    return jnp.dot(left, right, preferred_element_type=F32)


def dot_nt(left, right):
    return lax.dot_general(left, right, (((1,), (1,)), ((), ())), preferred_element_type=F32)


def dot_tn(left, right):
    return lax.dot_general(left, right, (((0,), (0,)), ((), ())), preferred_element_type=F32)


def tiles(columns):
    return pl.BlockSpec((TILE, columns), lambda i: (i, 0))


def whole(*shape):
    zeros = (0,) * len(shape)
    return pl.BlockSpec(shape, lambda i: zeros, pipeline_mode=pl.Buffered(1))


def held(*shape):
    zeros = (0,) * len(shape)
    return pl.BlockSpec(shape, lambda i: zeros)


SCALARS = pl.BlockSpec(memory_space=pltpu.SMEM)


def call(kernel, rows, in_specs, outs, out_specs, scratch=(), flops=0):
    return pl.pallas_call(
        kernel,
        grid=(rows // TILE,),
        in_specs=in_specs,
        out_specs=out_specs,
        out_shape=[jax.ShapeDtypeStruct(shape, dtype) for shape, dtype in outs],
        scratch_shapes=list(scratch),
        cost_estimate=pl.CostEstimate(flops=flops, bytes_accessed=0, transcendentals=0),
        compiler_params=pltpu.CompilerParams(vmem_limit_bytes=VMEM_LIMIT),
    )


def turned(value, cosine, sine):
    half_dim = KD // 2
    front, back = value[:, :half_dim], value[:, half_dim:]
    return jnp.concatenate([front * cosine - back * sine, back * cosine + front * sine], axis=1)


def tile_decay(log_decay, behind, docs_col, docs_row, pads_row):
    rows = lax.broadcasted_iota(jnp.int32, (TILE, 1), 0)
    cols = lax.broadcasted_iota(jnp.int32, (1, WIDE), 1)
    allowed = (docs_col == docs_row) & (rows + behind >= cols) & (pads_row > 0)
    rise = jnp.exp(rows.astype(F32) * log_decay)
    fall = jnp.exp((behind - cols).astype(F32) * log_decay)
    return jnp.where(allowed, rise * fall, 0.0)


def send_state(docs, acc, sum_out):
    sum_out[:, :KD, :] = acc[...].astype(BF)
    sum_out[:, KD:, :] = jnp.full((acc.shape[0], EXTRA, VD), docs[0].astype(F32), F32).astype(BF)


def lanes(shards):
    return jnp.concatenate([shards[i] for i in range(shards.shape[0])], axis=1)


def vector_of(rows, index):
    return rows[3 * index : 3 * index + 1] + rows[3 * index + 1 : 3 * index + 2] + rows[
        3 * index + 2 : 3 * index + 3
    ]


def entry_kernel(x, one, two, three, four, out):
    rows = x.shape[0]
    out[:rows] = x[...]
    pieces = []
    for vector in (one, two, three, four):
        value = vector[...]
        for _ in range(3):
            piece = value.astype(BF)
            pieces.append(piece.astype(F32))
            value = value - piece.astype(F32)
    pieces.append(jnp.zeros((EXTRA - len(pieces), x.shape[1]), F32))
    out[rows:] = jnp.concatenate(pieces, axis=0).astype(BF)


def project_kernel(
    heads, docs, x, vec, wq, wk, wv, cos, sin, end, ln_out, q_out, k_out, v_out, stat_out,
    sum_out, acc
):
    step = pl.program_id(0)
    rows = lanes(x).astype(F32)
    vectors = lanes(vec).astype(F32)
    mean = jnp.mean(rows, axis=1, keepdims=True)
    scale = lax.rsqrt(jnp.mean(rows * rows, axis=1, keepdims=True) - mean * mean + EPSILON)
    low = ((rows - mean) * scale * vector_of(vectors, 0) + vector_of(vectors, 1)).astype(BF)
    ln_out[...] = low
    stat_out[...] = jnp.concatenate([mean, scale], axis=1)
    values = dot(low, wv[...]).astype(BF)
    v_out[...] = values
    queries = dot(low, wq[...])
    keys = dot(low, wk[...])
    cosine, sine = cos[...], sin[...]

    @pl.when(step == 0)
    def _():
        acc[...] = jnp.zeros_like(acc)

    for h in range(heads):
        mine = slice(h * KD, (h + 1) * KD)
        q_out[:, mine] = turned(queries[:, mine], cosine, sine).astype(BF)
        key = (turned(keys[:, mine], cosine, sine) * KD ** (-0.5)).astype(BF)
        k_out[:, mine] = key
        key_end = (key.astype(F32) * end[:, h : h + 1]).astype(BF)
        acc[h] += dot_tn(key_end, values[:, h * VD : (h + 1) * VD])

    @pl.when(step == pl.num_programs(0) - 1)
    def _():
        send_state(docs, acc, sum_out)


def inner_kernel(heads, decay, low, wg, q, k, v, dcol, drow, prow, gate_out, inner_out):
    step = pl.program_id(0)
    gate_out[...] = dot(low[...], wg[...])
    docs_col = dcol[...]

    def turn(j, totals):
        at = pl.ds(pl.multiple_of(j * WIDE, WIDE), WIDE)
        sums = []
        for h in range(heads):
            mine = slice(h * KD, (h + 1) * KD)
            wide = slice(h * VD, (h + 1) * VD)
            factor = tile_decay(decay[h], step * TILE - j * WIDE, docs_col, drow[:, at], prow[:, at])
            weights = (dot_nt(q[:, mine], k[at, mine]) * factor).astype(BF)
            sums.append(totals[h] + dot(weights, v[at, wide]))
        return tuple(sums)

    zeros = tuple(jnp.zeros((TILE, VD), F32) for _ in range(heads))
    totals = lax.fori_loop(0, step * TILE // WIDE + 1, turn, zeros)
    for h in range(heads):
        inner_out[:, h * VD : (h + 1) * VD] = totals[h]


def joined_state(decay, rows, one, two, three, link_two, link_three):
    states = []
    for h in range(one.shape[0]):
        far = jnp.exp(jnp.full((1, 1), rows, F32) * decay[h])
        states.append(
            (
                one[h, :KD].astype(F32)
                + two[h, :KD].astype(F32) * (link_two * far)
                + three[h, :KD].astype(F32) * (link_three * far * far)
            ).astype(BF)
        )
    return states


def doc_in(payload):
    return payload[0, KD : KD + 1, 0:1].astype(F32)


def mix_kernel(
    heads, rows, decay, inner, q, one, two, three, gate, dcol, pcol, wo, group_out, scale_out,
    gated_out, part_out, state_out, carry_out
):
    step = pl.program_id(0)
    before = doc_in(one)

    @pl.when(step == 0)
    def _():
        link_two = (doc_in(two) == before).astype(F32)
        link_three = (doc_in(three) == before).astype(F32)
        states = joined_state(decay, rows, one, two, three, link_two, link_three)
        for h in range(heads):
            state_out[h] = states[h]

    same = (dcol[...].astype(F32) == before).astype(F32)
    place = (step * TILE + 1 + lax.broadcasted_iota(jnp.int32, (TILE, 1), 0)).astype(F32)
    for h in range(heads):
        mine = slice(h * KD, (h + 1) * KD)
        wide = slice(h * VD, (h + 1) * VD)
        carry = same * jnp.exp(place * decay[h])
        carry_out[:, h : h + 1] = carry
        carried = (q[:, mine].astype(F32) * carry).astype(BF)
        mixed = inner[:, wide] + dot(carried, state_out[h])
        mean = jnp.mean(mixed, axis=1, keepdims=True)
        scale = lax.rsqrt(jnp.mean(mixed * mixed, axis=1, keepdims=True) - mean * mean + 1.0)
        grouped = (mixed - mean) * scale
        group_out[:, wide] = grouped
        scale_out[:, h : h + 1] = scale
        gate_h = gate[:, wide]
        gated_out[:, wide] = (pcol[...] * gate_h * jax.nn.sigmoid(gate_h) * grouped).astype(BF)
    part = dot(gated_out[...], wo[...]).astype(BF)
    sides, width = part_out.shape[1], part_out.shape[4]
    for side in range(sides):
        for f in range(2):
            first = (f * sides + side) * width
            part_out[0, side, f] = part[:, first : first + width]


def gate_kernel(heads, grad, wo, gate, group, scale, pcol, dgate_out, mix_out):
    sides = grad.shape[1]
    rows = jnp.concatenate(
        [grad[0, side, f] for f in range(2) for side in range(sides)], axis=1
    )
    passed = dot_nt(rows, wo[...]) * pcol[...]
    for h in range(heads):
        wide = slice(h * VD, (h + 1) * VD)
        gate_h, grouped = gate[:, wide], group[:, wide]
        squash = jax.nn.sigmoid(gate_h)
        upstream = passed[:, wide]
        dgate_out[:, wide] = (
            upstream * grouped * (squash + gate_h * squash * (1.0 - squash))
        ).astype(BF)
        grad_group = upstream * gate_h * squash
        mean = jnp.mean(grad_group, axis=1, keepdims=True)
        cross = jnp.mean(grad_group * grouped, axis=1, keepdims=True)
        mix_out[:, wide] = (scale[:, h : h + 1] * (grad_group - mean - grouped * cross)).astype(BF)


def back_kernel(
    heads, docs, decay, mix, q, k, v, carry, state, dcol, drow, prow, cos, sin, dq_out, dk_out,
    dv_out, sum_out, acc
):
    step = pl.program_id(0)

    @pl.when(step == 0)
    def _():
        acc[...] = jnp.zeros_like(acc)
        dk_out[...] = jnp.zeros_like(dk_out)
        dv_out[...] = jnp.zeros_like(dv_out)

    docs_col = dcol[...]

    def turn(j, totals):
        at = pl.ds(pl.multiple_of(j * WIDE, WIDE), WIDE)
        sums = []
        for h in range(heads):
            mine = slice(h * KD, (h + 1) * KD)
            wide = slice(h * VD, (h + 1) * VD)
            query, grad_mixed, key = q[:, mine], mix[:, wide], k[at, mine]
            factor = tile_decay(decay[h], step * TILE - j * WIDE, docs_col, drow[:, at], prow[:, at])
            weights = (dot_nt(query, key) * factor).astype(BF)
            grads = (dot_nt(grad_mixed, v[at, wide]) * factor).astype(BF)
            dk_out[at, mine] += dot_tn(grads, query)
            dv_out[at, wide] += dot_tn(weights, grad_mixed)
            sums.append(totals[h] + dot(grads, key))
        return tuple(sums)

    zeros = tuple(jnp.zeros((TILE, KD), F32) for _ in range(heads))
    totals = lax.fori_loop(0, step * TILE // WIDE + 1, turn, zeros)
    for h in range(heads):
        mine = slice(h * KD, (h + 1) * KD)
        wide = slice(h * VD, (h + 1) * VD)
        lift = carry[:, h : h + 1]
        total = totals[h] + lift * dot_nt(mix[:, wide], state[h])
        dq_out[:, mine] = turned(total, cos[...], -sin[...]).astype(BF)
        acc[h] += dot_tn((q[:, mine].astype(F32) * lift).astype(BF), mix[:, wide])

    @pl.when(step == pl.num_programs(0) - 1)
    def _():
        send_state(docs, acc, sum_out)


def finish_kernel(
    heads, size, docs, decay, dk_in, dv_in, k, v, end, one, two, three, dq, dgate, wq, wk, wv, wg,
    cos, sin, x, stat, vec, dk_out, dv_out, part_out, rows_out, cols_out, state
):
    step = pl.program_id(0)

    @pl.when(step == 0)
    def _():
        last = docs[0].astype(F32)
        link_two = (doc_in(one) == last).astype(F32)
        link_three = (doc_in(two) == last).astype(F32)
        states = joined_state(decay, size, one, two, three, link_two, link_three)
        for h in range(heads):
            state[h] = states[h]

    cosine, sine = cos[...], -sin[...]
    for h in range(heads):
        mine = slice(h * KD, (h + 1) * KD)
        wide = slice(h * VD, (h + 1) * VD)
        lift = end[:, h : h + 1]
        grad_key = dk_in[:, mine] + lift * dot_nt(v[:, wide], state[h])
        dk_out[:, mine] = (turned(grad_key, cosine, sine) * KD ** (-0.5)).astype(BF)
        key_end = (k[:, mine].astype(F32) * lift).astype(BF)
        dv_out[:, wide] = (dv_in[:, wide] + dot(key_end, state[h])).astype(BF)
    part = (
        dot_nt(dq[...], wq[...])
        + dot_nt(dk_out[...], wk[...])
        + dot_nt(dv_out[...], wv[...])
        + dot_nt(dgate[...], wg[...])
    )
    count, width = part_out.shape[0], part_out.shape[2]
    for shard in range(count):
        part_out[shard] = part[:, shard * width : (shard + 1) * width].astype(BF)
    normed = (lanes(x).astype(F32) - stat[:, 0:1]) * stat[:, 1:2]
    scaled = part * vec[0:1, :]
    ones = jnp.ones((8, scaled.shape[1]), BF)
    rows_out[0, 0:8] = dot_nt(ones, scaled.astype(BF))
    rows_out[0, 8:16] = dot_nt(ones, (scaled * normed).astype(BF))
    sums = jnp.concatenate(
        [jnp.sum(part * normed, axis=0, keepdims=True), jnp.sum(part, axis=0, keepdims=True)],
        axis=0,
    )

    @pl.when(step == 0)
    def _():
        cols_out[...] = jnp.zeros_like(cols_out)

    cols_out[...] += sums


def feed_kernel(
    chunks, x, grads, vec, up_near, up_far, down_near, down_far, ln_out, grad_out, act_out,
    dup_out, part_out, stat_out, rows_out, cols_out, acc
):
    step = pl.program_id(0)
    count = x.shape[1]
    steps = count // TILE

    def at_rows(r):
        return pl.ds(pl.multiple_of(r * TILE, TILE), TILE)

    @pl.when(step == 0)
    def _():
        def start(r, carry):
            at = at_rows(r)
            rows = jnp.concatenate([x[i, at, :] for i in range(x.shape[0])], axis=1).astype(F32)
            mean = jnp.mean(rows, axis=1, keepdims=True)
            scale = lax.rsqrt(jnp.mean(rows * rows, axis=1, keepdims=True) - mean * mean + EPSILON)
            stat_out[at, :] = jnp.concatenate([mean, scale], axis=1)
            ln_out[at, :] = ((rows - mean) * scale * vec[2:3, :] + vec[3:4, :]).astype(BF)
            grad_out[at, :] = jnp.concatenate(
                [grads[i, at, :] for i in range(grads.shape[0])], axis=1
            )
            acc[at, :] = jnp.zeros((TILE, acc.shape[1]), F32)
            return carry

        lax.fori_loop(0, steps, start, 0)

    def units(up, down):
        def turn(r, carry):
            at = at_rows(r)
            lifted = dot(ln_out[at, :], up[...])
            share = 0.5 * (1.0 + lax.erf(lifted * 0.5**0.5))
            act_out[at, :] = (lifted * share).astype(BF)
            slope = share + lifted * jnp.exp(-0.5 * lifted * lifted) * 0.3989422804014327
            lowered = (slope * dot_nt(grad_out[at, :], down[...])).astype(BF)
            dup_out[at, :] = lowered
            acc[at, :] += dot_nt(lowered, up[...])
            return carry

        lax.fori_loop(0, steps, turn, 0)

    @pl.when(step < chunks)
    def _():
        units(up_near, down_near)

    @pl.when(step >= chunks)
    def _():
        units(up_far, down_far)

    @pl.when(step == pl.num_programs(0) - 1)
    def _():
        cols_out[...] = jnp.zeros_like(cols_out)
        sides, width = part_out.shape[1], part_out.shape[3]

        def finish(r, carry):
            at = at_rows(r)
            part = acc[at, :]
            for f in range(2):
                for side in range(sides):
                    first = (f * sides + side) * width
                    part_out[f, side, at, :] = part[:, first : first + width].astype(BF)
            rows = jnp.concatenate([x[i, at, :] for i in range(x.shape[0])], axis=1).astype(F32)
            normed = (rows - stat_out[at, 0:1]) * stat_out[at, 1:2]
            scaled = part * vec[2:3, :]
            ones = jnp.ones((8, scaled.shape[1]), BF)
            rows_out[r, 0:8] = dot_nt(ones, scaled.astype(BF))
            rows_out[r, 8:16] = dot_nt(ones, (scaled * normed).astype(BF))
            cols_out[...] += jnp.concatenate(
                [
                    jnp.sum(part * normed, axis=0, keepdims=True),
                    jnp.sum(part, axis=0, keepdims=True),
                ],
                axis=0,
            )
            return carry

        lax.fori_loop(0, steps, finish, 0)


def branch_kernel(full, mine, keep, other, hidden, grads, gain, stat, near, far, out):
    sums = (near[0] + far[0]) * (1.0 / full)
    one, two = (
        sums[at : at + 8].T[:, 0:1] for at in (0, 8)
    )
    upstream = keep[0, 0].astype(F32) + other[0, 0].astype(F32)
    scale = stat[:, 1:2]
    normed = (hidden[0] - stat[:, 0:1]) * scale
    out[0] = (
        grads[0].astype(F32)
        + scale
        * (upstream * gain[0] - one - normed * two)
    ).astype(BF)


def lower_kernel(act, down_near, down_far, out):
    units = down_near.shape[0]
    part = (dot(act[:, :units], down_near[...]) + dot(act[:, units:], down_far[...])).astype(BF)
    sides, width = out.shape[1], out.shape[3]
    for f in range(2):
        for side in range(sides):
            first = (f * sides + side) * width
            out[f, side] = part[:, first : first + width]


def prefetched(kernel, grid, in_specs, out_specs, outs, flops=0):
    return pl.pallas_call(
        kernel,
        grid_spec=pltpu.PrefetchScalarGridSpec(
            num_scalar_prefetch=1, grid=grid, in_specs=in_specs, out_specs=out_specs
        ),
        out_shape=[jax.ShapeDtypeStruct(shape, dtype) for shape, dtype in outs],
        cost_estimate=pl.CostEstimate(flops=flops, bytes_accessed=0, transcendentals=0),
        compiler_params=pltpu.CompilerParams(vmem_limit_bytes=VMEM_LIMIT),
    )


def bit_value(bit):
    return my_bit("tok", bit)[None].astype(jnp.int32)


def split_source(groups, rows, block):
    per_half = rows // (2 * block)
    count = groups * per_half

    def source(i, mine):
        keeps = (i >= count).astype(jnp.int32)
        half = jnp.where(keeps == 1, mine[0], 1 - mine[0])
        j = i - keeps * count
        return (j // per_half) * (2 * per_half) + half * per_half + j % per_half

    give = lambda i, mine: (jnp.minimum(i, count - 1), 0)
    keep = lambda i, mine: (jnp.maximum(i - count, 0), 0)
    return count, source, give, keep


def weight_kernel(count, mine, left, *refs):
    give, keep = refs[-2:]

    def fill(out):
        first = 0
        for right in refs[:-2]:
            width = right.shape[1]
            out[:, first : first + width] = dot_tn(left[...], right[...]).astype(BF)
            first += width

    @pl.when(pl.program_id(0) < count)
    def _():
        fill(give)

    @pl.when(pl.program_id(0) >= count)
    def _():
        fill(keep)


def weight_grad(bit, groups, left, *rights):
    rows, columns = left.shape
    width = sum(right.shape[1] for right in rights)
    block = min(CHUNK, columns // groups // 2)
    count, source, give, keep = split_source(groups, columns // groups, block)
    half = (columns // 2, width)
    return prefetched(
        partial(weight_kernel, count),
        (2 * count,),
        [pl.BlockSpec((rows, block), lambda i, mine: (0, source(i, mine)))]
        + [
            pl.BlockSpec(right.shape, lambda i, mine: (0, 0), pipeline_mode=pl.Buffered(1))
            for right in rights
        ],
        [pl.BlockSpec((block, width), give), pl.BlockSpec((block, width), keep)],
        [(half, BF), (half, BF)],
        4 * rows * columns * width,
    )(bit_value(bit), left, *rights)


def turned_place(i, order):
    place = 0
    for k, bit in enumerate(order):
        place = place + (((i >> (len(order) - 1 - k)) & 1) << bit)
    return place


def outer_kernel(mine, gated, grad, give, keep):
    part = dot_tn(gated[...], jnp.concatenate([grad[0, 0, 0], grad[1, 0, 0]], axis=0)).astype(BF)
    half = give.shape[0]

    @pl.when(mine[0] == 0)
    def _():
        keep[...] = part[:half]
        give[...] = part[half:]

    @pl.when(mine[0] == 1)
    def _():
        keep[...] = part[half:]
        give[...] = part[:half]


def fold_kernel(count, mine, one, two, give, keep):
    total = (one[...].astype(F32) + two[...].astype(F32)).astype(BF)

    @pl.when(pl.program_id(0) < count)
    def _():
        give[...] = total

    @pl.when(pl.program_id(0) >= count)
    def _():
        keep[...] = total


def fold(bit, groups, one, two):
    rows, columns = one.shape
    block = min(CHUNK // 2, rows // groups // 2)
    count, source, give, keep = split_source(groups, rows // groups, block)
    spec = pl.BlockSpec((block, columns), lambda i, mine: (source(i, mine), 0))
    half = (rows // 2, columns)
    return prefetched(
        partial(fold_kernel, count),
        (2 * count,),
        [spec, spec],
        [pl.BlockSpec((block, columns), give), pl.BlockSpec((block, columns), keep)],
        [(half, BF), (half, BF)],
    )(bit_value(bit), one, two)


def scatter_rest(give, keep, order, groups=1, waits=None):
    values, others = [], []
    for place, bit in enumerate(order):
        if waits and place in waits:
            give = after(give, *waits[place])
        other = swapped(give, "tok", 1 << bit)
        if waits and ("seen", place) in waits:
            other = after(other, *waits["seen", place])
        others.append(other)
        if place + 1 < len(order):
            give, keep = fold(order[place + 1], groups, keep, other)
            values.append(give)
        else:
            values.append((keep, other))
    return values, others


def total(pair):
    return pair[0].astype(F32) + pair[1].astype(F32)


def spread_kernel(per_half, mine, near, other, out):
    here = pl.program_id(0) // per_half == mine[0]

    @pl.when(here)
    def _():
        out[...] = near[...].astype(out.dtype)

    @pl.when(jnp.logical_not(here))
    def _():
        out[...] = other[...].astype(out.dtype)


def gather_one(value, bit):
    return joined(value, swapped(value, "tok", 1 << bit), my_bit("tok", bit) == 0, 0)


def gather_wide(value, order):
    for bit in order[:0:-1]:
        value = gather_one(value, bit)
    bit = order[0]
    other = swapped(value, "tok", 1 << bit)
    rows, columns = value.shape
    block = min(CHUNK // 2, rows)
    per_half = rows // block

    def spec(mirror):
        def index(i, mine):
            half = 1 - mine[0] if mirror else mine[0]
            return (jnp.clip(i - half * per_half, 0, per_half - 1), 0)

        return pl.BlockSpec((block, columns), index)

    return prefetched(
        partial(spread_kernel, per_half),
        (2 * per_half,),
        [spec(False), spec(True)],
        [pl.BlockSpec((block, columns), lambda i, mine: (i, 0))],
        [((2 * rows, columns), F32)],
    )(bit_value(bit), value, other)[0], value


def order_kernel(plan, *refs):
    outs = list(refs[len(plan) :])
    for part, count in zip(refs, plan, strict=False):
        if count == 1:
            out = outs.pop(0)
            rows, columns = out.shape[0], part.shape[2]
            for i in range(part.shape[1] // rows):
                at = slice(i * columns, (i + 1) * columns)
                out[:, at] = part[0, i * rows : (i + 1) * rows].astype(F32)
            continue
        first = 0
        for _ in range(count):
            out = outs.pop(0)
            out[...] = part[0, :, first : first + out.shape[1]].astype(F32)
            first += out.shape[1]


def packed_pieces(first, *others):
    columns = others[0].shape[1]
    parts = [first[:, i : i + columns] for i in range(0, first.shape[1], columns)]
    return jnp.concatenate([*parts, *others], axis=0)


def in_order(pieces, plan):
    count, rows, columns = pieces.shape
    part = rows // len(plan)

    def spec(which, order):
        return pl.BlockSpec(
            (1, part, columns), lambda i: (turned_place(i, order), which, 0)
        )

    shapes = [shape for _, parts in plan for shape in parts]
    return pl.pallas_call(
        partial(order_kernel, [len(parts) for _, parts in plan]),
        grid=(count,),
        in_specs=[spec(which, order) for which, (order, _) in enumerate(plan)],
        out_specs=[pl.BlockSpec(shape, lambda i: (i, 0)) for shape in shapes],
        out_shape=[jax.ShapeDtypeStruct((count * high, wide), F32) for high, wide in shapes],
        cost_estimate=pl.CostEstimate(flops=0, bytes_accessed=0, transcendentals=0),
        compiler_params=pltpu.CompilerParams(vmem_limit_bytes=VMEM_LIMIT),
    )(*[pieces] * len(plan))


def body(
    tokens,
    mix_gain,
    mix_bias,
    query_weight,
    key_weight,
    value_weight,
    gate_weight,
    output_weight,
    feed_gain,
    feed_bias,
    up_weight,
    down_weight,
    doc_ids,
    pad_mask,
    out_grad,
):
    row_count, width = tokens.shape
    heads_here = query_weight.shape[1] // KD
    shards = lax.axis_size("head")
    full_width = width * shards
    sides = shards // 2
    spread = lax.axis_index("head") // sides
    side = lax.axis_index("head") % sides
    half_rows = row_count // 2
    block = lax.axis_index("tok")

    packed = pl.pallas_call(
        entry_kernel,
        out_shape=jax.ShapeDtypeStruct((row_count + EXTRA, width), BF),
        compiler_params=pltpu.CompilerParams(vmem_limit_bytes=VMEM_LIMIT),
    )(tokens, mix_gain[None], mix_bias[None], feed_gain[None], feed_bias[None])
    rows_raw = lax.all_gather(packed, "head", axis=0)
    vector_rows = rows_raw[:, row_count:, :].astype(F32)
    vectors = (vector_rows[:, 0:12:3] + vector_rows[:, 1:12:3] + vector_rows[:, 2:12:3]).transpose(
        1, 0, 2
    )
    side_vectors = lax.dynamic_index_in_dim(
        vectors.reshape(4, 2, sides, width), side, 2, keepdims=False
    )
    vectors = vectors.reshape(4, full_width)

    order_one, order_two = bit_orders()
    first_head = lax.axis_index("head") * heads_here
    log_decay = jnp.log(
        1.0 - 2.0 ** (-5.0 - (first_head + jnp.arange(heads_here, dtype=jnp.int32)).astype(F32))
    )
    position = jnp.arange(row_count, dtype=jnp.int32)
    frequency = 10000.0 ** (-2.0 * jnp.arange(KD // 2, dtype=jnp.int32).astype(F32) / KD)
    angles = (block * row_count + position).astype(F32)[:, None] * frequency[None, :]
    cosine, sine = jnp.cos(angles), jnp.sin(angles)
    padding = pad_mask.astype(F32)
    last_doc = doc_ids[row_count - 1]

    end_factor = (padding * (doc_ids == last_doc).astype(F32))[:, None] * jnp.exp(
        (row_count - 1 - position).astype(F32)[:, None] * log_decay[None, :]
    )

    late_grad = after(out_grad, rows_raw, cosine, sine, end_factor)
    grad_keep, grad_give = halves(late_grad, "head", shards.bit_length() - 2, 0)
    grad_seen = swapped(grad_give, "head", sides)
    up_piece, down_piece = own_piece(up_weight, order_one), own_piece(down_weight, order_two)
    both_pieces = jnp.concatenate([up_piece, down_piece.reshape(up_piece.shape)], axis=0)

    docs_col, docs_row = doc_ids[:, None], doc_ids[None, :]
    pads_col, pads_row = padding[:, None], padding[None, :]
    inner_width, value_width = heads_here * KD, heads_here * VD
    states = pltpu.VMEM((heads_here, KD, VD), F32)
    state_shape = (heads_here, KD, VD)
    sent_shape = (heads_here, KD + EXTRA, VD)
    shard_tiles = pl.BlockSpec((shards, TILE, width), lambda i: (0, i, 0))
    per_half = half_rows // TILE
    split_tiles = pl.BlockSpec(
        (1, sides, 2, TILE, width), lambda i: (i // per_half, 0, 0, i % per_half, 0)
    )
    last_docs = doc_ids[row_count - 1 :]
    rows_first, query_rot, key_rot, values, stats, summary = call(
        partial(project_kernel, heads_here),
        row_count,
        [
            SCALARS,
            shard_tiles,
            pl.BlockSpec((shards, EXTRA, width), lambda i: (0, row_count // EXTRA, 0)),
            whole(full_width, inner_width),
            whole(full_width, inner_width),
            whole(full_width, value_width),
            tiles(KD // 2),
            tiles(KD // 2),
            tiles(heads_here),
        ],
        [
            ((row_count, full_width), BF),
            ((row_count, inner_width), BF),
            ((row_count, inner_width), BF),
            ((row_count, value_width), BF),
            ((row_count, 2), F32),
            (sent_shape, BF),
        ],
        [
            tiles(full_width),
            tiles(inner_width),
            tiles(inner_width),
            tiles(value_width),
            tiles(2),
            held(*sent_shape),
        ],
        [states],
    )(
        last_docs,
        rows_raw,
        rows_raw,
        query_weight,
        key_weight,
        value_weight,
        cosine,
        sine,
        end_factor,
    )
    one_back, two_back, three_back = (shifted(summary, by) for by in (1, 2, 3))
    grad_seen = after(grad_seen, summary)
    side_grads = joined(grad_keep[None], grad_seen[None], spread == 0, 0)
    grad_rows, grads_last = gather_side(side_grads[:, None])
    grad_rows = grad_rows.reshape(shards, half_rows, width)
    (both_seen,) = far_swap(after(both_pieces, grad_seen))
    up_seen = both_seen[: up_piece.shape[0]]
    down_seen = both_seen[up_piece.shape[0] :].reshape(down_piece.shape)
    up_other = gather_back(up_seen, order_one)
    down_other = gather_back(down_seen, order_two)
    gate_pre, inner_part = call(
        partial(inner_kernel, heads_here),
        row_count,
        [
            SCALARS,
            tiles(full_width),
            whole(full_width, value_width),
            tiles(inner_width),
            whole(row_count, inner_width),
            whole(row_count, value_width),
            tiles(1),
            whole(1, row_count),
            whole(1, row_count),
        ],
        [((row_count, value_width), F32)] * 2,
        [tiles(value_width)] * 2,
    )(
        after(log_decay, side_grads),
        rows_first,
        gate_weight,
        query_rot,
        key_rot,
        values,
        docs_col,
        docs_row,
        pads_row,
    )
    flat_group, group_scale, gated, mix_part, state_low, carry_factor = call(
        partial(mix_kernel, heads_here, row_count),
        row_count,
        [
            SCALARS,
            tiles(value_width),
            tiles(inner_width),
            whole(*sent_shape),
            whole(*sent_shape),
            whole(*sent_shape),
            tiles(value_width),
            tiles(1),
            tiles(1),
            whole(value_width, full_width),
        ],
        [
            ((row_count, value_width), F32),
            ((row_count, heads_here), F32),
            ((row_count, value_width), BF),
            ((2, sides, 2, half_rows, width), BF),
            (state_shape, BF),
            ((row_count, heads_here), F32),
        ],
        [
            tiles(value_width),
            tiles(heads_here),
            tiles(value_width),
            split_tiles,
            held(*state_shape),
            tiles(heads_here),
        ],
    )(
        log_decay,
        inner_part,
        query_rot,
        one_back,
        two_back,
        three_back,
        gate_pre,
        docs_col,
        pads_col,
        output_weight,
    )
    mix_part = after(mix_part, grads_last, both_seen)
    side_tokens = lax.dynamic_index_in_dim(
        lax.dynamic_slice_in_dim(rows_raw, spread * half_rows, half_rows, axis=1).reshape(
            2, sides, half_rows, width
        ),
        side,
        1,
        keepdims=False,
    )
    mixed_sum = lax.psum_scatter(
        mix_part.reshape(shards, 2, half_rows, width), "head", scatter_dimension=0
    )
    hidden = lax.optimization_barrier(side_tokens.astype(F32) + mixed_sum.astype(F32))
    hidden_rows = gather_side(hidden.astype(BF)[:, None])[0].reshape(shards, half_rows, width)
    units = up_weight.shape[1]
    chunks = units // CHUNK
    rows_second, grad_plain, act_low, grad_up, feed_part, stats_second, row_second, cols_second = (
        pl.pallas_call(
            partial(feed_kernel, chunks),
            grid=(2 * chunks,),
            in_specs=[
                whole(shards, half_rows, width),
                whole(shards, half_rows, width),
                whole(4, full_width),
                pl.BlockSpec((full_width, CHUNK), lambda i: (0, jnp.minimum(i, chunks - 1))),
                pl.BlockSpec((full_width, CHUNK), lambda i: (0, jnp.maximum(i - chunks, 0))),
                pl.BlockSpec((CHUNK, full_width), lambda i: (jnp.minimum(i, chunks - 1), 0)),
                pl.BlockSpec((CHUNK, full_width), lambda i: (jnp.maximum(i - chunks, 0), 0)),
            ],
            out_specs=[
                held(half_rows, full_width),
                held(half_rows, full_width),
                pl.BlockSpec((half_rows, CHUNK), lambda i: (0, i)),
                pl.BlockSpec((half_rows, CHUNK), lambda i: (0, i)),
                held(2, sides, half_rows, width),
                held(half_rows, 2),
                held(half_rows // TILE, 16, TILE),
                held(2, full_width),
            ],
            out_shape=[
                jax.ShapeDtypeStruct((half_rows, full_width), BF),
                jax.ShapeDtypeStruct((half_rows, full_width), BF),
                jax.ShapeDtypeStruct((half_rows, 2 * units), BF),
                jax.ShapeDtypeStruct((half_rows, 2 * units), BF),
                jax.ShapeDtypeStruct((2, sides, half_rows, width), BF),
                jax.ShapeDtypeStruct((half_rows, 2), F32),
                jax.ShapeDtypeStruct((half_rows // TILE, 16, TILE), F32),
                jax.ShapeDtypeStruct((2, full_width), F32),
            ],
            scratch_shapes=[pltpu.VMEM((half_rows, full_width), F32)],
            cost_estimate=pl.CostEstimate(flops=0, bytes_accessed=0, transcendentals=0),
            compiler_params=pltpu.CompilerParams(vmem_limit_bytes=VMEM_LIMIT),
        )(hidden_rows, grad_rows, vectors, up_weight, up_other, down_weight, down_other)
    )
    feed_value, feed_seen = scatter_side_start(feed_part)
    for bit in list(side_bits())[:0:-1]:
        row_second = row_second + swapped(row_second, "head", 1 << bit)
    row_seen = swapped(row_second, "head", 1)
    down_give, down_keep = weight_grad(order_one[0], 2, act_low, grad_plain)
    up_give, up_keep = weight_grad(order_two[0], 1, rows_second, grad_up)
    row_seen = after(row_seen, down_give, up_give)
    half_block = pl.BlockSpec((1, TILE, width), lambda f, i, mine: (f, i, 0))
    row_block = pl.BlockSpec((TILE, 2), lambda f, i, mine: (i, 0))
    sum_block = pl.BlockSpec((1, 16, TILE), lambda f, i, mine: (i, 0, 0))
    (branch,) = prefetched(
        partial(branch_kernel, full_width),
        (2, half_rows // TILE),
        [
            pl.BlockSpec((1, 1, TILE, width), lambda f, i, mine: (f, mine[0], i, 0)),
            pl.BlockSpec((1, 1, TILE, width), lambda f, i, mine: (f, 0, i, 0)),
            half_block,
            half_block,
            pl.BlockSpec((1, 1, width), lambda f, i, mine: (f, 0, 0)),
            row_block,
            sum_block,
            sum_block,
        ],
        [half_block],
        [((2, half_rows, width), BF)],
    )(
        my_bit("head", 0)[None].astype(jnp.int32),
        feed_value,
        feed_seen[:, None] if feed_seen.ndim == 3 else feed_seen,
        hidden,
        side_grads,
        side_vectors[2][:, None, :],
        stats_second,
        row_second,
        row_seen,
    )
    grad_branch = lax.all_gather(branch, "head", axis=0).reshape(
        2, sides, 2, half_rows, width
    )

    down_part = pl.pallas_call(
        lower_kernel,
        grid=(half_rows // TILE,),
        in_specs=[tiles(2 * units), whole(units, full_width), whole(units, full_width)],
        out_specs=pl.BlockSpec((2, sides, TILE, width), lambda i: (0, 0, i, 0)),
        out_shape=jax.ShapeDtypeStruct((2, sides, half_rows, width), BF),
        cost_estimate=pl.CostEstimate(flops=0, bytes_accessed=0, transcendentals=0),
        compiler_params=pltpu.CompilerParams(vmem_limit_bytes=VMEM_LIMIT),
    )(after(act_low, branch), down_weight, down_other)

    down_sum, down_seen_all = scatter_rest(
        down_give, down_keep, order_one, 2, {0: (branch,), ("seen", 1): (down_part,)}
    )
    up_sum, up_seen_all = scatter_rest(
        up_give, up_keep, order_two, 1, {0: (branch,), ("seen", 1): (down_part,)}
    )

    dgate, grad_mixed = call(
        partial(gate_kernel, heads_here),
        row_count,
        [
            split_tiles,
            whole(value_width, full_width),
            tiles(value_width),
            tiles(value_width),
            tiles(heads_here),
            tiles(1),
        ],
        [((row_count, value_width), BF), ((row_count, value_width), BF)],
        [tiles(value_width), tiles(value_width)],
    )(
        grad_branch,
        output_weight,
        gate_pre,
        flat_group,
        group_scale,
        after(pads_col, down_sum[1], up_sum[1]),
    )
    half_down = down_sum[-1][0].shape[0] // 2
    up_pair = lax.optimization_barrier((*up_sum[-1], dgate))[:2]
    down_pair = lax.optimization_barrier((*down_sum[-1], dgate))[:2]
    up_give = total([part[:, units:] for part in up_pair]).astype(BF)
    down_give = total([part[half_down:] for part in down_pair]).astype(BF)
    dq, dk_part, dv_part, grad_state = call(
        partial(back_kernel, heads_here),
        row_count,
        [
            SCALARS,
            SCALARS,
            tiles(value_width),
            tiles(inner_width),
            whole(row_count, inner_width),
            whole(row_count, value_width),
            tiles(heads_here),
            whole(*state_shape),
            tiles(1),
            whole(1, row_count),
            whole(1, row_count),
            tiles(KD // 2),
            tiles(KD // 2),
        ],
        [
            ((row_count, inner_width), BF),
            ((row_count, inner_width), F32),
            ((row_count, value_width), F32),
            (sent_shape, BF),
        ],
        [
            tiles(inner_width),
            held(row_count, inner_width),
            held(row_count, value_width),
            held(*sent_shape),
        ],
        [states],
        10 * row_count * full_width * value_width,
    )(
        last_docs,
        after(log_decay, down_part, up_give, down_give),
        grad_mixed,
        query_rot,
        key_rot,
        values,
        carry_factor,
        state_low,
        docs_col,
        docs_row,
        pads_row,
        cosine,
        sine,
    )
    width_out = (value_width // 2, full_width)
    outw_give, outw_keep = prefetched(
        outer_kernel,
        (shards,),
        [
            pl.BlockSpec(
                (row_count, value_width), lambda i, mine: (0, 0), pipeline_mode=pl.Buffered(1)
            ),
            pl.BlockSpec(
                (2, 1, 1, half_rows, width), lambda i, mine: (0, i % sides, i // sides, 0, 0)
            ),
        ],
        [pl.BlockSpec((value_width // 2, width), lambda i, mine: (0, i))] * 2,
        [(width_out, BF), (width_out, BF)],
        4 * row_count * value_width * full_width,
    )(bit_value(order_one[0]), after(gated, dq, up_give, down_give), grad_branch)
    outw_sum, outw_seen = scatter_rest(outw_give, outw_keep, order_one)
    gw_give, gw_keep = weight_grad(order_two[0], 1, rows_first, after(dgate, dq))
    gw_sum, gw_seen = scatter_rest(gw_give, gw_keep, order_two)
    one_on, two_on, three_on = (shifted(grad_state, -by) for by in (1, 2, 3))
    up_far, down_far = far_swap(up_give, down_give)
    up_far, down_far = after(up_far, gw_give, outw_give), after(down_far, gw_give, outw_give)
    up_near = total([part[:, :units] for part in up_pair]) + up_far.astype(F32)
    down_near = total([part[:half_down] for part in down_pair]) + down_far.astype(F32)
    down_low, up_low = down_near.astype(BF), up_near.astype(BF)
    feed_pieces = after(packed_pieces(down_low, up_low), one_on, two_on, three_on)
    feed_pieces = lax.all_gather(feed_pieces, "tok", axis=0)
    grad_down, grad_upw = in_order(
        feed_pieces, ((order_one, [down_low.shape]), (order_two, [up_low.shape]))
    )
    dk, dv, last_part, row_sums, column_first = call(
        partial(finish_kernel, heads_here, row_count),
        row_count,
        [
            SCALARS,
            SCALARS,
            tiles(inner_width),
            tiles(value_width),
            tiles(inner_width),
            tiles(value_width),
            tiles(heads_here),
            whole(*sent_shape),
            whole(*sent_shape),
            whole(*sent_shape),
            tiles(inner_width),
            tiles(value_width),
            whole(full_width, inner_width),
            whole(full_width, inner_width),
            whole(full_width, value_width),
            whole(full_width, value_width),
            tiles(KD // 2),
            tiles(KD // 2),
            shard_tiles,
            tiles(2),
            whole(4, full_width),
        ],
        [
            ((row_count, inner_width), BF),
            ((row_count, value_width), BF),
            ((shards, row_count + EXTRA, width), BF),
            ((row_count // TILE, 16, TILE), F32),
            ((2, full_width), F32),
        ],
        [
            tiles(inner_width),
            tiles(value_width),
            shard_tiles,
            pl.BlockSpec((1, 16, TILE), lambda i: (i, 0, 0)),
            held(2, full_width),
        ],
        [pltpu.VMEM(state_shape, BF)],
        12 * row_count * full_width * value_width,
    )(
        last_docs,
        after(log_decay, up_near, down_near),
        dk_part,
        dv_part,
        key_rot,
        values,
        end_factor,
        one_on,
        two_on,
        three_on,
        dq,
        dgate,
        query_weight,
        key_weight,
        value_weight,
        gate_weight,
        cosine,
        sine,
        rows_raw,
        stats,
        vectors,
    )
    count = row_count // TILE
    line = jnp.concatenate([row_sums[:, 0], row_sums[:, 8]], axis=0)
    line = jnp.pad(line, ((0, EXTRA - 2 * count - 4), (0, width - TILE)))
    columns = jnp.concatenate([column_first, cols_second]).reshape(4, shards, width)
    extra = jnp.concatenate(
        [jnp.broadcast_to(line[None], (shards, *line.shape)), columns.transpose(1, 0, 2)], axis=1
    )
    last_part = lax.dynamic_update_slice_in_dim(last_part, extra.astype(BF), row_count, axis=1)
    vw_give, vw_keep = weight_grad(order_one[0], 1, rows_first, dv)
    qkw_give, qkw_keep = weight_grad(order_two[0], 1, rows_first, dq, dk)
    last_part = after(last_part, feed_pieces, vw_give, qkw_give, outw_sum[0], gw_seen[0])
    last_sum = lax.psum_scatter(last_part, "head", scatter_dimension=0).astype(F32)
    grad_ln1 = last_sum[:row_count]
    sums_first = last_sum[row_count:, :TILE] / full_width
    sums_first = jnp.stack(
        [sums_first[:count].reshape(row_count), sums_first[count : 2 * count].reshape(row_count)],
        axis=1,
    )
    columns = lax.psum(last_sum[row_count + EXTRA - 4 :], "tok")
    result = (hidden + scatter_side(after(down_part, last_sum))).astype(BF)
    result_keep = lax.dynamic_index_in_dim(result, spread, 0, keepdims=False)
    result_give = lax.dynamic_index_in_dim(result, 1 - spread, 0, keepdims=False)
    layer_out = joined(result_keep, swapped(result_give, "head", sides), spread == 0, 0)

    outw_low, gw_low = total(outw_sum[-1]).astype(BF), total(gw_sum[-1]).astype(BF)
    waits = {1: (gw_sum[0],), 2: (outw_sum[1], gw_sum[1])}
    vw_sum, _ = scatter_rest(vw_give, vw_keep, order_one, 1, waits)
    qkw_sum, _ = scatter_rest(qkw_give, qkw_keep, order_two, 1, waits)
    vw_low, qkw_low = total(vw_sum[-1]).astype(BF), total(qkw_sum[-1]).astype(BF)
    pieces = packed_pieces(outw_low, gw_low, vw_low, qkw_low)
    pieces = lax.all_gather(pieces, "tok", axis=0)
    high = qkw_low.shape[0]
    grad_outw, grad_gw, grad_vw, grad_qw, grad_kw = in_order(
        pieces,
        (
            (order_one, [outw_low.shape]),
            (order_two, [gw_low.shape]),
            (order_one, [vw_low.shape]),
            (order_two, [(high, inner_width), (high, inner_width)]),
        ),
    )

    norm_first = (tokens.astype(F32) - stats[:, 0:1]) * stats[:, 1:2]
    branch_rows = lax.dynamic_index_in_dim(
        lax.dynamic_index_in_dim(grad_branch, side, 1, keepdims=False), spread, 1, keepdims=False
    ).reshape(row_count, width)
    tokens_grad = branch_rows.astype(F32) + stats[:, 1:2] * (
        grad_ln1 * mix_gain - sums_first[:, 0:1] - norm_first * sums_first[:, 1:2]
    )
    return (
        layer_out,
        tokens_grad,
        columns[0],
        columns[1],
        grad_qw,
        grad_kw,
        grad_vw,
        grad_gw,
        grad_outw,
        columns[2],
        columns[3],
        grad_upw,
        grad_down,
    )


def solution(mesh):
    rows = P("tok", "head")
    columns = P(None, "head")
    return jax.shard_map(
        body,
        mesh=mesh,
        in_specs=(
            rows,
            P("head"),
            P("head"),
            columns,
            columns,
            columns,
            columns,
            P("head", None),
            P("head"),
            P("head"),
            columns,
            P("head", None),
            P("tok"),
            P("tok"),
            rows,
        ),
        out_specs=(
            rows,
            rows,
            P("head"),
            P("head"),
            columns,
            columns,
            columns,
            columns,
            P("head", None),
            P("head"),
            P("head"),
            columns,
            P("head", None),
        ),
        check_vma=False,
    )
```

```python
from functools import partial

import jax
import jax.numpy as jnp
from jax import lax
from jax.experimental import pallas as pl
from jax.experimental.pallas import tpu as pltpu
from jax.sharding import PartitionSpec as P

KD = 256
VD = 512
EPSILON = 1e-05
BF = jnp.bfloat16
F32 = jnp.float32


def after(value, *others):
    return lax.optimization_barrier((value, *others))[0]


def shifted(value, by):
    length = lax.axis_size("tok")
    pairs = [(i, i + by) for i in range(length) if 0 <= i + by < length]
    return lax.ppermute(value, "tok", pairs)


def swapped(value, axis, mask):
    return lax.ppermute(value, axis, [(i, i ^ mask) for i in range(lax.axis_size(axis))])


def my_bit(axis, bit):
    return (lax.axis_index(axis) >> bit) & 1


def joined(value, other, first, axis):
    return jnp.where(
        first,
        jnp.concatenate([value, other], axis=axis),
        jnp.concatenate([other, value], axis=axis),
    )


def bit_orders():
    bits = lax.axis_size("tok").bit_length() - 1
    first = list(range(bits))
    second = [0, 2, 1] if bits == 3 else first[bits // 2 :] + first[: bits // 2]
    return first, second


def halves(value, axis, bit, dim):
    shape = value.shape
    pieces = value.reshape(*shape[:dim], 2, shape[dim] // 2, *shape[dim + 1 :])
    mine = my_bit(axis, bit)
    keep = lax.dynamic_index_in_dim(pieces, mine, dim, keepdims=False)
    give = lax.dynamic_index_in_dim(pieces, 1 - mine, dim, keepdims=False)
    return keep, give


def own_piece(value, order, dim=0):
    for bit in order:
        value = halves(value, "tok", bit, dim)[0]
    return value


def gather_back(value, order):
    for bit in order[::-1]:
        other = swapped(value, "tok", 1 << bit)
        value = joined(value, other, my_bit("tok", bit) == 0, 0)
    return value


def far_swap(*values):
    return [swapped(value, "head", lax.axis_size("head") // 2) for value in values]


def side_bits():
    return range(lax.axis_size("head").bit_length() - 2)


def gather_side(value):
    for bit in side_bits():
        other = swapped(value, "head", 1 << bit)
        value = joined(value, other, my_bit("head", bit) == 0, 1)
    return value, other


def scatter_side_start(value):
    for bit in list(side_bits())[:0:-1]:
        keep, give = halves(value, "head", bit, 1)
        value = keep.astype(F32) + swapped(give.astype(BF), "head", 1 << bit).astype(F32)
    give = halves(value, "head", 0, 1)[1]
    return value, swapped(give.astype(BF), "head", 1)


def scatter_side(value):
    for bit in list(side_bits())[::-1]:
        keep, give = halves(value, "head", bit, 1)
        value = keep.astype(F32) + swapped(give.astype(BF), "head", 1 << bit).astype(F32)
    return value[:, 0]


def sum_side(value):
    for bit in side_bits():
        value = value + swapped(value, "head", 1 << bit)
    return value


TILE = 256
EXTRA = 16
CHUNK = 512
WIDE = 512
VMEM_LIMIT = 58 << 20


def dot(left, right):
    return jnp.dot(left, right, preferred_element_type=F32)


def dot_nt(left, right):
    return lax.dot_general(left, right, (((1,), (1,)), ((), ())), preferred_element_type=F32)


def dot_tn(left, right):
    return lax.dot_general(left, right, (((0,), (0,)), ((), ())), preferred_element_type=F32)


def tiles(columns):
    return pl.BlockSpec((TILE, columns), lambda i: (i, 0))


def whole(*shape):
    zeros = (0,) * len(shape)
    return pl.BlockSpec(shape, lambda i: zeros, pipeline_mode=pl.Buffered(1))


def held(*shape):
    zeros = (0,) * len(shape)
    return pl.BlockSpec(shape, lambda i: zeros)


SCALARS = pl.BlockSpec(memory_space=pltpu.SMEM)


def call(kernel, rows, in_specs, outs, out_specs, scratch=(), flops=0):
    return pl.pallas_call(
        kernel,
        grid=(rows // TILE,),
        in_specs=in_specs,
        out_specs=out_specs,
        out_shape=[jax.ShapeDtypeStruct(shape, dtype) for shape, dtype in outs],
        scratch_shapes=list(scratch),
        cost_estimate=pl.CostEstimate(flops=flops, bytes_accessed=0, transcendentals=0),
        compiler_params=pltpu.CompilerParams(vmem_limit_bytes=VMEM_LIMIT),
    )


def turned(value, cosine, sine):
    half_dim = KD // 2
    front, back = value[:, :half_dim], value[:, half_dim:]
    return jnp.concatenate([front * cosine - back * sine, back * cosine + front * sine], axis=1)


def tile_decay(log_decay, behind, docs_col, docs_row, pads_row):
    rows = lax.broadcasted_iota(jnp.int32, (TILE, 1), 0)
    cols = lax.broadcasted_iota(jnp.int32, (1, WIDE), 1)
    allowed = (docs_col == docs_row) & (rows + behind >= cols) & (pads_row > 0)
    rise = jnp.exp(rows.astype(F32) * log_decay)
    fall = jnp.exp((behind - cols).astype(F32) * log_decay)
    return jnp.where(allowed, rise * fall, 0.0)


def send_state(docs, acc, sum_out):
    sum_out[:, :KD, :] = acc[...].astype(BF)
    sum_out[:, KD:, :] = jnp.full((acc.shape[0], EXTRA, VD), docs[0].astype(F32), F32).astype(BF)


def lanes(shards):
    return jnp.concatenate([shards[i] for i in range(shards.shape[0])], axis=1)


def vector_of(rows, index):
    return rows[3 * index : 3 * index + 1] + rows[3 * index + 1 : 3 * index + 2] + rows[
        3 * index + 2 : 3 * index + 3
    ]


def entry_kernel(x, one, two, three, four, out):
    rows = x.shape[0]
    out[:rows] = x[...]
    pieces = []
    for vector in (one, two, three, four):
        value = vector[...]
        for _ in range(3):
            piece = value.astype(BF)
            pieces.append(piece.astype(F32))
            value = value - piece.astype(F32)
    pieces.append(jnp.zeros((EXTRA - len(pieces), x.shape[1]), F32))
    out[rows:] = jnp.concatenate(pieces, axis=0).astype(BF)


def project_kernel(
    heads, docs, x, vec, wq, wk, wv, cos, sin, end, ln_out, q_out, k_out, v_out, stat_out,
    sum_out, acc
):
    step = pl.program_id(0)
    rows = lanes(x).astype(F32)
    vectors = lanes(vec).astype(F32)
    mean = jnp.mean(rows, axis=1, keepdims=True)
    scale = lax.rsqrt(jnp.mean(rows * rows, axis=1, keepdims=True) - mean * mean + EPSILON)
    low = ((rows - mean) * scale * vector_of(vectors, 0) + vector_of(vectors, 1)).astype(BF)
    ln_out[...] = low
    stat_out[...] = jnp.concatenate([mean, scale], axis=1)
    values = dot(low, wv[...]).astype(BF)
    v_out[...] = values
    queries = dot(low, wq[...])
    keys = dot(low, wk[...])
    cosine, sine = cos[...], sin[...]

    @pl.when(step == 0)
    def _():
        acc[...] = jnp.zeros_like(acc)

    for h in range(heads):
        mine = slice(h * KD, (h + 1) * KD)
        q_out[:, mine] = turned(queries[:, mine], cosine, sine).astype(BF)
        key = (turned(keys[:, mine], cosine, sine) * KD ** (-0.5)).astype(BF)
        k_out[:, mine] = key
        key_end = (key.astype(F32) * end[:, h : h + 1]).astype(BF)
        acc[h] += dot_tn(key_end, values[:, h * VD : (h + 1) * VD])

    @pl.when(step == pl.num_programs(0) - 1)
    def _():
        send_state(docs, acc, sum_out)


def inner_kernel(heads, decay, low, wg, q, k, v, dcol, drow, prow, gate_out, inner_out):
    step = pl.program_id(0)
    gate_out[...] = dot(low[...], wg[...])
    docs_col = dcol[...]

    def turn(j, totals):
        at = pl.ds(pl.multiple_of(j * WIDE, WIDE), WIDE)
        sums = []
        for h in range(heads):
            mine = slice(h * KD, (h + 1) * KD)
            wide = slice(h * VD, (h + 1) * VD)
            factor = tile_decay(decay[h], step * TILE - j * WIDE, docs_col, drow[:, at], prow[:, at])
            weights = (dot_nt(q[:, mine], k[at, mine]) * factor).astype(BF)
            sums.append(totals[h] + dot(weights, v[at, wide]))
        return tuple(sums)

    zeros = tuple(jnp.zeros((TILE, VD), F32) for _ in range(heads))
    totals = lax.fori_loop(0, step * TILE // WIDE + 1, turn, zeros)
    for h in range(heads):
        inner_out[:, h * VD : (h + 1) * VD] = totals[h]


def joined_state(decay, rows, one, two, three, link_two, link_three):
    states = []
    for h in range(one.shape[0]):
        far = jnp.exp(jnp.full((1, 1), rows, F32) * decay[h])
        states.append(
            (
                one[h, :KD].astype(F32)
                + two[h, :KD].astype(F32) * (link_two * far)
                + three[h, :KD].astype(F32) * (link_three * far * far)
            ).astype(BF)
        )
    return states


def doc_in(payload):
    return payload[0, KD : KD + 1, 0:1].astype(F32)


def mix_kernel(
    heads, rows, decay, inner, q, one, two, three, gate, dcol, pcol, wo, group_out, scale_out,
    gated_out, part_out, state_out, carry_out
):
    step = pl.program_id(0)
    before = doc_in(one)

    @pl.when(step == 0)
    def _():
        link_two = (doc_in(two) == before).astype(F32)
        link_three = (doc_in(three) == before).astype(F32)
        states = joined_state(decay, rows, one, two, three, link_two, link_three)
        for h in range(heads):
            state_out[h] = states[h]

    same = (dcol[...].astype(F32) == before).astype(F32)
    place = (step * TILE + 1 + lax.broadcasted_iota(jnp.int32, (TILE, 1), 0)).astype(F32)
    for h in range(heads):
        mine = slice(h * KD, (h + 1) * KD)
        wide = slice(h * VD, (h + 1) * VD)
        carry = same * jnp.exp(place * decay[h])
        carry_out[:, h : h + 1] = carry
        carried = (q[:, mine].astype(F32) * carry).astype(BF)
        mixed = inner[:, wide] + dot(carried, state_out[h])
        mean = jnp.mean(mixed, axis=1, keepdims=True)
        scale = lax.rsqrt(jnp.mean(mixed * mixed, axis=1, keepdims=True) - mean * mean + 1.0)
        grouped = (mixed - mean) * scale
        group_out[:, wide] = grouped
        scale_out[:, h : h + 1] = scale
        gate_h = gate[:, wide]
        gated_out[:, wide] = (pcol[...] * gate_h * jax.nn.sigmoid(gate_h) * grouped).astype(BF)
    part = dot(gated_out[...], wo[...]).astype(BF)
    sides, width = part_out.shape[1], part_out.shape[4]
    for side in range(sides):
        for f in range(2):
            first = (f * sides + side) * width
            part_out[0, side, f] = part[:, first : first + width]


def gate_kernel(heads, grad, wo, gate, group, scale, pcol, dgate_out, mix_out):
    sides = grad.shape[1]
    rows = jnp.concatenate(
        [grad[0, side, f] for f in range(2) for side in range(sides)], axis=1
    )
    passed = dot_nt(rows, wo[...]) * pcol[...]
    for h in range(heads):
        wide = slice(h * VD, (h + 1) * VD)
        gate_h, grouped = gate[:, wide], group[:, wide]
        squash = jax.nn.sigmoid(gate_h)
        upstream = passed[:, wide]
        dgate_out[:, wide] = (
            upstream * grouped * (squash + gate_h * squash * (1.0 - squash))
        ).astype(BF)
        grad_group = upstream * gate_h * squash
        mean = jnp.mean(grad_group, axis=1, keepdims=True)
        cross = jnp.mean(grad_group * grouped, axis=1, keepdims=True)
        mix_out[:, wide] = (scale[:, h : h + 1] * (grad_group - mean - grouped * cross)).astype(BF)


def back_kernel(
    heads, docs, decay, mix, q, k, v, carry, state, dcol, drow, prow, cos, sin, dq_out, dk_out,
    dv_out, sum_out, acc
):
    step = pl.program_id(0)

    @pl.when(step == 0)
    def _():
        acc[...] = jnp.zeros_like(acc)
        dk_out[...] = jnp.zeros_like(dk_out)
        dv_out[...] = jnp.zeros_like(dv_out)

    docs_col = dcol[...]

    def turn(j, totals):
        at = pl.ds(pl.multiple_of(j * WIDE, WIDE), WIDE)
        sums = []
        for h in range(heads):
            mine = slice(h * KD, (h + 1) * KD)
            wide = slice(h * VD, (h + 1) * VD)
            query, grad_mixed, key = q[:, mine], mix[:, wide], k[at, mine]
            factor = tile_decay(decay[h], step * TILE - j * WIDE, docs_col, drow[:, at], prow[:, at])
            weights = (dot_nt(query, key) * factor).astype(BF)
            grads = (dot_nt(grad_mixed, v[at, wide]) * factor).astype(BF)
            dk_out[at, mine] += dot_tn(grads, query)
            dv_out[at, wide] += dot_tn(weights, grad_mixed)
            sums.append(totals[h] + dot(grads, key))
        return tuple(sums)

    zeros = tuple(jnp.zeros((TILE, KD), F32) for _ in range(heads))
    totals = lax.fori_loop(0, step * TILE // WIDE + 1, turn, zeros)
    for h in range(heads):
        mine = slice(h * KD, (h + 1) * KD)
        wide = slice(h * VD, (h + 1) * VD)
        lift = carry[:, h : h + 1]
        total = totals[h] + lift * dot_nt(mix[:, wide], state[h])
        dq_out[:, mine] = turned(total, cos[...], -sin[...]).astype(BF)
        acc[h] += dot_tn((q[:, mine].astype(F32) * lift).astype(BF), mix[:, wide])

    @pl.when(step == pl.num_programs(0) - 1)
    def _():
        send_state(docs, acc, sum_out)


def finish_kernel(
    heads, size, docs, decay, dk_in, dv_in, k, v, end, one, two, three, dq, dgate, wq, wk, wv, wg,
    cos, sin, x, stat, vec, dk_out, dv_out, part_out, rows_out, cols_out, state
):
    step = pl.program_id(0)

    @pl.when(step == 0)
    def _():
        last = docs[0].astype(F32)
        link_two = (doc_in(one) == last).astype(F32)
        link_three = (doc_in(two) == last).astype(F32)
        states = joined_state(decay, size, one, two, three, link_two, link_three)
        for h in range(heads):
            state[h] = states[h]

    cosine, sine = cos[...], -sin[...]
    for h in range(heads):
        mine = slice(h * KD, (h + 1) * KD)
        wide = slice(h * VD, (h + 1) * VD)
        lift = end[:, h : h + 1]
        grad_key = dk_in[:, mine] + lift * dot_nt(v[:, wide], state[h])
        dk_out[:, mine] = (turned(grad_key, cosine, sine) * KD ** (-0.5)).astype(BF)
        key_end = (k[:, mine].astype(F32) * lift).astype(BF)
        dv_out[:, wide] = (dv_in[:, wide] + dot(key_end, state[h])).astype(BF)
    part = (
        dot_nt(dq[...], wq[...])
        + dot_nt(dk_out[...], wk[...])
        + dot_nt(dv_out[...], wv[...])
        + dot_nt(dgate[...], wg[...])
    )
    count, width = part_out.shape[0], part_out.shape[2]
    for shard in range(count):
        part_out[shard] = part[:, shard * width : (shard + 1) * width].astype(BF)
    normed = (lanes(x).astype(F32) - stat[:, 0:1]) * stat[:, 1:2]
    scaled = part * vec[0:1, :]
    ones = jnp.ones((8, scaled.shape[1]), BF)
    rows_out[0, 0:8] = dot_nt(ones, scaled.astype(BF))
    rows_out[0, 8:16] = dot_nt(ones, (scaled * normed).astype(BF))
    sums = jnp.concatenate(
        [jnp.sum(part * normed, axis=0, keepdims=True), jnp.sum(part, axis=0, keepdims=True)],
        axis=0,
    )

    @pl.when(step == 0)
    def _():
        cols_out[...] = jnp.zeros_like(cols_out)

    cols_out[...] += sums


def feed_kernel(
    chunks, x, grads, vec, up_near, up_far, down_near, down_far, ln_out, grad_out, act_out,
    dup_out, part_out, stat_out, rows_out, cols_out, acc
):
    step = pl.program_id(0)
    count = x.shape[1]
    steps = count // TILE

    def at_rows(r):
        return pl.ds(pl.multiple_of(r * TILE, TILE), TILE)

    @pl.when(step == 0)
    def _():
        def start(r, carry):
            at = at_rows(r)
            rows = jnp.concatenate([x[i, at, :] for i in range(x.shape[0])], axis=1).astype(F32)
            mean = jnp.mean(rows, axis=1, keepdims=True)
            scale = lax.rsqrt(jnp.mean(rows * rows, axis=1, keepdims=True) - mean * mean + EPSILON)
            stat_out[at, :] = jnp.concatenate([mean, scale], axis=1)
            ln_out[at, :] = ((rows - mean) * scale * vec[2:3, :] + vec[3:4, :]).astype(BF)
            grad_out[at, :] = jnp.concatenate(
                [grads[i, at, :] for i in range(grads.shape[0])], axis=1
            )
            acc[at, :] = jnp.zeros((TILE, acc.shape[1]), F32)
            return carry

        lax.fori_loop(0, steps, start, 0)

    def units(up, down):
        def turn(r, carry):
            at = at_rows(r)
            lifted = dot(ln_out[at, :], up[...])
            share = 0.5 * (1.0 + lax.erf(lifted * 0.5**0.5))
            act_out[at, :] = (lifted * share).astype(BF)
            slope = share + lifted * jnp.exp(-0.5 * lifted * lifted) * 0.3989422804014327
            lowered = (slope * dot_nt(grad_out[at, :], down[...])).astype(BF)
            dup_out[at, :] = lowered
            acc[at, :] += dot_nt(lowered, up[...])
            return carry

        lax.fori_loop(0, steps, turn, 0, unroll=True)

    @pl.when(step < chunks)
    def _():
        units(up_near, down_near)

    @pl.when(step >= chunks)
    def _():
        units(up_far, down_far)

    @pl.when(step == pl.num_programs(0) - 1)
    def _():
        cols_out[...] = jnp.zeros_like(cols_out)
        sides, width = part_out.shape[1], part_out.shape[3]

        def finish(r, carry):
            at = at_rows(r)
            part = acc[at, :]
            for f in range(2):
                for side in range(sides):
                    first = (f * sides + side) * width
                    part_out[f, side, at, :] = part[:, first : first + width].astype(BF)
            rows = jnp.concatenate([x[i, at, :] for i in range(x.shape[0])], axis=1).astype(F32)
            normed = (rows - stat_out[at, 0:1]) * stat_out[at, 1:2]
            scaled = part * vec[2:3, :]
            ones = jnp.ones((8, scaled.shape[1]), BF)
            rows_out[r, 0:8] = dot_nt(ones, scaled.astype(BF))
            rows_out[r, 8:16] = dot_nt(ones, (scaled * normed).astype(BF))
            cols_out[...] += jnp.concatenate(
                [
                    jnp.sum(part * normed, axis=0, keepdims=True),
                    jnp.sum(part, axis=0, keepdims=True),
                ],
                axis=0,
            )
            return carry

        lax.fori_loop(0, steps, finish, 0)


def branch_kernel(full, mine, keep, other, hidden, grads, gain, stat, near, far, out):
    sums = (near[0] + far[0]) * (1.0 / full)
    one, two = (
        sums[at : at + 8].T[:, 0:1] for at in (0, 8)
    )
    upstream = keep[0, 0].astype(F32) + other[0, 0].astype(F32)
    scale = stat[:, 1:2]
    normed = (hidden[0] - stat[:, 0:1]) * scale
    out[0] = (
        grads[0].astype(F32)
        + scale
        * (upstream * gain[0] - one - normed * two)
    ).astype(BF)


def lower_kernel(act, down_near, down_far, out):
    units = down_near.shape[0]
    part = (dot(act[:, :units], down_near[...]) + dot(act[:, units:], down_far[...])).astype(BF)
    sides, width = out.shape[1], out.shape[3]
    for f in range(2):
        for side in range(sides):
            first = (f * sides + side) * width
            out[f, side] = part[:, first : first + width]


def prefetched(kernel, grid, in_specs, out_specs, outs, flops=0):
    return pl.pallas_call(
        kernel,
        grid_spec=pltpu.PrefetchScalarGridSpec(
            num_scalar_prefetch=1, grid=grid, in_specs=in_specs, out_specs=out_specs
        ),
        out_shape=[jax.ShapeDtypeStruct(shape, dtype) for shape, dtype in outs],
        cost_estimate=pl.CostEstimate(flops=flops, bytes_accessed=0, transcendentals=0),
        compiler_params=pltpu.CompilerParams(vmem_limit_bytes=VMEM_LIMIT),
    )


def bit_value(bit):
    return my_bit("tok", bit)[None].astype(jnp.int32)


def split_source(groups, rows, block):
    per_half = rows // (2 * block)
    count = groups * per_half

    def source(i, mine):
        keeps = (i >= count).astype(jnp.int32)
        half = jnp.where(keeps == 1, mine[0], 1 - mine[0])
        j = i - keeps * count
        return (j // per_half) * (2 * per_half) + half * per_half + j % per_half

    give = lambda i, mine: (jnp.minimum(i, count - 1), 0)
    keep = lambda i, mine: (jnp.maximum(i - count, 0), 0)
    return count, source, give, keep


def weight_kernel(count, mine, left, *refs):
    give, keep = refs[-2:]

    def fill(out):
        first = 0
        for right in refs[:-2]:
            width = right.shape[1]
            out[:, first : first + width] = dot_tn(left[...], right[...]).astype(BF)
            first += width

    @pl.when(pl.program_id(0) < count)
    def _():
        fill(give)

    @pl.when(pl.program_id(0) >= count)
    def _():
        fill(keep)


def weight_grad(bit, groups, left, *rights):
    rows, columns = left.shape
    width = sum(right.shape[1] for right in rights)
    block = min(CHUNK, columns // groups // 2)
    count, source, give, keep = split_source(groups, columns // groups, block)
    half = (columns // 2, width)
    return prefetched(
        partial(weight_kernel, count),
        (2 * count,),
        [pl.BlockSpec((rows, block), lambda i, mine: (0, source(i, mine)))]
        + [
            pl.BlockSpec(right.shape, lambda i, mine: (0, 0), pipeline_mode=pl.Buffered(1))
            for right in rights
        ],
        [pl.BlockSpec((block, width), give), pl.BlockSpec((block, width), keep)],
        [(half, BF), (half, BF)],
        4 * rows * columns * width,
    )(bit_value(bit), left, *rights)


def turned_place(i, order):
    place = 0
    for k, bit in enumerate(order):
        place = place + (((i >> (len(order) - 1 - k)) & 1) << bit)
    return place


def outer_kernel(mine, gated, grad, give, keep):
    part = dot_tn(gated[...], jnp.concatenate([grad[0, 0, 0], grad[1, 0, 0]], axis=0)).astype(BF)
    half = give.shape[0]

    @pl.when(mine[0] == 0)
    def _():
        keep[...] = part[:half]
        give[...] = part[half:]

    @pl.when(mine[0] == 1)
    def _():
        keep[...] = part[half:]
        give[...] = part[:half]


def fold_kernel(count, mine, one, two, give, keep):
    total = (one[...].astype(F32) + two[...].astype(F32)).astype(BF)

    @pl.when(pl.program_id(0) < count)
    def _():
        give[...] = total

    @pl.when(pl.program_id(0) >= count)
    def _():
        keep[...] = total


def fold(bit, groups, one, two):
    rows, columns = one.shape
    block = min(CHUNK // 2, rows // groups // 2)
    count, source, give, keep = split_source(groups, rows // groups, block)
    spec = pl.BlockSpec((block, columns), lambda i, mine: (source(i, mine), 0))
    half = (rows // 2, columns)
    return prefetched(
        partial(fold_kernel, count),
        (2 * count,),
        [spec, spec],
        [pl.BlockSpec((block, columns), give), pl.BlockSpec((block, columns), keep)],
        [(half, BF), (half, BF)],
    )(bit_value(bit), one, two)


def scatter_rest(give, keep, order, groups=1, waits=None):
    values, others = [], []
    for place, bit in enumerate(order):
        if waits and place in waits:
            give = after(give, *waits[place])
        other = swapped(give, "tok", 1 << bit)
        if waits and ("seen", place) in waits:
            other = after(other, *waits["seen", place])
        others.append(other)
        if place + 1 < len(order):
            give, keep = fold(order[place + 1], groups, keep, other)
            values.append(give)
        else:
            values.append((keep, other))
    return values, others


def total(pair):
    return pair[0].astype(F32) + pair[1].astype(F32)


def spread_kernel(per_half, mine, near, other, out):
    here = pl.program_id(0) // per_half == mine[0]

    @pl.when(here)
    def _():
        out[...] = near[...].astype(out.dtype)

    @pl.when(jnp.logical_not(here))
    def _():
        out[...] = other[...].astype(out.dtype)


def gather_one(value, bit):
    return joined(value, swapped(value, "tok", 1 << bit), my_bit("tok", bit) == 0, 0)


def gather_wide(value, order):
    for bit in order[:0:-1]:
        value = gather_one(value, bit)
    bit = order[0]
    other = swapped(value, "tok", 1 << bit)
    rows, columns = value.shape
    block = min(CHUNK // 2, rows)
    per_half = rows // block

    def spec(mirror):
        def index(i, mine):
            half = 1 - mine[0] if mirror else mine[0]
            return (jnp.clip(i - half * per_half, 0, per_half - 1), 0)

        return pl.BlockSpec((block, columns), index)

    return prefetched(
        partial(spread_kernel, per_half),
        (2 * per_half,),
        [spec(False), spec(True)],
        [pl.BlockSpec((block, columns), lambda i, mine: (i, 0))],
        [((2 * rows, columns), F32)],
    )(bit_value(bit), value, other)[0], value


def order_kernel(plan, *refs):
    outs = list(refs[len(plan) :])
    for part, count in zip(refs, plan, strict=False):
        if count == 1:
            out = outs.pop(0)
            rows, columns = out.shape[0], part.shape[2]
            for i in range(part.shape[1] // rows):
                at = slice(i * columns, (i + 1) * columns)
                out[:, at] = part[0, i * rows : (i + 1) * rows].astype(F32)
            continue
        first = 0
        for _ in range(count):
            out = outs.pop(0)
            out[...] = part[0, :, first : first + out.shape[1]].astype(F32)
            first += out.shape[1]


def packed_pieces(first, *others):
    columns = others[0].shape[1]
    parts = [first[:, i : i + columns] for i in range(0, first.shape[1], columns)]
    return jnp.concatenate([*parts, *others], axis=0)


def in_order(pieces, plan):
    count, rows, columns = pieces.shape
    part = rows // len(plan)

    def spec(which, order):
        return pl.BlockSpec(
            (1, part, columns), lambda i: (turned_place(i, order), which, 0)
        )

    shapes = [shape for _, parts in plan for shape in parts]
    return pl.pallas_call(
        partial(order_kernel, [len(parts) for _, parts in plan]),
        grid=(count,),
        in_specs=[spec(which, order) for which, (order, _) in enumerate(plan)],
        out_specs=[pl.BlockSpec(shape, lambda i: (i, 0)) for shape in shapes],
        out_shape=[jax.ShapeDtypeStruct((count * high, wide), F32) for high, wide in shapes],
        cost_estimate=pl.CostEstimate(flops=0, bytes_accessed=0, transcendentals=0),
        compiler_params=pltpu.CompilerParams(vmem_limit_bytes=VMEM_LIMIT),
    )(*[pieces] * len(plan))


def body(
    tokens,
    mix_gain,
    mix_bias,
    query_weight,
    key_weight,
    value_weight,
    gate_weight,
    output_weight,
    feed_gain,
    feed_bias,
    up_weight,
    down_weight,
    doc_ids,
    pad_mask,
    out_grad,
):
    row_count, width = tokens.shape
    heads_here = query_weight.shape[1] // KD
    shards = lax.axis_size("head")
    full_width = width * shards
    sides = shards // 2
    spread = lax.axis_index("head") // sides
    side = lax.axis_index("head") % sides
    half_rows = row_count // 2
    block = lax.axis_index("tok")

    packed = pl.pallas_call(
        entry_kernel,
        out_shape=jax.ShapeDtypeStruct((row_count + EXTRA, width), BF),
        compiler_params=pltpu.CompilerParams(vmem_limit_bytes=VMEM_LIMIT),
    )(tokens, mix_gain[None], mix_bias[None], feed_gain[None], feed_bias[None])
    rows_raw = lax.all_gather(packed, "head", axis=0)
    vector_rows = rows_raw[:, row_count:, :].astype(F32)
    vectors = (vector_rows[:, 0:12:3] + vector_rows[:, 1:12:3] + vector_rows[:, 2:12:3]).transpose(
        1, 0, 2
    )
    side_vectors = lax.dynamic_index_in_dim(
        vectors.reshape(4, 2, sides, width), side, 2, keepdims=False
    )
    vectors = vectors.reshape(4, full_width)

    order_one, order_two = bit_orders()
    first_head = lax.axis_index("head") * heads_here
    log_decay = jnp.log(
        1.0 - 2.0 ** (-5.0 - (first_head + jnp.arange(heads_here, dtype=jnp.int32)).astype(F32))
    )
    position = jnp.arange(row_count, dtype=jnp.int32)
    frequency = 10000.0 ** (-2.0 * jnp.arange(KD // 2, dtype=jnp.int32).astype(F32) / KD)
    angles = (block * row_count + position).astype(F32)[:, None] * frequency[None, :]
    cosine, sine = jnp.cos(angles), jnp.sin(angles)
    padding = pad_mask.astype(F32)
    last_doc = doc_ids[row_count - 1]

    end_factor = (padding * (doc_ids == last_doc).astype(F32))[:, None] * jnp.exp(
        (row_count - 1 - position).astype(F32)[:, None] * log_decay[None, :]
    )

    late_grad = after(out_grad, rows_raw, cosine, sine, end_factor)
    grad_keep, grad_give = halves(late_grad, "head", shards.bit_length() - 2, 0)
    grad_seen = swapped(grad_give, "head", sides)
    up_piece, down_piece = own_piece(up_weight, order_one), own_piece(down_weight, order_two)
    both_pieces = jnp.concatenate([up_piece, down_piece.reshape(up_piece.shape)], axis=0)

    docs_col, docs_row = doc_ids[:, None], doc_ids[None, :]
    pads_col, pads_row = padding[:, None], padding[None, :]
    inner_width, value_width = heads_here * KD, heads_here * VD
    states = pltpu.VMEM((heads_here, KD, VD), F32)
    state_shape = (heads_here, KD, VD)
    sent_shape = (heads_here, KD + EXTRA, VD)
    shard_tiles = pl.BlockSpec((shards, TILE, width), lambda i: (0, i, 0))
    per_half = half_rows // TILE
    split_tiles = pl.BlockSpec(
        (1, sides, 2, TILE, width), lambda i: (i // per_half, 0, 0, i % per_half, 0)
    )
    last_docs = doc_ids[row_count - 1 :]
    rows_first, query_rot, key_rot, values, stats, summary = call(
        partial(project_kernel, heads_here),
        row_count,
        [
            SCALARS,
            shard_tiles,
            pl.BlockSpec((shards, EXTRA, width), lambda i: (0, row_count // EXTRA, 0)),
            whole(full_width, inner_width),
            whole(full_width, inner_width),
            whole(full_width, value_width),
            tiles(KD // 2),
            tiles(KD // 2),
            tiles(heads_here),
        ],
        [
            ((row_count, full_width), BF),
            ((row_count, inner_width), BF),
            ((row_count, inner_width), BF),
            ((row_count, value_width), BF),
            ((row_count, 2), F32),
            (sent_shape, BF),
        ],
        [
            tiles(full_width),
            tiles(inner_width),
            tiles(inner_width),
            tiles(value_width),
            tiles(2),
            held(*sent_shape),
        ],
        [states],
    )(
        last_docs,
        rows_raw,
        rows_raw,
        query_weight,
        key_weight,
        value_weight,
        cosine,
        sine,
        end_factor,
    )
    one_back, two_back, three_back = (shifted(summary, by) for by in (1, 2, 3))
    grad_seen = after(grad_seen, summary)
    side_grads = joined(grad_keep[None], grad_seen[None], spread == 0, 0)
    grad_rows, grads_last = gather_side(side_grads[:, None])
    grad_rows = grad_rows.reshape(shards, half_rows, width)
    (both_seen,) = far_swap(after(both_pieces, grad_seen))
    up_seen = both_seen[: up_piece.shape[0]]
    down_seen = both_seen[up_piece.shape[0] :].reshape(down_piece.shape)
    up_other = gather_back(up_seen, order_one)
    down_other = gather_back(down_seen, order_two)
    gate_pre, inner_part = call(
        partial(inner_kernel, heads_here),
        row_count,
        [
            SCALARS,
            tiles(full_width),
            whole(full_width, value_width),
            tiles(inner_width),
            whole(row_count, inner_width),
            whole(row_count, value_width),
            tiles(1),
            whole(1, row_count),
            whole(1, row_count),
        ],
        [((row_count, value_width), F32)] * 2,
        [tiles(value_width)] * 2,
    )(
        after(log_decay, side_grads),
        rows_first,
        gate_weight,
        query_rot,
        key_rot,
        values,
        docs_col,
        docs_row,
        pads_row,
    )
    flat_group, group_scale, gated, mix_part, state_low, carry_factor = call(
        partial(mix_kernel, heads_here, row_count),
        row_count,
        [
            SCALARS,
            tiles(value_width),
            tiles(inner_width),
            whole(*sent_shape),
            whole(*sent_shape),
            whole(*sent_shape),
            tiles(value_width),
            tiles(1),
            tiles(1),
            whole(value_width, full_width),
        ],
        [
            ((row_count, value_width), F32),
            ((row_count, heads_here), F32),
            ((row_count, value_width), BF),
            ((2, sides, 2, half_rows, width), BF),
            (state_shape, BF),
            ((row_count, heads_here), F32),
        ],
        [
            tiles(value_width),
            tiles(heads_here),
            tiles(value_width),
            split_tiles,
            held(*state_shape),
            tiles(heads_here),
        ],
    )(
        log_decay,
        inner_part,
        query_rot,
        one_back,
        two_back,
        three_back,
        gate_pre,
        docs_col,
        pads_col,
        output_weight,
    )
    mix_part = after(mix_part, grads_last, both_seen)
    side_tokens = lax.dynamic_index_in_dim(
        lax.dynamic_slice_in_dim(rows_raw, spread * half_rows, half_rows, axis=1).reshape(
            2, sides, half_rows, width
        ),
        side,
        1,
        keepdims=False,
    )
    mixed_sum = lax.psum_scatter(
        mix_part.reshape(shards, 2, half_rows, width), "head", scatter_dimension=0
    )
    hidden = lax.optimization_barrier(side_tokens.astype(F32) + mixed_sum.astype(F32))
    hidden_rows = gather_side(hidden.astype(BF)[:, None])[0].reshape(shards, half_rows, width)
    units = up_weight.shape[1]
    chunks = units // CHUNK
    rows_second, grad_plain, act_low, grad_up, feed_part, stats_second, row_second, cols_second = (
        pl.pallas_call(
            partial(feed_kernel, chunks),
            grid=(2 * chunks,),
            in_specs=[
                whole(shards, half_rows, width),
                whole(shards, half_rows, width),
                whole(4, full_width),
                pl.BlockSpec((full_width, CHUNK), lambda i: (0, jnp.minimum(i, chunks - 1))),
                pl.BlockSpec((full_width, CHUNK), lambda i: (0, jnp.maximum(i - chunks, 0))),
                pl.BlockSpec((CHUNK, full_width), lambda i: (jnp.minimum(i, chunks - 1), 0)),
                pl.BlockSpec((CHUNK, full_width), lambda i: (jnp.maximum(i - chunks, 0), 0)),
            ],
            out_specs=[
                held(half_rows, full_width),
                held(half_rows, full_width),
                pl.BlockSpec((half_rows, CHUNK), lambda i: (0, i)),
                pl.BlockSpec((half_rows, CHUNK), lambda i: (0, i)),
                held(2, sides, half_rows, width),
                held(half_rows, 2),
                held(half_rows // TILE, 16, TILE),
                held(2, full_width),
            ],
            out_shape=[
                jax.ShapeDtypeStruct((half_rows, full_width), BF),
                jax.ShapeDtypeStruct((half_rows, full_width), BF),
                jax.ShapeDtypeStruct((half_rows, 2 * units), BF),
                jax.ShapeDtypeStruct((half_rows, 2 * units), BF),
                jax.ShapeDtypeStruct((2, sides, half_rows, width), BF),
                jax.ShapeDtypeStruct((half_rows, 2), F32),
                jax.ShapeDtypeStruct((half_rows // TILE, 16, TILE), F32),
                jax.ShapeDtypeStruct((2, full_width), F32),
            ],
            scratch_shapes=[pltpu.VMEM((half_rows, full_width), F32)],
            cost_estimate=pl.CostEstimate(flops=0, bytes_accessed=0, transcendentals=0),
            compiler_params=pltpu.CompilerParams(vmem_limit_bytes=VMEM_LIMIT),
        )(hidden_rows, grad_rows, vectors, up_weight, up_other, down_weight, down_other)
    )
    feed_value, feed_seen = scatter_side_start(feed_part)
    for bit in list(side_bits())[:0:-1]:
        row_second = row_second + swapped(row_second, "head", 1 << bit)
    row_seen = swapped(row_second, "head", 1)
    down_give, down_keep = weight_grad(order_one[0], 2, act_low, grad_plain)
    up_give, up_keep = weight_grad(order_two[0], 1, rows_second, grad_up)
    row_seen = after(row_seen, down_give, up_give)
    half_block = pl.BlockSpec((1, TILE, width), lambda f, i, mine: (f, i, 0))
    row_block = pl.BlockSpec((TILE, 2), lambda f, i, mine: (i, 0))
    sum_block = pl.BlockSpec((1, 16, TILE), lambda f, i, mine: (i, 0, 0))
    (branch,) = prefetched(
        partial(branch_kernel, full_width),
        (2, half_rows // TILE),
        [
            pl.BlockSpec((1, 1, TILE, width), lambda f, i, mine: (f, mine[0], i, 0)),
            pl.BlockSpec((1, 1, TILE, width), lambda f, i, mine: (f, 0, i, 0)),
            half_block,
            half_block,
            pl.BlockSpec((1, 1, width), lambda f, i, mine: (f, 0, 0)),
            row_block,
            sum_block,
            sum_block,
        ],
        [half_block],
        [((2, half_rows, width), BF)],
    )(
        my_bit("head", 0)[None].astype(jnp.int32),
        feed_value,
        feed_seen[:, None] if feed_seen.ndim == 3 else feed_seen,
        hidden,
        side_grads,
        side_vectors[2][:, None, :],
        stats_second,
        row_second,
        row_seen,
    )
    grad_branch = lax.all_gather(branch, "head", axis=0).reshape(
        2, sides, 2, half_rows, width
    )

    down_part = pl.pallas_call(
        lower_kernel,
        grid=(half_rows // TILE,),
        in_specs=[tiles(2 * units), whole(units, full_width), whole(units, full_width)],
        out_specs=pl.BlockSpec((2, sides, TILE, width), lambda i: (0, 0, i, 0)),
        out_shape=jax.ShapeDtypeStruct((2, sides, half_rows, width), BF),
        cost_estimate=pl.CostEstimate(flops=0, bytes_accessed=0, transcendentals=0),
        compiler_params=pltpu.CompilerParams(vmem_limit_bytes=VMEM_LIMIT),
    )(after(act_low, branch), down_weight, down_other)

    down_sum, down_seen_all = scatter_rest(
        down_give, down_keep, order_one, 2, {0: (branch,), ("seen", 1): (down_part,)}
    )
    up_sum, up_seen_all = scatter_rest(
        up_give, up_keep, order_two, 1, {0: (branch,), ("seen", 1): (down_part,)}
    )

    dgate, grad_mixed = call(
        partial(gate_kernel, heads_here),
        row_count,
        [
            split_tiles,
            whole(value_width, full_width),
            tiles(value_width),
            tiles(value_width),
            tiles(heads_here),
            tiles(1),
        ],
        [((row_count, value_width), BF), ((row_count, value_width), BF)],
        [tiles(value_width), tiles(value_width)],
    )(
        grad_branch,
        output_weight,
        gate_pre,
        flat_group,
        group_scale,
        after(pads_col, down_sum[1], up_sum[1]),
    )
    half_down = down_sum[-1][0].shape[0] // 2
    up_pair = lax.optimization_barrier((*up_sum[-1], dgate))[:2]
    down_pair = lax.optimization_barrier((*down_sum[-1], dgate))[:2]
    up_give = total([part[:, units:] for part in up_pair]).astype(BF)
    down_give = total([part[half_down:] for part in down_pair]).astype(BF)
    dq, dk_part, dv_part, grad_state = call(
        partial(back_kernel, heads_here),
        row_count,
        [
            SCALARS,
            SCALARS,
            tiles(value_width),
            tiles(inner_width),
            whole(row_count, inner_width),
            whole(row_count, value_width),
            tiles(heads_here),
            whole(*state_shape),
            tiles(1),
            whole(1, row_count),
            whole(1, row_count),
            tiles(KD // 2),
            tiles(KD // 2),
        ],
        [
            ((row_count, inner_width), BF),
            ((row_count, inner_width), F32),
            ((row_count, value_width), F32),
            (sent_shape, BF),
        ],
        [
            tiles(inner_width),
            held(row_count, inner_width),
            held(row_count, value_width),
            held(*sent_shape),
        ],
        [states],
        10 * row_count * full_width * value_width,
    )(
        last_docs,
        after(log_decay, down_part, up_give, down_give),
        grad_mixed,
        query_rot,
        key_rot,
        values,
        carry_factor,
        state_low,
        docs_col,
        docs_row,
        pads_row,
        cosine,
        sine,
    )
    width_out = (value_width // 2, full_width)
    outw_give, outw_keep = prefetched(
        outer_kernel,
        (shards,),
        [
            pl.BlockSpec(
                (row_count, value_width), lambda i, mine: (0, 0), pipeline_mode=pl.Buffered(1)
            ),
            pl.BlockSpec(
                (2, 1, 1, half_rows, width), lambda i, mine: (0, i % sides, i // sides, 0, 0)
            ),
        ],
        [pl.BlockSpec((value_width // 2, width), lambda i, mine: (0, i))] * 2,
        [(width_out, BF), (width_out, BF)],
        4 * row_count * value_width * full_width,
    )(bit_value(order_one[0]), after(gated, dq, up_give, down_give), grad_branch)
    outw_sum, outw_seen = scatter_rest(outw_give, outw_keep, order_one)
    gw_give, gw_keep = weight_grad(order_two[0], 1, rows_first, after(dgate, dq))
    gw_sum, gw_seen = scatter_rest(gw_give, gw_keep, order_two)
    one_on, two_on, three_on = (shifted(grad_state, -by) for by in (1, 2, 3))
    up_far, down_far = far_swap(up_give, down_give)
    up_far, down_far = after(up_far, gw_give, outw_give), after(down_far, gw_give, outw_give)
    up_near = total([part[:, :units] for part in up_pair]) + up_far.astype(F32)
    down_near = total([part[:half_down] for part in down_pair]) + down_far.astype(F32)
    down_low, up_low = down_near.astype(BF), up_near.astype(BF)
    feed_pieces = after(packed_pieces(down_low, up_low), one_on, two_on, three_on)
    feed_pieces = lax.all_gather(feed_pieces, "tok", axis=0)
    grad_down, grad_upw = in_order(
        feed_pieces, ((order_one, [down_low.shape]), (order_two, [up_low.shape]))
    )
    dk, dv, last_part, row_sums, column_first = call(
        partial(finish_kernel, heads_here, row_count),
        row_count,
        [
            SCALARS,
            SCALARS,
            tiles(inner_width),
            tiles(value_width),
            tiles(inner_width),
            tiles(value_width),
            tiles(heads_here),
            whole(*sent_shape),
            whole(*sent_shape),
            whole(*sent_shape),
            tiles(inner_width),
            tiles(value_width),
            whole(full_width, inner_width),
            whole(full_width, inner_width),
            whole(full_width, value_width),
            whole(full_width, value_width),
            tiles(KD // 2),
            tiles(KD // 2),
            shard_tiles,
            tiles(2),
            whole(4, full_width),
        ],
        [
            ((row_count, inner_width), BF),
            ((row_count, value_width), BF),
            ((shards, row_count + EXTRA, width), BF),
            ((row_count // TILE, 16, TILE), F32),
            ((2, full_width), F32),
        ],
        [
            tiles(inner_width),
            tiles(value_width),
            shard_tiles,
            pl.BlockSpec((1, 16, TILE), lambda i: (i, 0, 0)),
            held(2, full_width),
        ],
        [pltpu.VMEM(state_shape, BF)],
        12 * row_count * full_width * value_width,
    )(
        last_docs,
        after(log_decay, up_near, down_near),
        dk_part,
        dv_part,
        key_rot,
        values,
        end_factor,
        one_on,
        two_on,
        three_on,
        dq,
        dgate,
        query_weight,
        key_weight,
        value_weight,
        gate_weight,
        cosine,
        sine,
        rows_raw,
        stats,
        vectors,
    )
    count = row_count // TILE
    line = jnp.concatenate([row_sums[:, 0], row_sums[:, 8]], axis=0)
    line = jnp.pad(line, ((0, EXTRA - 2 * count - 4), (0, width - TILE)))
    columns = jnp.concatenate([column_first, cols_second]).reshape(4, shards, width)
    extra = jnp.concatenate(
        [jnp.broadcast_to(line[None], (shards, *line.shape)), columns.transpose(1, 0, 2)], axis=1
    )
    last_part = lax.dynamic_update_slice_in_dim(last_part, extra.astype(BF), row_count, axis=1)
    vw_give, vw_keep = weight_grad(order_one[0], 1, rows_first, dv)
    qkw_give, qkw_keep = weight_grad(order_two[0], 1, rows_first, dq, dk)
    last_part = after(last_part, feed_pieces, vw_give, qkw_give, outw_sum[0], gw_seen[0])
    last_sum = lax.psum_scatter(last_part, "head", scatter_dimension=0).astype(F32)
    grad_ln1 = last_sum[:row_count]
    sums_first = last_sum[row_count:, :TILE] / full_width
    sums_first = jnp.stack(
        [sums_first[:count].reshape(row_count), sums_first[count : 2 * count].reshape(row_count)],
        axis=1,
    )
    columns = lax.psum(last_sum[row_count + EXTRA - 4 :], "tok")
    result = (hidden + scatter_side(after(down_part, last_sum))).astype(BF)
    result_keep = lax.dynamic_index_in_dim(result, spread, 0, keepdims=False)
    result_give = lax.dynamic_index_in_dim(result, 1 - spread, 0, keepdims=False)
    layer_out = joined(result_keep, swapped(result_give, "head", sides), spread == 0, 0)

    outw_low, gw_low = total(outw_sum[-1]).astype(BF), total(gw_sum[-1]).astype(BF)
    waits = {1: (gw_sum[0],), 2: (outw_sum[1], gw_sum[1])}
    vw_sum, _ = scatter_rest(vw_give, vw_keep, order_one, 1, waits)
    qkw_sum, _ = scatter_rest(qkw_give, qkw_keep, order_two, 1, waits)
    vw_low, qkw_low = total(vw_sum[-1]).astype(BF), total(qkw_sum[-1]).astype(BF)
    pieces = packed_pieces(outw_low, gw_low, vw_low, qkw_low)
    pieces = lax.all_gather(pieces, "tok", axis=0)
    high = qkw_low.shape[0]
    grad_outw, grad_gw, grad_vw, grad_qw, grad_kw = in_order(
        pieces,
        (
            (order_one, [outw_low.shape]),
            (order_two, [gw_low.shape]),
            (order_one, [vw_low.shape]),
            (order_two, [(high, inner_width), (high, inner_width)]),
        ),
    )

    norm_first = (tokens.astype(F32) - stats[:, 0:1]) * stats[:, 1:2]
    branch_rows = lax.dynamic_index_in_dim(
        lax.dynamic_index_in_dim(grad_branch, side, 1, keepdims=False), spread, 1, keepdims=False
    ).reshape(row_count, width)
    tokens_grad = branch_rows.astype(F32) + stats[:, 1:2] * (
        grad_ln1 * mix_gain - sums_first[:, 0:1] - norm_first * sums_first[:, 1:2]
    )
    return (
        layer_out,
        tokens_grad,
        columns[0],
        columns[1],
        grad_qw,
        grad_kw,
        grad_vw,
        grad_gw,
        grad_outw,
        columns[2],
        columns[3],
        grad_upw,
        grad_down,
    )


def solution(mesh):
    rows = P("tok", "head")
    columns = P(None, "head")
    return jax.shard_map(
        body,
        mesh=mesh,
        in_specs=(
            rows,
            P("head"),
            P("head"),
            columns,
            columns,
            columns,
            columns,
            P("head", None),
            P("head"),
            P("head"),
            columns,
            P("head", None),
            P("tok"),
            P("tok"),
            rows,
        ),
        out_specs=(
            rows,
            rows,
            P("head"),
            P("head"),
            columns,
            columns,
            columns,
            columns,
            P("head", None),
            P("head"),
            P("head"),
            columns,
            P("head", None),
        ),
        check_vma=False,
    )
```
